32 devices in a mesh: patch: 8 (over y, x, core), tm: 4 (over z).
Axes of the slice: x: 2, y: 2, z: 4, core: 2. Of those that a mesh axis runs over, the one named last changes fastest.
Arguments:
- bits: int32 [32, 8, 26, 24], P('patch', 'tm'), may hold values 0 or 1
- partners: int32 [4, 32], P('tm'), may hold values from 0 to 31, as said below
- gate_round: int32 [4], P('tm'), may hold values from 0 to 7, as said below
- first_kernel: bfloat16 [3, 3, 3, 32], replicated, may hold values from -1.25 to 1.25
- second_kernels: bfloat16 [2, 3, 3, 3, 32, 32], replicated, may hold values from -0.21875 to 0.21875
- conv_bias: float32 [3, 32], replicated, may hold values from -3 to 3
- couple_down: bfloat16 [2, 32, 16], replicated, may hold values from -1 to 1
- couple_up: bfloat16 [2, 2, 16, 32], replicated, may hold values from -1.5 to 1.5
- head: bfloat16 [32], replicated, may hold values from -1 to 1
- cell_bias: float32 [624], replicated, may hold values from -4 to 4
Outputs:
- priors: float32 [32, 8, 624], P('patch', 'tm')
The draws below stay inside these ranges and needn't reach their ends.
Inputs may be any that keep to these rules, and one draw needn't show every extreme that they name: `partners`: in each gate layer every patch has a partner other than itself, and the partner of the partner is the patch. Split the patches into aligned blocks of 4: no patch is paired within its own block, and a block pairs with exactly 4 other blocks, with exactly 1 of its patches in each. `gate_round`: gate layer g acts in one of the rounds g * 2 to (g + 1) * 2 - 1; the first gate layer acts in round 0 and the last in round 8 - 1.
All inputs are finite; a program needn't handle non-finite values. No bound on the sum of `bits` on one device may be relied on, other than what follows from the above.
Results may differ from the reference program's by a relative error of at most 0.0054.
Values may be sent and summed in bfloat16 or wider, within the bound.
No kernel may reach another device: no remote copies, remote signals or barrier semaphores. Data moves between devices by JAX's collectives and lax.ppermute only.
A program may use at most 64 MiB of HBM per device.

```python
import jax
import jax.numpy as jnp
from jax import lax

CHANNELS = 32
LATENT = 16
PATCH_DEV = 4
ROUND_DEV = 2
CAPACITY = 1
HEIGHT = 26
WIDTH = 24
CELLS = 624
PATCHES = 32
ROUNDS = 8
GATES = 4


def pair_position(position, turn, devices):
    last = devices - 1
    other = (2 * turn - position) % last
    other = jnp.where(position == turn, last, other)
    return jnp.where(position == last, turn, other).astype(jnp.int32)


def draw_partners(key, part):
    devices = PATCHES // PATCH_DEV
    groups = PATCH_DEV // CAPACITY

    def one_layer(layer_key):
        shuffle_key, turn_key, order_key = jax.random.split(layer_key, 3)
        shuffle = jax.random.permutation(shuffle_key, devices).astype(jnp.int32)
        place = jnp.zeros((devices,), jnp.int32).at[shuffle].set(jnp.arange(devices, dtype=jnp.int32))
        turns = jax.random.permutation(turn_key, devices - 1)[:groups].astype(jnp.int32)
        orders = jax.vmap(lambda inner: jax.random.permutation(inner, PATCH_DEV))(jax.random.split(order_key, devices)).astype(jnp.int32)
        owner = jnp.arange(devices, dtype=jnp.int32)[:, None, None]
        group = jnp.arange(groups, dtype=jnp.int32)[None, :, None]
        member = jnp.arange(CAPACITY, dtype=jnp.int32)[None, None, :]
        other = shuffle[pair_position(place[owner], turns[group], devices)]
        slot = group * CAPACITY + member
        self_ids = owner * PATCH_DEV + orders[owner, slot]
        companion_indices = other * PATCH_DEV + orders[other, slot]
        empty = jnp.zeros((PATCHES,), jnp.int32)
        return empty.at[self_ids.reshape(-1)].set(companion_indices.reshape(-1).astype(jnp.int32))
    layer_keys = jax.random.split(jax.random.fold_in(key, 11), GATES)
    return jax.vmap(one_layer)(layer_keys).astype(jnp.int32)


def draw_gate_round(key, part):
    offsets = jax.random.randint(jax.random.fold_in(key, 5), (GATES,), 0, ROUND_DEV).astype(jnp.int32)
    positions = jnp.arange(GATES)
    offsets = jnp.where(positions == 0, 0, offsets)
    offsets = jnp.where(positions == GATES - 1, ROUND_DEV - 1, offsets)
    return (positions * ROUND_DEV + offsets).astype(jnp.int32)


def set_ends(values, own_key, low, top_value):
    dims = values.shape
    index_at = [jax.random.randint(jax.random.fold_in(own_key, axis), (), 0, dims[axis]) for axis in range(len(dims))]
    values = values.at[tuple(index_at)].set(low)
    longest = dims.index(max(dims))
    index_at[longest] = (index_at[longest] + 1) % dims[longest]
    return values.at[tuple(index_at)].set(top_value)


def normal_values(own_key, dims, spread, most, held_as=jnp.bfloat16):
    values = spread * jax.random.normal(own_key, dims, jnp.float32)
    return jnp.clip(values, min=-most, max=most).astype(held_as)


def setup_inputs(seed: int = 0) -> dict:
    keys = jax.random.split(jax.random.key(seed), 11)
    bits = set_ends((jax.random.randint(keys[0], (PATCHES, ROUNDS, HEIGHT, WIDTH), 0, 4) < 1).astype(jnp.int32), jax.random.fold_in(keys[0], 1), 0, 1)
    partners = draw_partners(jax.random.fold_in(keys[10], 71), 0)
    gate_round = draw_gate_round(jax.random.fold_in(keys[10], 71), 0)
    first_kernel = normal_values(keys[3], (3, 3, 3, CHANNELS), 27 ** -0.5, 1.25)
    second_kernels = normal_values(keys[4], (2, 3, 3, 3, CHANNELS, CHANNELS), (27 * CHANNELS) ** -0.5, 0.21875)
    conv_bias = normal_values(keys[5], (3, CHANNELS), 0.5, 3.0, jnp.float32)
    couple_down = normal_values(keys[6], (2, CHANNELS, LATENT), CHANNELS ** -0.5, 1.0)
    couple_up = normal_values(keys[7], (2, 2, LATENT, CHANNELS), LATENT ** -0.5, 1.5)
    head = normal_values(keys[8], (CHANNELS,), CHANNELS ** -0.5, 1.0)
    cell_bias = normal_values(keys[9], (CELLS,), 1.0, 4.0, jnp.float32)
    return dict(bits=bits, partners=partners, gate_round=gate_round, first_kernel=first_kernel, second_kernels=second_kernels, conv_bias=conv_bias, couple_down=couple_down, couple_up=couple_up, head=head, cell_bias=cell_bias)


def convolve(volume, kernel):
    return lax.conv_general_dilated(volume[None], kernel, (1, 1, 1), [(1, 1), (1, 1), (1, 1)], dimension_numbers=("NDHWC", "DHWIO", "NDHWC"), precision=lax.Precision.HIGHEST)[0]


def couple(activation_maps, partners, gate_round, down, up_ctrl, up_targ):
    patch_ids = jnp.arange(PATCHES)
    for layer_index in range(GATES):
        moment = gate_round[layer_index].astype(jnp.int32)
        lattice_portion = lax.dynamic_index_in_dim(activation_maps, moment, 1, keepdims=False)
        latent_features = jnp.einsum("phwc,ck->phwk", lattice_portion.astype(jnp.float32), down.astype(jnp.float32), precision=lax.Precision.HIGHEST).astype(jnp.bfloat16)
        mates = partners[layer_index]
        taken = latent_features[mates].astype(jnp.float32)
        control_contribution = jnp.einsum("phwk,kc->phwc", taken, up_ctrl.astype(jnp.float32), precision=lax.Precision.HIGHEST)
        targ_term = jnp.einsum("phwk,kc->phwc", taken, up_targ.astype(jnp.float32), precision=lax.Precision.HIGHEST)
        control_qubit = (patch_ids < mates)[:, None, None, None]
        updated = (lattice_portion.astype(jnp.float32) + jnp.where(control_qubit, control_contribution, targ_term)).astype(jnp.bfloat16)
        activation_maps = lax.dynamic_update_index_in_dim(activation_maps, updated, moment, 1)
    return activation_maps


def reference(bits, partners, gate_round, first_kernel, second_kernels, conv_bias, couple_down, couple_up, head, cell_bias):
    kernel_one = first_kernel.astype(jnp.float32)[:, :, :, None, :]
    kernel_two = second_kernels[0].astype(jnp.float32)
    kernel_three = second_kernels[1].astype(jnp.float32)
    head_f = head.astype(jnp.float32)
    offsets = cell_bias.reshape(HEIGHT, WIDTH)

    def layer_one(volume):
        return jax.nn.relu(convolve(volume, kernel_one) + conv_bias[0]).astype(jnp.bfloat16)

    def layer_two(volume):
        base = volume.astype(jnp.float32)
        return (jax.nn.relu(convolve(base, kernel_two) + conv_bias[1]) + base).astype(jnp.bfloat16)

    def layer_three(volume):
        base = volume.astype(jnp.float32)
        intermediate_activations = jax.nn.relu(convolve(base, kernel_three) + conv_bias[2]) + base
        logits = jnp.einsum("rhwc,c->rhw", intermediate_activations, head_f, precision=lax.Precision.HIGHEST) + offsets
        return logits.reshape(logits.shape[0], HEIGHT * WIDTH)

    first = lax.map(layer_one, bits.astype(jnp.float32)[..., None])
    coupled_one = couple(first, partners, gate_round, couple_down[0], couple_up[0, 0], couple_up[0, 1])
    second = lax.map(layer_two, coupled_one)
    linked_pair_output = couple(second, partners, gate_round, couple_down[1], couple_up[1, 0], couple_up[1, 1])
    return lax.map(layer_three, linked_pair_output)
```

```python
import functools

import jax
import jax.numpy as jnp
from jax import lax
from jax.experimental import pallas as pl
from jax.experimental.pallas import tpu as pltpu
from jax.sharding import PartitionSpec as P

F32 = jnp.float32
BF16 = jnp.bfloat16
LANES = 128
COUNT = 4
DEPTH = 2
HEIGHT = 26
WIDTH = 24
CHANS = 32
WINDOW = 6
SLOTS = 8
BLOCKS = WIDTH // WINDOW
WIDE = SLOTS * CHANS
FLAT = 640
OWN, MATE, UNITS = 24, 16, 96
HALF = HEIGHT // 2


def iota(shape, dim):
    return lax.broadcasted_iota(jnp.int32, shape, dim)


def rounded(x):
    return x.astype(BF16).astype(F32)


def dot(a, b):
    return jnp.dot(a, b, preferred_element_type=F32)


def pack_kernel(bits_ref, partners_ref, gate_ref, out_ref):
    units = COUNT * DEPTH
    bits = bits_ref[...].reshape(units, HEIGHT, WIDTH).astype(F32)
    rows = [bits[:, y, :] for y in range(HEIGHT)]
    flat = jnp.concatenate(rows + [jnp.zeros((units, FLAT - HEIGHT * WIDTH), F32)], axis=1)
    out_ref[:, :FLAT] = flat.astype(BF16)
    patches = partners_ref.shape[1]
    names = partners_ref[...].astype(F32)
    if patches < LANES:
        names = jnp.concatenate([names, jnp.full((1, LANES - patches), -1.0, F32)], axis=1)
    moment = jnp.full((1, LANES), gate_ref[0], jnp.int32).astype(F32)
    sub = iota((units, LANES), 0)
    out_ref[:, FLAT:] = jnp.where(sub == 0, names, jnp.where(sub == 1, moment, 0.0)).astype(BF16)


def weights_kernel(
    first_ref, second_ref, bias_ref, down_ref, up_ref, head_ref,
    wf_ref, w2_ref, w3_ref, dn_ref, un_ref, rd_ref, bs_ref, scr_ref,
):
    total = BLOCKS * WIDE
    spread = (iota((CHANS, WIDE), 1) % CHANS == iota((CHANS, WIDE), 0)).astype(BF16)
    slot = iota((CHANS, WIDE), 1) // CHANS
    inner = (slot >= 1) & (slot <= WINDOW)
    for layer, w_ref in enumerate((w2_ref, w3_ref)):
        for tap in range(9):
            base = (layer * 27 + tap * 3) * CHANS
            tiled = dot(second_ref[base : base + 3 * CHANS, :], spread)
            for kc in range(SLOTS):
                block = jnp.zeros((CHANS, WIDE), F32)
                for dc in range(3):
                    block = jnp.where(
                        inner & (slot == kc - dc + 1), tiled[dc * CHANS : (dc + 1) * CHANS], block
                    )
                w_ref[tap * WIDE + kc * CHANS : tap * WIDE + (kc + 1) * CHANS, :] = block.astype(BF16)
    across = (iota((CHANS, total), 1) % CHANS == iota((CHANS, total), 0)).astype(BF16)
    taps = dot(first_ref[...], across)
    lane = iota((WIDTH, total), 1)
    column = (lane // WIDE) * WINDOW - 1 + (lane % WIDE) // CHANS
    real = (column >= 0) & (column < WIDTH)
    offset = iota((WIDTH, total), 0) - column + 1
    for pair in range(9):
        block = jnp.zeros((WIDTH, total), F32)
        for dc in range(3):
            block = jnp.where(real & (offset == dc), taps[pair * 3 + dc : pair * 3 + dc + 1, :], block)
        scr_ref[pair * WIDTH : (pair + 1) * WIDTH, :] = block
    scr_ref[9 * WIDTH :, :] = jnp.zeros((WIDE - 9 * WIDTH, total), F32)
    wf_ref[...] = scr_ref[...].astype(BF16)
    latent = down_ref.shape[1]
    low = SLOTS * latent
    thin = (iota((latent, low), 1) % latent == iota((latent, low), 0)).astype(BF16)
    for layer in range(2):
        tiled = dot(down_ref[layer * CHANS : (layer + 1) * CHANS, :], thin)
        for kc in range(SLOTS):
            keep = iota((CHANS, low), 1) // latent == kc
            dn_ref[layer * WIDE + kc * CHANS : layer * WIDE + (kc + 1) * CHANS, :] = jnp.where(
                keep, tiled, 0.0
            ).astype(BF16)
        for role in range(2):
            at = (layer * 2 + role) * latent
            tiled = dot(up_ref[at : at + latent, :], spread)
            for kc in range(SLOTS):
                keep = iota((latent, WIDE), 1) // CHANS == kc
                top = (layer * 2 + role) * low + kc * latent
                un_ref[top : top + latent, :] = jnp.where(keep, tiled, 0.0).astype(BF16)
    row = iota((total, CHANS), 0)
    chosen = jnp.where(row % CHANS == iota((total, CHANS), 1), head_ref[...].astype(F32), 0.0)
    values = dot(chosen.astype(BF16), jnp.ones((CHANS, LANES), BF16))
    row = iota((total, LANES), 0)
    place = (row % WIDE) // CHANS
    target = (row // WIDE) * WINDOW - 1 + place
    keep = (place >= 1) & (place <= WINDOW) & (target == iota((total, LANES), 1))
    rd_ref[...] = jnp.where(keep, values, 0.0).astype(BF16)
    biases = jnp.dot(
        bias_ref[...], across.astype(F32), preferred_element_type=F32, precision=lax.Precision.HIGHEST
    )
    lane = iota((8, total), 1)
    place = (lane % WIDE) // CHANS
    column = (lane // WIDE) * WINDOW - 1 + place
    real = (column >= 0) & (column < WIDTH)
    inside = (place >= 1) & (place <= WINDOW)
    top = iota((8, total), 0) == 0
    keep = (top & real) | (~top & inside)
    bs_ref[...] = jnp.where(keep, biases, 0.0)


def window_rows(gathered, y, lane):
    start = WIDTH * (y - 1)
    length = 3 * WIDTH
    tiles = [None, None]
    for dt in range(3):
        begin = length * dt
        shift = begin - start
        for src in range(FLAT // LANES):
            lo = max(start, 0, src * LANES)
            hi = min(start + length, FLAT, (src + 1) * LANES)
            if lo >= hi:
                continue
            source = gathered[dt][:, src * LANES : (src + 1) * LANES]
            turned = pltpu.roll(source, shift % LANES, 1) if shift % LANES else source
            for dst in range(2):
                a = max(lo + shift, dst * LANES) - dst * LANES
                b = min(hi + shift, (dst + 1) * LANES) - dst * LANES
                if a >= b:
                    continue
                old = jnp.zeros_like(turned) if tiles[dst] is None else tiles[dst]
                tiles[dst] = jnp.where((lane >= a) & (lane < b), turned, old)
    return tiles


def main_kernel(
    sizes, all_ref, meta_ref, wf_ref, w2_ref, w3_ref, dn_ref, un_ref, rd_ref, bs_ref, cell_ref,
    out_ref, x_ref, f_ref, s_ref, c2_ref, s3_ref,
):
    devices, steps, exact = sizes
    near = meta_ref.shape[0] // 8
    me = lax.axis_index("patch")
    now = lax.axis_index("tm")
    sub = iota((8, LANES), 0)
    low_half = sub < 4

    names, moments = [], []
    for j in range(3):
        there = now - 1 + j
        valid = (there >= 0) & (there < steps)
        safe = jnp.clip(there, 0, steps - 1)
        block = (safe ^ now) if exact else (2, 0, 1)[j]
        tile = meta_ref[pl.ds(pl.multiple_of(block * 8, 8), 8), :].astype(F32).astype(jnp.int32)
        names.append(jnp.where(valid, tile[0:1, :], -1))
        moments.append(jnp.broadcast_to(jnp.where(valid, tile[1:2, :], -1000), (8, LANES)))
    first_round = 2 * now - 2
    own_patch = COUNT * me + sub % COUNT

    def pair(parts):
        return jnp.concatenate(
            [jnp.where(low_half, parts[0], parts[1]), jnp.where(low_half, parts[1], parts[2])], axis=0
        )

    hot = [(jnp.broadcast_to(names[j], (8, LANES)) == own_patch).astype(F32) for j in range(3)]
    hot24 = jnp.concatenate(hot, axis=0).astype(BF16)
    hot16f = pair(hot)
    hot16 = hot16f.astype(BF16)
    square = iota((LANES, LANES), 0)
    even = moments[1] == 2 * now
    other = jnp.where(even[0:1, :], names[0], names[2])
    perm_one = (square == names[1]).astype(BF16)
    perm_other = (square == other).astype(BF16)
    middle = (iota((16, LANES), 0) >= 4) & (iota((16, LANES), 0) < 12)
    hot_far = jnp.where(middle, dot(hot16, perm_other), dot(hot16, perm_one))
    hots = jnp.concatenate([hot24, hot_far.astype(BF16), hot16], axis=0)
    index = dot(hots, square.astype(F32).astype(BF16)).astype(jnp.int32)
    mate24, far16, mate16 = index[0:24], index[24:40], index[40:56]
    own24 = jnp.concatenate([own_patch] * 3, axis=0)
    own16 = jnp.concatenate([own_patch] * 2, axis=0)

    moment24 = jnp.concatenate(moments, axis=0)
    moment16 = pair(moments)
    round24 = first_round + iota((24, LANES), 0) // 4
    round16 = first_round + 1 + iota((16, LANES), 0) // 4
    last = DEPTH * steps - 1
    step_far = pair([jnp.full((8, LANES), 1, jnp.int32), jnp.where(even, -1, 1), jnp.full((8, LANES), -1, jnp.int32)])
    moment_far = pair([moments[1], jnp.where(even, moments[0], moments[2]), moments[1]])
    touches = moment_far == moment16 + step_far
    far_low = touches & (step_far < 0)
    far_high = touches & (step_far > 0)

    columns = all_ref.shape[0]
    col = iota((1, columns), 1)
    block = col // (8 * near)
    half = devices // 2
    source = me ^ (2 * (block % half) + block // half) if devices > 1 else me + 0 * block
    patch_of = COUNT * source + (col % 8) // DEPTH
    step = (col // 8) % near
    if exact:
        time_of = now ^ step
    else:
        time_of = now + jnp.where(step == 1, 1, jnp.where(step == 2, -1, jnp.where(step == 3, 2, jnp.where(step == 4, -2, 0))))
    round_of = DEPTH * time_of + col % DEPTH
    expand = (iota((LANES, columns), 0) == patch_of).astype(BF16)
    spread = dot(hots, expand)

    def lanes_of(x):
        return jnp.broadcast_to(x[:, :1], (x.shape[0], columns))

    is_own = (patch_of == lanes_of(own24)).astype(F32)
    patch_sel = jnp.concatenate(
        [is_own, spread[0:24], spread[24:40], spread[40:56], spread[40:56]], axis=0
    )
    want = jnp.concatenate(
        [
            lanes_of(round24),
            lanes_of(moment24),
            lanes_of(moment16 + step_far),
            lanes_of(moment16 - 1),
            lanes_of(moment16 + 1),
        ],
        axis=0,
    )
    gathered = []
    for dt in range(3):
        choose = jnp.where(round_of == want + (dt - 1), patch_sel, 0.0).astype(BF16)
        gathered.append(dot(choose, all_ref[...]))
    lane = iota((UNITS, LANES), 1)
    for y in range(HEIGHT):
        tiles = window_rows(gathered, y, lane)
        x_ref[y * UNITS : (y + 1) * UNITS, :] = jnp.concatenate(tiles, axis=1).astype(BF16)

    s_ref[:, 0:32, :] = jnp.zeros((3, 32, WIDE), BF16)
    s_ref[:, 27 * 32 :, :] = jnp.zeros((3, 32, WIDE), BF16)

    def wide(mask):
        return jnp.concatenate([mask.astype(jnp.int32)] * 2, axis=1) != 0

    ctrl_up = jnp.concatenate([mate24 - own24, own16 - mate16, far16 - mate16], axis=0) > 0
    gate24 = wide(round24 == moment24)
    gate16 = wide(round16 == moment16)
    ok24 = wide((round24 >= 0) & (round24 <= last))
    ok16 = wide((round16 >= 0) & (round16 <= last))
    ok_low = wide((moment16 - 1 >= 0) & (moment16 - 1 <= last))
    ok_high = wide((moment16 + 1 >= 0) & (moment16 + 1 <= last))
    far_low, far_high = wide(far_low), wide(far_high)
    ctrl_own16 = own16 < mate16
    at_moment = round24 == moment24

    def swap(x):
        return pltpu.roll(x, 4, 0)

    def body(b, carry):
        lanes = pl.ds(pl.multiple_of(b * WIDE, WIDE), WIDE)
        bias1 = bs_ref[0:1, lanes]
        bias2 = bs_ref[1:2, lanes]
        total = dot(x_ref[...], wf_ref[:, lanes])
        f_ref[...] = rounded(jnp.maximum(total + bias1, 0.0)).reshape(HEIGHT, UNITS, WIDE)
        packed = f_ref[:, 0:64, :].reshape(HEIGHT * 64, WIDE).astype(BF16)
        latent = rounded(dot(packed, dn_ref[0:WIDE, :])).reshape(HEIGHT, 64, LANES)
        rows = []
        for y in range(HEIGHT):
            lat = latent[y]
            mine = [lat[8 * j : 8 * j + 8] for j in range(3)]
            mine = [jnp.where(at_moment[8 * j : 8 * j + 8], mine[j], swap(mine[j])) for j in range(3)]
            rows.append(jnp.concatenate([lat[24:48], pair(mine), lat[48:64]], axis=0))
        given = jnp.stack(rows, axis=0)
        both = jnp.concatenate(
            [jnp.where(ctrl_up, given, 0.0), jnp.where(ctrl_up, 0.0, given)], axis=2
        ).reshape(HEIGHT * 56, WIDE)
        added = dot(both.astype(BF16), un_ref[0:WIDE, :]).reshape(HEIGHT, 56, WIDE)
        half_mask = wide(low_half)
        for y in range(HEIGHT):
            here = f_ref[y]
            add = added[y]
            own = rounded(here[0:24] + jnp.where(gate24, add[0:24], 0.0))
            own = jnp.where(ok24, own, 0.0)
            m = [here[24 + 8 * j : 32 + 8 * j] for j in range(3)]
            mid = jnp.concatenate(
                [jnp.where(half_mask, m[0], m[1]), jnp.where(half_mask, m[1], m[2])], axis=0
            )
            mid = rounded(mid + add[24:40])
            far = add[40:56]
            lower = jnp.where(ok_low, rounded(here[64:80] + jnp.where(far_low, far, 0.0)), 0.0)
            upper = jnp.where(ok_high, rounded(here[80:96] + jnp.where(far_high, far, 0.0)), 0.0)
            turned = [swap(own[8 * j : 8 * j + 8]) for j in range(3)]
            center = jnp.concatenate(
                [jnp.where(half_mask, turned[0], turned[1]), jnp.where(half_mask, turned[1], turned[2])], axis=0
            )
            top = (y + 1) * 32
            s_ref[0, top : top + 32, :] = jnp.concatenate([own[0:16], lower], axis=0).astype(BF16)
            s_ref[1, top : top + 32, :] = jnp.concatenate([center, mid], axis=0).astype(BF16)
            s_ref[2, top : top + 32, :] = jnp.concatenate([own[8:24], upper], axis=0).astype(BF16)
        size = HEIGHT * 32
        acc = jnp.zeros((size, WIDE), F32)
        for tap in range(9):
            dt, dr = divmod(tap, 3)
            acc = acc + dot(
                s_ref[dt, dr * 32 : dr * 32 + size, :], w2_ref[tap * WIDE : (tap + 1) * WIDE, :]
            )
        second = jnp.maximum(acc + bias2, 0.0) + s_ref[1, 32 : 32 + size, :].astype(F32)
        second = second.reshape(HEIGHT, 32, WIDE)
        mates = second[:, 16:32, :].reshape(HEIGHT * 16, WIDE).astype(BF16)
        latent = rounded(dot(mates, dn_ref[WIDE:, :])).reshape(HEIGHT, 16, LANES)
        both = jnp.concatenate(
            [jnp.where(ctrl_own16, latent, 0.0), jnp.where(ctrl_own16, 0.0, latent)], axis=2
        ).reshape(HEIGHT * 16, WIDE)
        added = dot(both.astype(BF16), un_ref[WIDE:, :]).reshape(HEIGHT, 16, WIDE)
        two = rounded(rounded(second[:, 0:16, :]) + jnp.where(gate16, added, 0.0))
        c2_ref[b] = jnp.where(ok16, two, 0.0)
        return carry

    lax.fori_loop(0, BLOCKS, body, 0)

    lane8 = iota((8, LANES), 1)

    def placed(y, dt):
        if y < 0 or y >= HEIGHT:
            return jnp.zeros((8, BLOCKS * WIDE), F32)
        tiles = []
        for b in range(BLOCKS):
            for t in range(2):
                group = c2_ref[b, y, :, t * LANES : (t + 1) * LANES]
                if t == 0:
                    old = pltpu.roll(c2_ref[b - 1, y, :, LANES:], 64, 1) if b else jnp.zeros((16, LANES), F32)
                    group = jnp.where(iota((16, LANES), 1) < CHANS, old, group)
                else:
                    old = pltpu.roll(c2_ref[b + 1, y, :, :LANES], 64, 1) if b + 1 < BLOCKS else jnp.zeros((16, LANES), F32)
                    group = jnp.where(iota((16, LANES), 1) >= LANES - CHANS, old, group)
                if dt == 0:
                    group = group[0:8]
                elif dt == 2:
                    group = group[8:16]
                else:
                    group = jnp.where(low_half, swap(group[0:8]), swap(group[8:16]))
                tiles.append(group)
        return jnp.concatenate(tiles, axis=1)

    for dt in range(3):
        for r in range(HALF + 2):
            s3_ref[dt, r * 16 : (r + 1) * 16, :] = jnp.concatenate(
                [placed(r - 1, dt), placed(r + HALF - 1, dt)], axis=0
            ).astype(BF16)

    size = HALF * 16
    logits = jnp.zeros((size, LANES), F32)
    for b in range(BLOCKS):
        lanes = slice(b * WIDE, (b + 1) * WIDE)
        acc = jnp.zeros((size, WIDE), F32)
        for tap in range(9):
            dt, dr = divmod(tap, 3)
            acc = acc + dot(
                s3_ref[dt, dr * 16 : dr * 16 + size, lanes], w3_ref[tap * WIDE : (tap + 1) * WIDE, :]
            )
        third = jnp.maximum(acc + bs_ref[2:3, lanes], 0.0) + s3_ref[1, 16 : 16 + size, lanes].astype(F32)
        high = third.astype(BF16)
        rest = (third - high.astype(F32)).astype(BF16)
        logits = logits + dot(high, rd_ref[lanes, :]) + dot(rest, rd_ref[lanes, :])
    logits = logits.reshape(HALF, 16, LANES)
    flat = [jnp.zeros((8, LANES), F32) for _ in range(FLAT // LANES)]
    for y in range(HEIGHT):
        row = logits[y % HALF, (y // HALF) * 8 : (y // HALF) * 8 + 8]
        begin = y * WIDTH
        turned = pltpu.roll(row, begin % LANES, 1) if begin % LANES else row
        for dst in range(FLAT // LANES):
            a = max(begin, dst * LANES) - dst * LANES
            e = min(begin + WIDTH, (dst + 1) * LANES) - dst * LANES
            if a < e:
                flat[dst] = jnp.where((lane8 >= a) & (lane8 < e), turned, flat[dst])
    flat = jnp.concatenate(flat, axis=1)[:, : HEIGHT * WIDTH] + cell_ref[...]
    for j in range(DEPTH):
        for p in range(COUNT):
            out_ref[p, j : j + 1, :] = flat[4 * j + p : 4 * j + p + 1, :]


def swapped(block, axis, mask):
    count = lax.axis_size(axis)
    return lax.ppermute(block, axis, [(i, i ^ mask) for i in range(count)])


def shifted(block, axis, offset):
    count = lax.axis_size(axis)
    return lax.ppermute(block, axis, [(i, i - offset) for i in range(count) if 0 <= i - offset < count])


def shards(
    bits, partners, gate_round, first_kernel, second_kernels, conv_bias, couple_down, couple_up, head, cell_bias
):
    devices, steps = lax.axis_size("patch"), lax.axis_size("tm")
    latent = couple_down.shape[-1]
    total = BLOCKS * WIDE
    vmem = pl.BlockSpec(memory_space=pltpu.VMEM)
    smem = pl.BlockSpec(memory_space=pltpu.SMEM)
    mine = pl.pallas_call(
        pack_kernel,
        out_shape=jax.ShapeDtypeStruct((8, FLAT + LANES), BF16),
        in_specs=[vmem, vmem, smem],
        out_specs=vmem,
        name="pack",
    )(bits, partners, gate_round)

    exact = steps <= 4
    if exact:
        blocks = [mine] + [
            lax.ppermute(mine, "tm", [(i, i ^ k) for i in range(steps) if abs(i - (i ^ k)) <= 2])
            for k in range(1, steps)
        ]
    else:
        blocks = [mine] + [shifted(mine, "tm", k) for k in (1, -1, 2, -2)]
    near = jnp.concatenate(blocks, axis=0)
    meta = near[:, FLAT:]
    every = near[:, :FLAT]
    parts = [every] + [swapped(every, "patch", 2 * m) for m in range(1, devices // 2)]
    every = jnp.concatenate(parts, axis=0)
    every = jnp.concatenate([every, swapped(every, "patch", 1)], axis=0)

    weights = pl.pallas_call(
        weights_kernel,
        out_shape=[
            jax.ShapeDtypeStruct((WIDE, total), BF16),
            jax.ShapeDtypeStruct((9 * WIDE, WIDE), BF16),
            jax.ShapeDtypeStruct((9 * WIDE, WIDE), BF16),
            jax.ShapeDtypeStruct((2 * WIDE, SLOTS * latent), BF16),
            jax.ShapeDtypeStruct((4 * SLOTS * latent, WIDE), BF16),
            jax.ShapeDtypeStruct((total, LANES), BF16),
            jax.ShapeDtypeStruct((8, total), F32),
        ],
        in_specs=[vmem] * 6,
        out_specs=[vmem] * 7,
        scratch_shapes=[pltpu.VMEM((WIDE, total), F32)],
        cost_estimate=pl.CostEstimate(flops=10**9, bytes_accessed=10**7, transcendentals=0),
        name="weights",
    )(
        first_kernel.reshape(27, CHANS),
        second_kernels.reshape(54 * CHANS, CHANS),
        jnp.pad(conv_bias, ((0, 5), (0, 0))),
        couple_down.reshape(2 * CHANS, latent),
        couple_up.reshape(4 * latent, CHANS),
        head.reshape(1, CHANS),
    )

    return pl.pallas_call(
        functools.partial(main_kernel, (devices, steps, exact)),
        out_shape=jax.ShapeDtypeStruct((COUNT, DEPTH, HEIGHT * WIDTH), F32),
        in_specs=[vmem] * 10,
        out_specs=vmem,
        scratch_shapes=[
            pltpu.VMEM((HEIGHT * UNITS, WIDE), BF16),
            pltpu.VMEM((HEIGHT, UNITS, WIDE), F32),
            pltpu.VMEM((3, 28 * 32, WIDE), BF16),
            pltpu.VMEM((BLOCKS, HEIGHT, 16, WIDE), F32),
            pltpu.VMEM((3, (HALF + 2) * 16, total), BF16),
        ],
        name="decode",
    )(every, meta, *weights, cell_bias.reshape(1, HEIGHT * WIDTH))


def solution(mesh):
    in_specs = (
        P("patch", "tm", None, None),
        P("tm", None),
        P("tm"),
        P(),
        P(),
        P(),
        P(),
        P(),
        P(),
        P(),
    )
    out_specs = P("patch", "tm", None)
    return jax.shard_map(shards, mesh=mesh, in_specs=in_specs, out_specs=out_specs, check_vma=False)
```

```python
import functools

import jax
import jax.numpy as jnp
from jax import lax
from jax.experimental import pallas as pl
from jax.experimental.pallas import tpu as pltpu
from jax.sharding import PartitionSpec as P

F32 = jnp.float32
BF16 = jnp.bfloat16
LANES = 128
COUNT = 4
DEPTH = 2
HEIGHT = 26
WIDTH = 24
CHANS = 32
WINDOW = 6
SLOTS = 8
BLOCKS = WIDTH // WINDOW
WIDE = SLOTS * CHANS
FLAT = 640
OWN, MATE, UNITS = 24, 16, 96
HALF = HEIGHT // 2


def iota(shape, dim):
    return lax.broadcasted_iota(jnp.int32, shape, dim)


def rounded(x):
    return x.astype(BF16).astype(F32)


def dot(a, b):
    return jnp.dot(a, b, preferred_element_type=F32)


def fetch(pairs, sems):
    copies = [pltpu.make_async_copy(src, dst, sems.at[i]) for i, (src, dst) in enumerate(pairs)]
    for copy in copies:
        copy.start()
    for copy in copies:
        copy.wait()


def pack_kernel(bits_hbm, partners_hbm, gate_ref, out_ref, bits_ref, partners_ref, sems):
    fetch(((bits_hbm, bits_ref), (partners_hbm, partners_ref)), sems)
    units = COUNT * DEPTH
    bits = bits_ref[...].reshape(units, WIDTH, HEIGHT).astype(F32)
    bits = jnp.swapaxes(bits, 1, 2)
    rows = [bits[:, y, :] for y in range(HEIGHT)]
    flat = jnp.concatenate(rows + [jnp.zeros((units, FLAT - HEIGHT * WIDTH), F32)], axis=1)
    out_ref[:, :FLAT] = flat.astype(BF16)
    patches = partners_ref.shape[1]
    names = partners_ref[...].astype(F32)
    if patches < LANES:
        names = jnp.concatenate([names, jnp.full((1, LANES - patches), -1.0, F32)], axis=1)
    moment = jnp.full((1, LANES), gate_ref[0], jnp.int32).astype(F32)
    sub = iota((units, LANES), 0)
    out_ref[:, FLAT:] = jnp.where(sub == 0, names, jnp.where(sub == 1, moment, 0.0)).astype(BF16)


def weights_kernel(
    first_hbm, second_hbm, bias_hbm, down_hbm, up_hbm, head_hbm,
    wf_ref, w2_ref, w3_ref, dn_ref, un_ref, rd_ref, bs_ref,
    scr_ref, first_ref, second_ref, bias_ref, down_ref, up_ref, head_ref, sems,
):
    sources = (first_hbm, second_hbm, bias_hbm, down_hbm, up_hbm, head_hbm)
    fetch(zip(sources, (first_ref, second_ref, bias_ref, down_ref, up_ref, head_ref)), sems)
    total = BLOCKS * WIDE
    spread = (iota((CHANS, WIDE), 1) % CHANS == iota((CHANS, WIDE), 0)).astype(BF16)
    slot = iota((CHANS, WIDE), 1) // CHANS
    inner = (slot >= 1) & (slot <= WINDOW)
    for layer, w_ref in enumerate((w2_ref, w3_ref)):
        for tap in range(9):
            base = (layer * 27 + tap * 3) * CHANS
            tiled = dot(second_ref[base : base + 3 * CHANS, :], spread)
            for kc in range(SLOTS):
                block = jnp.zeros((CHANS, WIDE), F32)
                for dc in range(3):
                    block = jnp.where(
                        inner & (slot == kc - dc + 1), tiled[dc * CHANS : (dc + 1) * CHANS], block
                    )
                w_ref[tap * WIDE + kc * CHANS : tap * WIDE + (kc + 1) * CHANS, :] = block.astype(BF16)
    across = (iota((CHANS, total), 1) % CHANS == iota((CHANS, total), 0)).astype(BF16)
    for pair in range(9):
        scr_ref[8 * pair : 8 * pair + 3, :CHANS] = first_ref[pair // 3, pair % 3].astype(F32)
    taps = dot(scr_ref[0:72, :CHANS].astype(BF16), across)
    lane = iota((WIDTH, total), 1)
    column = (lane // WIDE) * WINDOW - 1 + (lane % WIDE) // CHANS
    real = (column >= 0) & (column < WIDTH)
    offset = iota((WIDTH, total), 0) - column + 1
    for pair in range(9):
        block = jnp.zeros((WIDTH, total), F32)
        for dc in range(3):
            block = jnp.where(real & (offset == dc), taps[pair * 8 + dc : pair * 8 + dc + 1, :], block)
        scr_ref[pair * WIDTH : (pair + 1) * WIDTH, :] = block
    scr_ref[9 * WIDTH :, :] = jnp.zeros((WIDE - 9 * WIDTH, total), F32)
    wf_ref[...] = scr_ref[...].astype(BF16)
    latent = down_ref.shape[1]
    low = SLOTS * latent
    thin = (iota((latent, low), 1) % latent == iota((latent, low), 0)).astype(BF16)
    for layer in range(2):
        tiled = lax.dot_general(
            down_ref[layer], thin, (((0,), (0,)), ((), ())), preferred_element_type=F32
        )
        for kc in range(SLOTS):
            keep = iota((CHANS, low), 1) // latent == kc
            dn_ref[layer * WIDE + kc * CHANS : layer * WIDE + (kc + 1) * CHANS, :] = jnp.where(
                keep, tiled, 0.0
            ).astype(BF16)
        for role in range(2):
            tiled = dot(up_ref[layer, role], spread)
            for kc in range(SLOTS):
                keep = iota((latent, WIDE), 1) // CHANS == kc
                top = (layer * 2 + role) * low + kc * latent
                un_ref[top : top + latent, :] = jnp.where(keep, tiled, 0.0).astype(BF16)
    row = iota((total, CHANS), 0)
    chosen = jnp.where(row % CHANS == iota((total, CHANS), 1), head_ref[...].astype(F32), 0.0)
    values = dot(chosen.astype(BF16), jnp.ones((CHANS, LANES), BF16))
    row = iota((total, LANES), 0)
    place = (row % WIDE) // CHANS
    target = (row // WIDE) * WINDOW - 1 + place
    keep = (place >= 1) & (place <= WINDOW) & (target == iota((total, LANES), 1))
    rd_ref[...] = jnp.where(keep, values, 0.0).astype(BF16)
    scr_ref[0:8, :CHANS] = jnp.zeros((8, CHANS), F32)
    scr_ref[0:3, :CHANS] = bias_ref[...]
    biases = jnp.dot(
        scr_ref[0:8, :CHANS], across.astype(F32), preferred_element_type=F32, precision=lax.Precision.HIGHEST
    )
    lane = iota((8, total), 1)
    place = (lane % WIDE) // CHANS
    column = (lane // WIDE) * WINDOW - 1 + place
    real = (column >= 0) & (column < WIDTH)
    inside = (place >= 1) & (place <= WINDOW)
    top = iota((8, total), 0) == 0
    keep = (top & real) | (~top & inside)
    bs_ref[...] = jnp.where(keep, biases, 0.0)


def window_rows(gathered, y, lane):
    start = WIDTH * (y - 1)
    length = 3 * WIDTH
    tiles = [None, None]
    for dt in range(3):
        begin = length * dt
        shift = begin - start
        for src in range(FLAT // LANES):
            lo = max(start, 0, src * LANES)
            hi = min(start + length, FLAT, (src + 1) * LANES)
            if lo >= hi:
                continue
            source = gathered[dt][:, src * LANES : (src + 1) * LANES]
            turned = pltpu.roll(source, shift % LANES, 1) if shift % LANES else source
            for dst in range(2):
                a = max(lo + shift, dst * LANES) - dst * LANES
                b = min(hi + shift, (dst + 1) * LANES) - dst * LANES
                if a >= b:
                    continue
                old = jnp.zeros_like(turned) if tiles[dst] is None else tiles[dst]
                tiles[dst] = jnp.where((lane >= a) & (lane < b), turned, old)
    return tiles


def main_kernel(
    sizes, here_ref, there_ref, meta_ref, wf_ref, w2_ref, w3_ref, dn_ref, un_ref, rd_ref, bs_ref, cell_ref,
    out_ref, x_ref, f_ref, s_ref, c2_ref, s3_ref,
):
    devices, steps, exact = sizes
    near = meta_ref.shape[0] // 8
    me = lax.axis_index("patch")
    now = lax.axis_index("tm")
    sub = iota((8, LANES), 0)
    low_half = sub < 4

    names, moments = [], []
    for j in range(3):
        there = now - 1 + j
        valid = (there >= 0) & (there < steps)
        safe = jnp.clip(there, 0, steps - 1)
        block = (safe ^ now) if exact else (2, 0, 1)[j]
        tile = meta_ref[pl.ds(pl.multiple_of(block * 8, 8), 8), FLAT:].astype(F32).astype(jnp.int32)
        names.append(jnp.where(valid, tile[0:1, :], -1))
        moments.append(jnp.broadcast_to(jnp.where(valid, tile[1:2, :], -1000), (8, LANES)))
    first_round = 2 * now - 2
    own_patch = COUNT * me + sub % COUNT

    def pair(parts):
        return jnp.concatenate(
            [jnp.where(low_half, parts[0], parts[1]), jnp.where(low_half, parts[1], parts[2])], axis=0
        )

    hot = [(jnp.broadcast_to(names[j], (8, LANES)) == own_patch).astype(F32) for j in range(3)]
    hot24 = jnp.concatenate(hot, axis=0).astype(BF16)
    hot16f = pair(hot)
    hot16 = hot16f.astype(BF16)
    square = iota((LANES, LANES), 0)
    even = moments[1] == 2 * now
    other = jnp.where(even[0:1, :], names[0], names[2])
    perm_one = (square == names[1]).astype(BF16)
    perm_other = (square == other).astype(BF16)
    middle = (iota((16, LANES), 0) >= 4) & (iota((16, LANES), 0) < 12)
    hot_far = jnp.where(middle, dot(hot16, perm_other), dot(hot16, perm_one))
    hots = jnp.concatenate([hot24, hot_far.astype(BF16), hot16], axis=0)
    index = dot(hots, square.astype(F32).astype(BF16)).astype(jnp.int32)
    mate24, far16, mate16 = index[0:24], index[24:40], index[40:56]
    own24 = jnp.concatenate([own_patch] * 3, axis=0)
    own16 = jnp.concatenate([own_patch] * 2, axis=0)

    moment24 = jnp.concatenate(moments, axis=0)
    moment16 = pair(moments)
    round24 = first_round + iota((24, LANES), 0) // 4
    round16 = first_round + 1 + iota((16, LANES), 0) // 4
    last = DEPTH * steps - 1
    step_far = pair([jnp.full((8, LANES), 1, jnp.int32), jnp.where(even, -1, 1), jnp.full((8, LANES), -1, jnp.int32)])
    moment_far = pair([moments[1], jnp.where(even, moments[0], moments[2]), moments[1]])
    touches = moment_far == moment16 + step_far
    far_low = touches & (step_far < 0)
    far_high = touches & (step_far > 0)

    columns = 2 * here_ref.shape[0]
    events = jnp.concatenate([here_ref[...], there_ref[...]], axis=0)
    col = iota((1, columns), 1)
    block = col // (8 * near)
    half = devices // 2
    source = me ^ (2 * (block % half) + block // half) if devices > 1 else me + 0 * block
    patch_of = COUNT * source + (col % 8) // DEPTH
    step = (col // 8) % near
    if exact:
        time_of = now ^ step
    else:
        time_of = now + jnp.where(step == 1, 1, jnp.where(step == 2, -1, jnp.where(step == 3, 2, jnp.where(step == 4, -2, 0))))
    round_of = DEPTH * time_of + col % DEPTH
    expand = (iota((LANES, columns), 0) == patch_of).astype(BF16)
    spread = dot(hots, expand)

    def lanes_of(x):
        return jnp.broadcast_to(x[:, :1], (x.shape[0], columns))

    is_own = (patch_of == lanes_of(own24)).astype(F32)
    patch_sel = jnp.concatenate(
        [is_own, spread[0:24], spread[24:40], spread[40:56], spread[40:56]], axis=0
    )
    want = jnp.concatenate(
        [
            lanes_of(round24),
            lanes_of(moment24),
            lanes_of(moment16 + step_far),
            lanes_of(moment16 - 1),
            lanes_of(moment16 + 1),
        ],
        axis=0,
    )
    gathered = []
    for dt in range(3):
        choose = jnp.where(round_of == want + (dt - 1), patch_sel, 0.0).astype(BF16)
        gathered.append(dot(choose, events))
    lane = iota((UNITS, LANES), 1)
    for y in range(HEIGHT):
        tiles = window_rows(gathered, y, lane)
        x_ref[y * UNITS : (y + 1) * UNITS, :] = jnp.concatenate(tiles, axis=1).astype(BF16)

    s_ref[:, 0:32, :] = jnp.zeros((3, 32, WIDE), BF16)
    s_ref[:, 27 * 32 :, :] = jnp.zeros((3, 32, WIDE), BF16)

    def wide(mask):
        return jnp.concatenate([mask.astype(jnp.int32)] * 2, axis=1) != 0

    ctrl_up = jnp.concatenate([mate24 - own24, own16 - mate16, far16 - mate16], axis=0) > 0
    gate24 = wide(round24 == moment24)
    gate16 = wide(round16 == moment16)
    ok24 = wide((round24 >= 0) & (round24 <= last))
    ok16 = wide((round16 >= 0) & (round16 <= last))
    ok_low = wide((moment16 - 1 >= 0) & (moment16 - 1 <= last))
    ok_high = wide((moment16 + 1 >= 0) & (moment16 + 1 <= last))
    far_low, far_high = wide(far_low), wide(far_high)
    ctrl_own16 = own16 < mate16
    at_moment = round24 == moment24

    def swap(x):
        return pltpu.roll(x, 4, 0)

    def body(b, carry):
        lanes = pl.ds(pl.multiple_of(b * WIDE, WIDE), WIDE)
        bias1 = bs_ref[0:1, lanes]
        bias2 = bs_ref[1:2, lanes]
        total = dot(x_ref[...], wf_ref[:, lanes])
        f_ref[...] = rounded(jnp.maximum(total + bias1, 0.0)).reshape(HEIGHT, UNITS, WIDE)
        packed = f_ref[:, 0:64, :].reshape(HEIGHT * 64, WIDE).astype(BF16)
        latent = rounded(dot(packed, dn_ref[0:WIDE, :])).reshape(HEIGHT, 64, LANES)
        rows = []
        for y in range(HEIGHT):
            lat = latent[y]
            mine = [lat[8 * j : 8 * j + 8] for j in range(3)]
            mine = [jnp.where(at_moment[8 * j : 8 * j + 8], mine[j], swap(mine[j])) for j in range(3)]
            rows.append(jnp.concatenate([lat[24:48], pair(mine), lat[48:64]], axis=0))
        given = jnp.stack(rows, axis=0)
        both = jnp.concatenate(
            [jnp.where(ctrl_up, given, 0.0), jnp.where(ctrl_up, 0.0, given)], axis=2
        ).reshape(HEIGHT * 56, WIDE)
        added = dot(both.astype(BF16), un_ref[0:WIDE, :]).reshape(HEIGHT, 56, WIDE)
        half_mask = wide(low_half)
        for y in range(HEIGHT):
            here = f_ref[y]
            add = added[y]
            own = rounded(here[0:24] + jnp.where(gate24, add[0:24], 0.0))
            own = jnp.where(ok24, own, 0.0)
            m = [here[24 + 8 * j : 32 + 8 * j] for j in range(3)]
            mid = jnp.concatenate(
                [jnp.where(half_mask, m[0], m[1]), jnp.where(half_mask, m[1], m[2])], axis=0
            )
            mid = rounded(mid + add[24:40])
            far = add[40:56]
            lower = jnp.where(ok_low, rounded(here[64:80] + jnp.where(far_low, far, 0.0)), 0.0)
            upper = jnp.where(ok_high, rounded(here[80:96] + jnp.where(far_high, far, 0.0)), 0.0)
            turned = [swap(own[8 * j : 8 * j + 8]) for j in range(3)]
            center = jnp.concatenate(
                [jnp.where(half_mask, turned[0], turned[1]), jnp.where(half_mask, turned[1], turned[2])], axis=0
            )
            top = (y + 1) * 32
            s_ref[0, top : top + 32, :] = jnp.concatenate([own[0:16], lower], axis=0).astype(BF16)
            s_ref[1, top : top + 32, :] = jnp.concatenate([center, mid], axis=0).astype(BF16)
            s_ref[2, top : top + 32, :] = jnp.concatenate([own[8:24], upper], axis=0).astype(BF16)
        size = HEIGHT * 32
        acc = jnp.zeros((size, WIDE), F32)
        for tap in range(9):
            dt, dr = divmod(tap, 3)
            acc = acc + dot(
                s_ref[dt, dr * 32 : dr * 32 + size, :], w2_ref[tap * WIDE : (tap + 1) * WIDE, :]
            )
        second = jnp.maximum(acc + bias2, 0.0) + s_ref[1, 32 : 32 + size, :].astype(F32)
        second = second.reshape(HEIGHT, 32, WIDE)
        mates = second[:, 16:32, :].reshape(HEIGHT * 16, WIDE).astype(BF16)
        latent = rounded(dot(mates, dn_ref[WIDE:, :])).reshape(HEIGHT, 16, LANES)
        both = jnp.concatenate(
            [jnp.where(ctrl_own16, latent, 0.0), jnp.where(ctrl_own16, 0.0, latent)], axis=2
        ).reshape(HEIGHT * 16, WIDE)
        added = dot(both.astype(BF16), un_ref[WIDE:, :]).reshape(HEIGHT, 16, WIDE)
        two = rounded(rounded(second[:, 0:16, :]) + jnp.where(gate16, added, 0.0))
        c2_ref[b] = jnp.where(ok16, two, 0.0)
        return carry

    lax.fori_loop(0, BLOCKS, body, 0)

    lane8 = iota((8, LANES), 1)

    def placed(y, dt):
        if y < 0 or y >= HEIGHT:
            return jnp.zeros((8, BLOCKS * WIDE), F32)
        tiles = []
        for b in range(BLOCKS):
            for t in range(2):
                group = c2_ref[b, y, :, t * LANES : (t + 1) * LANES]
                if t == 0:
                    old = pltpu.roll(c2_ref[b - 1, y, :, LANES:], 64, 1) if b else jnp.zeros((16, LANES), F32)
                    group = jnp.where(iota((16, LANES), 1) < CHANS, old, group)
                else:
                    old = pltpu.roll(c2_ref[b + 1, y, :, :LANES], 64, 1) if b + 1 < BLOCKS else jnp.zeros((16, LANES), F32)
                    group = jnp.where(iota((16, LANES), 1) >= LANES - CHANS, old, group)
                if dt == 0:
                    group = group[0:8]
                elif dt == 2:
                    group = group[8:16]
                else:
                    group = jnp.where(low_half, swap(group[0:8]), swap(group[8:16]))
                tiles.append(group)
        return jnp.concatenate(tiles, axis=1)

    for dt in range(3):
        for r in range(HALF + 2):
            s3_ref[dt, r * 16 : (r + 1) * 16, :] = jnp.concatenate(
                [placed(r - 1, dt), placed(r + HALF - 1, dt)], axis=0
            ).astype(BF16)

    size = HALF * 16
    logits = jnp.zeros((size, LANES), F32)
    for b in range(BLOCKS):
        lanes = slice(b * WIDE, (b + 1) * WIDE)
        acc = jnp.zeros((size, WIDE), F32)
        for tap in range(9):
            dt, dr = divmod(tap, 3)
            acc = acc + dot(
                s3_ref[dt, dr * 16 : dr * 16 + size, lanes], w3_ref[tap * WIDE : (tap + 1) * WIDE, :]
            )
        third = jnp.maximum(acc + bs_ref[2:3, lanes], 0.0) + s3_ref[1, 16 : 16 + size, lanes].astype(F32)
        high = third.astype(BF16)
        rest = (third - high.astype(F32)).astype(BF16)
        logits = logits + dot(high, rd_ref[lanes, :]) + dot(rest, rd_ref[lanes, :])
    logits = logits.reshape(HALF, 16, LANES)
    flat = [jnp.zeros((8, LANES), F32) for _ in range(FLAT // LANES)]
    for y in range(HEIGHT):
        row = logits[y % HALF, (y // HALF) * 8 : (y // HALF) * 8 + 8]
        begin = y * WIDTH
        turned = pltpu.roll(row, begin % LANES, 1) if begin % LANES else row
        for dst in range(FLAT // LANES):
            a = max(begin, dst * LANES) - dst * LANES
            e = min(begin + WIDTH, (dst + 1) * LANES) - dst * LANES
            if a < e:
                flat[dst] = jnp.where((lane8 >= a) & (lane8 < e), turned, flat[dst])
    flat = jnp.concatenate(flat, axis=1)[:, : HEIGHT * WIDTH] + cell_ref[...]
    for j in range(DEPTH):
        for p in range(COUNT):
            out_ref[p, j : j + 1, :] = flat[4 * j + p : 4 * j + p + 1, :]


def in_hbm(x):
    return pltpu.with_memory_space_constraint(x, pltpu.HBM)


def swapped(block, axis, mask):
    count = lax.axis_size(axis)
    return lax.ppermute(block, axis, [(i, i ^ mask) for i in range(count)])


def shifted(block, axis, offset):
    count = lax.axis_size(axis)
    return lax.ppermute(block, axis, [(i, i - offset) for i in range(count) if 0 <= i - offset < count])


def shards(
    bits, partners, gate_round, first_kernel, second_kernels, conv_bias, couple_down, couple_up, head, cell_bias
):
    devices, steps = lax.axis_size("patch"), lax.axis_size("tm")
    latent = couple_down.shape[-1]
    total = BLOCKS * WIDE
    vmem = pl.BlockSpec(memory_space=pltpu.VMEM)
    hbm = pl.BlockSpec(memory_space=pltpu.HBM)
    mine = pl.pallas_call(
        pack_kernel,
        out_shape=jax.ShapeDtypeStruct((8, FLAT + LANES), BF16),
        in_specs=[hbm, hbm, pl.BlockSpec(memory_space=pltpu.SMEM)],
        out_specs=vmem,
        scratch_shapes=[
            pltpu.VMEM((COUNT, DEPTH, WIDTH, HEIGHT), jnp.int32),
            pltpu.VMEM(partners.shape, jnp.int32),
            pltpu.SemaphoreType.DMA((2,)),
        ],
        compiler_params=pltpu.CompilerParams(vmem_limit_bytes=2 << 20),
        name="pack",
    )(in_hbm(jnp.swapaxes(bits, 2, 3)), in_hbm(partners), gate_round)

    exact = steps <= 4
    if exact:
        blocks = [mine] + [
            lax.ppermute(mine, "tm", [(i, i ^ k) for i in range(steps) if abs(i - (i ^ k)) <= 2])
            for k in range(1, steps)
        ]
    else:
        blocks = [mine] + [shifted(mine, "tm", k) for k in (1, -1, 2, -2)]
    near = jnp.concatenate(blocks, axis=0)
    params = (
        first_kernel,
        second_kernels.reshape(54 * CHANS, CHANS),
        conv_bias,
        jnp.swapaxes(couple_down, 1, 2),
        couple_up,
        head.reshape(1, CHANS),
    )
    weights = pl.pallas_call(
        weights_kernel,
        out_shape=[
            jax.ShapeDtypeStruct((WIDE, total), BF16),
            jax.ShapeDtypeStruct((9 * WIDE, WIDE), BF16),
            jax.ShapeDtypeStruct((9 * WIDE, WIDE), BF16),
            jax.ShapeDtypeStruct((2 * WIDE, SLOTS * latent), BF16),
            jax.ShapeDtypeStruct((4 * SLOTS * latent, WIDE), BF16),
            jax.ShapeDtypeStruct((total, LANES), BF16),
            jax.ShapeDtypeStruct((8, total), F32),
        ],
        in_specs=[hbm] * 6,
        out_specs=[vmem] * 7,
        scratch_shapes=[pltpu.VMEM((WIDE, total), F32)]
        + [pltpu.VMEM(x.shape, x.dtype) for x in params]
        + [pltpu.SemaphoreType.DMA((6,))],
        cost_estimate=pl.CostEstimate(flops=10**9, bytes_accessed=10**7, transcendentals=0),
        compiler_params=pltpu.CompilerParams(vmem_limit_bytes=12 << 20),
        name="weights",
    )(*map(in_hbm, params))

    near, weights = lax.optimization_barrier((near, weights))
    every = near[:, :FLAT]
    parts = [every] + [swapped(every, "patch", 2 * m) for m in range(1, devices // 2)]
    every = jnp.concatenate(parts, axis=0)
    others = swapped(every, "patch", 1)

    return pl.pallas_call(
        functools.partial(main_kernel, (devices, steps, exact)),
        out_shape=jax.ShapeDtypeStruct((COUNT, DEPTH, HEIGHT * WIDTH), F32),
        in_specs=[vmem] * 11,
        out_specs=vmem,
        scratch_shapes=[
            pltpu.VMEM((HEIGHT * UNITS, WIDE), BF16),
            pltpu.VMEM((HEIGHT, UNITS, WIDE), F32),
            pltpu.VMEM((3, 28 * 32, WIDE), BF16),
            pltpu.VMEM((BLOCKS, HEIGHT, 16, WIDE), F32),
            pltpu.VMEM((3, (HALF + 2) * 16, total), BF16),
        ],
        compiler_params=pltpu.CompilerParams(vmem_limit_bytes=40 << 20),
        name="decode",
    )(every, others, near, *weights, cell_bias.reshape(1, HEIGHT * WIDTH))


def solution(mesh):
    in_specs = (
        P("patch", "tm", None, None),
        P("tm", None),
        P("tm"),
        P(),
        P(),
        P(),
        P(),
        P(),
        P(),
        P(),
    )
    out_specs = P("patch", "tm", None)
    return jax.shard_map(shards, mesh=mesh, in_specs=in_specs, out_specs=out_specs, check_vma=False)
```

```python
import functools

import jax
import jax.numpy as jnp
from jax import lax
from jax.experimental import pallas as pl
from jax.experimental.pallas import tpu as pltpu
from jax.sharding import PartitionSpec as P

F32 = jnp.float32
BF16 = jnp.bfloat16
LANES = 128
COUNT = 4
DEPTH = 2
HEIGHT = 26
WIDTH = 24
CHANS = 32
WINDOW = 6
SLOTS = 8
BLOCKS = WIDTH // WINDOW
WIDE = SLOTS * CHANS
FLAT = 640
OWN, MATE, UNITS = 24, 16, 96
HALF = HEIGHT // 2


def iota(shape, dim):
    return lax.broadcasted_iota(jnp.int32, shape, dim)


def rounded(x):
    return x.astype(BF16).astype(F32)


def dot(a, b):
    return jnp.dot(a, b, preferred_element_type=F32)


def fetch(pairs, sems):
    copies = [pltpu.make_async_copy(src, dst, sems.at[i]) for i, (src, dst) in enumerate(pairs)]
    for copy in copies:
        copy.start()
    for copy in copies:
        copy.wait()


def pack_kernel(bits_hbm, partners_hbm, gate_ref, out_ref, bits_ref, partners_ref, sems):
    fetch(((bits_hbm, bits_ref), (partners_hbm, partners_ref)), sems)
    units = COUNT * DEPTH
    bits = bits_ref[...].reshape(units, WIDTH, HEIGHT).astype(F32)
    bits = jnp.swapaxes(bits, 1, 2)
    rows = [bits[:, y, :] for y in range(HEIGHT)]
    flat = jnp.concatenate(rows + [jnp.zeros((units, FLAT - HEIGHT * WIDTH), F32)], axis=1)
    out_ref[:, :FLAT] = flat.astype(BF16)
    patches = partners_ref.shape[1]
    names = partners_ref[...].astype(F32)
    if patches < LANES:
        names = jnp.concatenate([names, jnp.full((1, LANES - patches), -1.0, F32)], axis=1)
    moment = jnp.full((1, LANES), gate_ref[0], jnp.int32).astype(F32)
    sub = iota((units, LANES), 0)
    out_ref[:, FLAT:] = jnp.where(sub == 0, names, jnp.where(sub == 1, moment, 0.0)).astype(BF16)


def weights_kernel(
    first_hbm, second_hbm, bias_hbm, down_hbm, up_hbm, head_hbm,
    wf_ref, w2_ref, w3_ref, dn_ref, un_ref, rd_ref, bs_ref,
    scr_ref, first_ref, second_ref, bias_ref, down_ref, up_ref, head_ref, sems,
):
    sources = (first_hbm, second_hbm, bias_hbm, down_hbm, up_hbm, head_hbm)
    fetch(zip(sources, (first_ref, second_ref, bias_ref, down_ref, up_ref, head_ref)), sems)
    total = BLOCKS * WIDE
    spread = (iota((CHANS, WIDE), 1) % CHANS == iota((CHANS, WIDE), 0)).astype(BF16)
    slot = iota((CHANS, WIDE), 1) // CHANS
    inner = (slot >= 1) & (slot <= WINDOW)
    for layer, w_ref in enumerate((w2_ref, w3_ref)):
        for tap in range(9):
            base = (layer * 27 + tap * 3) * CHANS
            tiled = dot(second_ref[base : base + 3 * CHANS, :], spread)
            for kc in range(SLOTS):
                block = jnp.zeros((CHANS, WIDE), F32)
                for dc in range(3):
                    block = jnp.where(
                        inner & (slot == kc - dc + 1), tiled[dc * CHANS : (dc + 1) * CHANS], block
                    )
                w_ref[tap * WIDE + kc * CHANS : tap * WIDE + (kc + 1) * CHANS, :] = block.astype(BF16)
    across = (iota((CHANS, total), 1) % CHANS == iota((CHANS, total), 0)).astype(BF16)
    for pair in range(9):
        scr_ref[8 * pair : 8 * pair + 3, :CHANS] = first_ref[pair // 3, pair % 3].astype(F32)
    taps = dot(scr_ref[0:72, :CHANS].astype(BF16), across)
    lane = iota((WIDTH, total), 1)
    column = (lane // WIDE) * WINDOW - 1 + (lane % WIDE) // CHANS
    real = (column >= 0) & (column < WIDTH)
    offset = iota((WIDTH, total), 0) - column + 1
    for pair in range(9):
        block = jnp.zeros((WIDTH, total), F32)
        for dc in range(3):
            block = jnp.where(real & (offset == dc), taps[pair * 8 + dc : pair * 8 + dc + 1, :], block)
        scr_ref[pair * WIDTH : (pair + 1) * WIDTH, :] = block
    scr_ref[9 * WIDTH :, :] = jnp.zeros((WIDE - 9 * WIDTH, total), F32)
    wf_ref[...] = scr_ref[...].astype(BF16)
    latent = down_ref.shape[1]
    low = SLOTS * latent
    thin = (iota((latent, low), 1) % latent == iota((latent, low), 0)).astype(BF16)
    for layer in range(2):
        tiled = lax.dot_general(
            down_ref[layer], thin, (((0,), (0,)), ((), ())), preferred_element_type=F32
        )
        for kc in range(SLOTS):
            keep = iota((CHANS, low), 1) // latent == kc
            dn_ref[layer * WIDE + kc * CHANS : layer * WIDE + (kc + 1) * CHANS, :] = jnp.where(
                keep, tiled, 0.0
            ).astype(BF16)
        for role in range(2):
            tiled = dot(up_ref[layer, role], spread)
            for kc in range(SLOTS):
                keep = iota((latent, WIDE), 1) // CHANS == kc
                top = (layer * 2 + role) * low + kc * latent
                un_ref[top : top + latent, :] = jnp.where(keep, tiled, 0.0).astype(BF16)
    row = iota((total, CHANS), 0)
    chosen = jnp.where(row % CHANS == iota((total, CHANS), 1), head_ref[...].astype(F32), 0.0)
    values = dot(chosen.astype(BF16), jnp.ones((CHANS, LANES), BF16))
    row = iota((total, LANES), 0)
    place = (row % WIDE) // CHANS
    target = (row // WIDE) * WINDOW - 1 + place
    keep = (place >= 1) & (place <= WINDOW) & (target == iota((total, LANES), 1))
    rd_ref[...] = jnp.where(keep, values, 0.0).astype(BF16)
    scr_ref[0:8, :CHANS] = jnp.zeros((8, CHANS), F32)
    scr_ref[0:3, :CHANS] = bias_ref[...]
    biases = jnp.dot(
        scr_ref[0:8, :CHANS], across.astype(F32), preferred_element_type=F32, precision=lax.Precision.HIGHEST
    )
    lane = iota((8, total), 1)
    place = (lane % WIDE) // CHANS
    column = (lane // WIDE) * WINDOW - 1 + place
    real = (column >= 0) & (column < WIDTH)
    inside = (place >= 1) & (place <= WINDOW)
    top = iota((8, total), 0) == 0
    keep = (top & real) | (~top & inside)
    bs_ref[...] = jnp.where(keep, biases, 0.0)


def window_rows(gathered, y, lane):
    start = WIDTH * (y - 1)
    length = 3 * WIDTH
    tiles = [None, None]
    for dt in range(3):
        begin = length * dt
        shift = begin - start
        for src in range(FLAT // LANES):
            lo = max(start, 0, src * LANES)
            hi = min(start + length, FLAT, (src + 1) * LANES)
            if lo >= hi:
                continue
            source = gathered[dt][:, src * LANES : (src + 1) * LANES]
            turned = pltpu.roll(source, shift % LANES, 1) if shift % LANES else source
            for dst in range(2):
                a = max(lo + shift, dst * LANES) - dst * LANES
                b = min(hi + shift, (dst + 1) * LANES) - dst * LANES
                if a >= b:
                    continue
                old = jnp.zeros_like(turned) if tiles[dst] is None else tiles[dst]
                tiles[dst] = jnp.where((lane >= a) & (lane < b), turned, old)
    return tiles


def main_kernel(
    sizes, here_ref, there_ref, meta_ref, wf_ref, w2_ref, w3_ref, dn_ref, un_ref, rd_ref, bs_ref, cell_ref,
    out_ref, x_ref, f_ref, s_ref, c2_ref, s3_ref,
):
    devices, steps, exact = sizes
    near = meta_ref.shape[0] // 8
    me = lax.axis_index("patch")
    now = lax.axis_index("tm")
    sub = iota((8, LANES), 0)
    low_half = sub < 4

    names, moments = gate_layers(meta_ref, now, steps, exact)
    first_round = 2 * now - 2
    own_patch = COUNT * me + sub % COUNT

    def pair(parts):
        return jnp.concatenate(
            [jnp.where(low_half, parts[0], parts[1]), jnp.where(low_half, parts[1], parts[2])], axis=0
        )

    hot = [(jnp.broadcast_to(names[j], (8, LANES)) == own_patch).astype(F32) for j in range(3)]
    hot24 = jnp.concatenate(hot, axis=0).astype(BF16)
    hot16f = pair(hot)
    hot16 = hot16f.astype(BF16)
    square = iota((LANES, LANES), 0)
    even = moments[1] == 2 * now
    other = jnp.where(even[0:1, :], names[0], names[2])
    perm_one = (square == names[1]).astype(BF16)
    perm_other = (square == other).astype(BF16)
    middle = (iota((16, LANES), 0) >= 4) & (iota((16, LANES), 0) < 12)
    hot_far = jnp.where(middle, dot(hot16, perm_other), dot(hot16, perm_one))
    hots = jnp.concatenate([hot24, hot_far.astype(BF16), hot16], axis=0)
    index = dot(hots, square.astype(F32).astype(BF16)).astype(jnp.int32)
    mate24, far16, mate16 = index[0:24], index[24:40], index[40:56]
    own24 = jnp.concatenate([own_patch] * 3, axis=0)
    own16 = jnp.concatenate([own_patch] * 2, axis=0)

    moment24 = jnp.concatenate(moments, axis=0)
    moment16 = pair(moments)
    round24 = first_round + iota((24, LANES), 0) // 4
    round16 = first_round + 1 + iota((16, LANES), 0) // 4
    last = DEPTH * steps - 1
    step_far = pair([jnp.full((8, LANES), 1, jnp.int32), jnp.where(even, -1, 1), jnp.full((8, LANES), -1, jnp.int32)])
    moment_far = pair([moments[1], jnp.where(even, moments[0], moments[2]), moments[1]])
    touches = moment_far == moment16 + step_far
    far_low = touches & (step_far < 0)
    far_high = touches & (step_far > 0)

    columns = 2 * here_ref.shape[0]
    events = jnp.concatenate([here_ref[...], there_ref[...]], axis=0)
    col = iota((1, columns), 1)
    block = col // (8 * near)
    half = devices // 2
    source = me ^ (2 * (block % half) + block // half) if devices > 1 else me + 0 * block
    patch_of = COUNT * source + (col % 8) // DEPTH
    step = (col // 8) % near
    if exact:
        time_of = now ^ step
    else:
        time_of = now + jnp.where(step == 1, 1, jnp.where(step == 2, -1, jnp.where(step == 3, 2, jnp.where(step == 4, -2, 0))))
    round_of = DEPTH * time_of + col % DEPTH
    expand = (iota((LANES, columns), 0) == patch_of).astype(BF16)
    spread = dot(hots, expand)

    def lanes_of(x):
        return jnp.broadcast_to(x[:, :1], (x.shape[0], columns))

    is_own = (patch_of == lanes_of(own24)).astype(F32)
    patch_sel = jnp.concatenate(
        [is_own, spread[0:24], spread[24:40], spread[40:56], spread[40:56]], axis=0
    )
    want = jnp.concatenate(
        [
            lanes_of(round24),
            lanes_of(moment24),
            lanes_of(moment16 + step_far),
            lanes_of(moment16 - 1),
            lanes_of(moment16 + 1),
        ],
        axis=0,
    )
    gathered = []
    for dt in range(3):
        choose = jnp.where(round_of == want + (dt - 1), patch_sel, 0.0).astype(BF16)
        gathered.append(dot(choose, events))
    lane = iota((UNITS, LANES), 1)
    for y in range(HEIGHT):
        tiles = window_rows(gathered, y, lane)
        x_ref[y * UNITS : (y + 1) * UNITS, :] = jnp.concatenate(tiles, axis=1).astype(BF16)

    s_ref[:, 0:32, :] = jnp.zeros((3, 32, WIDE), BF16)
    s_ref[:, 27 * 32 :, :] = jnp.zeros((3, 32, WIDE), BF16)

    def wide(mask):
        return jnp.concatenate([mask.astype(jnp.int32)] * 2, axis=1) != 0

    ctrl_up = jnp.concatenate([mate24 - own24, own16 - mate16, far16 - mate16], axis=0) > 0
    gate24 = wide(round24 == moment24)
    gate16 = wide(round16 == moment16)
    ok24 = wide((round24 >= 0) & (round24 <= last))
    ok16 = wide((round16 >= 0) & (round16 <= last))
    ok_low = wide((moment16 - 1 >= 0) & (moment16 - 1 <= last))
    ok_high = wide((moment16 + 1 >= 0) & (moment16 + 1 <= last))
    far_low, far_high = wide(far_low), wide(far_high)
    ctrl_own16 = own16 < mate16
    at_moment = round24 == moment24

    def swap(x):
        return pltpu.roll(x, 4, 0)

    def body(b, carry):
        lanes = pl.ds(pl.multiple_of(b * WIDE, WIDE), WIDE)
        bias1 = bs_ref[0:1, lanes]
        bias2 = bs_ref[1:2, lanes]
        total = dot(x_ref[...], wf_ref[:, lanes])
        f_ref[...] = rounded(jnp.maximum(total + bias1, 0.0)).reshape(HEIGHT, UNITS, WIDE)
        packed = f_ref[:, 0:64, :].reshape(HEIGHT * 64, WIDE).astype(BF16)
        latent = rounded(dot(packed, dn_ref[0:WIDE, :])).reshape(HEIGHT, 64, LANES)
        rows = []
        for y in range(HEIGHT):
            lat = latent[y]
            mine = [lat[8 * j : 8 * j + 8] for j in range(3)]
            mine = [jnp.where(at_moment[8 * j : 8 * j + 8], mine[j], swap(mine[j])) for j in range(3)]
            rows.append(jnp.concatenate([lat[24:48], pair(mine), lat[48:64]], axis=0))
        given = jnp.stack(rows, axis=0)
        both = jnp.concatenate(
            [jnp.where(ctrl_up, given, 0.0), jnp.where(ctrl_up, 0.0, given)], axis=2
        ).reshape(HEIGHT * 56, WIDE)
        added = dot(both.astype(BF16), un_ref[0:WIDE, :]).reshape(HEIGHT, 56, WIDE)
        half_mask = wide(low_half)
        for y in range(HEIGHT):
            here = f_ref[y]
            add = added[y]
            own = rounded(here[0:24] + jnp.where(gate24, add[0:24], 0.0))
            own = jnp.where(ok24, own, 0.0)
            m = [here[24 + 8 * j : 32 + 8 * j] for j in range(3)]
            mid = jnp.concatenate(
                [jnp.where(half_mask, m[0], m[1]), jnp.where(half_mask, m[1], m[2])], axis=0
            )
            mid = rounded(mid + add[24:40])
            far = add[40:56]
            lower = jnp.where(ok_low, rounded(here[64:80] + jnp.where(far_low, far, 0.0)), 0.0)
            upper = jnp.where(ok_high, rounded(here[80:96] + jnp.where(far_high, far, 0.0)), 0.0)
            turned = [swap(own[8 * j : 8 * j + 8]) for j in range(3)]
            center = jnp.concatenate(
                [jnp.where(half_mask, turned[0], turned[1]), jnp.where(half_mask, turned[1], turned[2])], axis=0
            )
            top = (y + 1) * 32
            s_ref[0, top : top + 32, :] = jnp.concatenate([own[0:16], lower], axis=0).astype(BF16)
            s_ref[1, top : top + 32, :] = jnp.concatenate([center, mid], axis=0).astype(BF16)
            s_ref[2, top : top + 32, :] = jnp.concatenate([own[8:24], upper], axis=0).astype(BF16)
        size = HEIGHT * 32
        acc = jnp.zeros((size, WIDE), F32)
        for tap in range(9):
            dt, dr = divmod(tap, 3)
            acc = acc + dot(
                s_ref[dt, dr * 32 : dr * 32 + size, :], w2_ref[tap * WIDE : (tap + 1) * WIDE, :]
            )
        second = jnp.maximum(acc + bias2, 0.0) + s_ref[1, 32 : 32 + size, :].astype(F32)
        second = second.reshape(HEIGHT, 32, WIDE)
        mates = second[:, 16:32, :].reshape(HEIGHT * 16, WIDE).astype(BF16)
        latent = rounded(dot(mates, dn_ref[WIDE:, :])).reshape(HEIGHT, 16, LANES)
        both = jnp.concatenate(
            [jnp.where(ctrl_own16, latent, 0.0), jnp.where(ctrl_own16, 0.0, latent)], axis=2
        ).reshape(HEIGHT * 16, WIDE)
        added = dot(both.astype(BF16), un_ref[WIDE:, :]).reshape(HEIGHT, 16, WIDE)
        two = rounded(rounded(second[:, 0:16, :]) + jnp.where(gate16, added, 0.0))
        c2_ref[b] = jnp.where(ok16, two, 0.0)
        return carry

    lax.fori_loop(0, BLOCKS, body, 0)


    def placed(y, dt):
        if y < 0 or y >= HEIGHT:
            return jnp.zeros((8, BLOCKS * WIDE), F32)
        tiles = []
        for b in range(BLOCKS):
            for t in range(2):
                group = c2_ref[b, y, :, t * LANES : (t + 1) * LANES]
                if t == 0:
                    old = pltpu.roll(c2_ref[b - 1, y, :, LANES:], 64, 1) if b else jnp.zeros((16, LANES), F32)
                    group = jnp.where(iota((16, LANES), 1) < CHANS, old, group)
                else:
                    old = pltpu.roll(c2_ref[b + 1, y, :, :LANES], 64, 1) if b + 1 < BLOCKS else jnp.zeros((16, LANES), F32)
                    group = jnp.where(iota((16, LANES), 1) >= LANES - CHANS, old, group)
                if dt == 0:
                    group = group[0:8]
                elif dt == 2:
                    group = group[8:16]
                else:
                    group = jnp.where(low_half, swap(group[0:8]), swap(group[8:16]))
                tiles.append(group)
        return jnp.concatenate(tiles, axis=1)

    for dt in range(3):
        for r in range(HALF + 2):
            s3_ref[dt, r * 16 : (r + 1) * 16, :] = jnp.concatenate(
                [placed(r - 1, dt), placed(r + HALF - 1, dt)], axis=0
            ).astype(BF16)

    size = HALF * 16
    logits = jnp.zeros((size, LANES), F32)
    for b in range(BLOCKS):
        lanes = slice(b * WIDE, (b + 1) * WIDE)
        acc = jnp.zeros((size, WIDE), F32)
        for tap in range(9):
            dt, dr = divmod(tap, 3)
            acc = acc + dot(
                s3_ref[dt, dr * 16 : dr * 16 + size, lanes], w3_ref[tap * WIDE : (tap + 1) * WIDE, :]
            )
        third = jnp.maximum(acc + bs_ref[2:3, lanes], 0.0) + s3_ref[1, 16 : 16 + size, lanes].astype(F32)
        high = third.astype(BF16)
        rest = (third - high.astype(F32)).astype(BF16)
        logits = logits + dot(high, rd_ref[lanes, :]) + dot(rest, rd_ref[lanes, :])
    finish(logits.reshape(HALF, 16, LANES), cell_ref, out_ref)


def gate_layers(near_ref, now, steps, exact):
    names, moments = [], []
    for j in range(3):
        there = now - 1 + j
        valid = (there >= 0) & (there < steps)
        safe = jnp.clip(there, 0, steps - 1)
        block = (safe ^ now) if exact else (2, 0, 1)[j]
        tile = near_ref[pl.ds(pl.multiple_of(block * 8, 8), 8), FLAT:].astype(F32).astype(jnp.int32)
        names.append(jnp.where(valid, tile[0:1, :], -1))
        moments.append(jnp.broadcast_to(jnp.where(valid, tile[1:2, :], -1000), (8, LANES)))
    return names, moments


def event_rows(gathered, x_ref, units):
    lane = iota((units, LANES), 1)
    for y in range(HEIGHT):
        tiles = window_rows(gathered, y, lane)
        x_ref[y * units : (y + 1) * units, :] = jnp.concatenate(tiles, axis=1).astype(BF16)


MASKS = (("up", 40), ("gate24", 24), ("ok24", 24), ("low", 8), ("high", 8), ("far_low", 8), ("far_high", 8), ("own", 16), ("gate16", 16), ("ok16", 16))
MASK_AT = {}
MASK_ROWS = 0
for _name, _rows in MASKS:
    MASK_AT[_name] = (MASK_ROWS, _rows)
    MASK_ROWS += _rows
MATES = 48


def early_kernel(
    sizes, near_ref, wf_ref, dn_ref, bs_ref, own_ref, pick_ref, choose_ref, mask_ref, x_ref, f_ref
):
    devices, steps = sizes
    near = steps
    me = lax.axis_index("patch")
    now = lax.axis_index("tm")
    sub = iota((8, LANES), 0)
    low_half = sub < 4
    names, moments = gate_layers(near_ref, now, steps, True)
    late = now < steps // 2
    first_round = 2 * now - 2
    last = DEPTH * steps - 1
    own8 = COUNT * me + sub % COUNT
    name_x = jnp.where(late, names[2], names[0])
    moment_x = jnp.where(late, moments[2], moments[0])

    def half(a, b):
        return jnp.where(low_half, a, b)

    def hot(name):
        return (jnp.broadcast_to(name, (8, LANES)) == own8).astype(F32)

    hots = [hot(name) for name in names]
    hot8 = half(hots[1], hot(name_x))
    moment8 = half(moments[1], moment_x)
    even = moments[1] == 2 * now
    other = jnp.where(even[0:1, :], names[0], names[2])
    square = iota((LANES, LANES), 0)
    wide_hot = jnp.concatenate([hot8, hot8], axis=0).astype(BF16)
    to_own = dot(wide_hot, (square == names[1]).astype(BF16))[0:8]
    to_other = dot(wide_hot, (square == other).astype(BF16))[0:8]
    hot_far = half(to_other, to_own)
    every = jnp.concatenate(hots + [hot_far, hot8, jnp.zeros((8, LANES), F32)], axis=0).astype(BF16)
    index = dot(every, square.astype(F32).astype(BF16)).astype(jnp.int32)
    mate24, far8, mate8 = index[0:24], index[24:32], index[32:40]
    own24 = jnp.concatenate([own8] * 3, axis=0)
    moment24 = jnp.concatenate(moments, axis=0)
    round24 = first_round + iota((24, LANES), 0) // 4
    round16 = first_round + 1 + iota((16, LANES), 0) // 4
    moment16 = jnp.concatenate([half(moments[0], moments[1]), half(moments[1], moments[2])], axis=0)
    step_far = half(jnp.where(even, -1, 1), jnp.where(late, -1, 1))
    moment_far = half(jnp.where(even, moments[0], moments[2]), moments[1])
    touches = (moment_far == moment8 + step_far).astype(F32)
    values = dict(
        up=jnp.concatenate([(own24 < mate24).astype(F32), (mate8 < own8).astype(F32), (mate8 < far8).astype(F32)], axis=0),
        gate24=(round24 == moment24).astype(F32),
        ok24=((round24 >= 0) & (round24 <= last)).astype(F32),
        low=((moment8 - 1 >= 0) & (moment8 - 1 <= last)).astype(F32),
        high=((moment8 + 1 >= 0) & (moment8 + 1 <= last)).astype(F32),
        far_low=jnp.where(step_far < 0, touches, 0.0),
        far_high=jnp.where(step_far > 0, touches, 0.0),
        own=jnp.concatenate([(own8 < mate8).astype(F32)] * 2, axis=0),
        gate16=(round16 == moment16).astype(F32),
        ok16=((round16 >= 0) & (round16 <= last)).astype(F32),
    )
    for name, (at, rows) in MASK_AT.items():
        mask_ref[at : at + rows, :] = values[name]

    columns = choose_ref.shape[1]
    col = iota((1, columns), 1)
    block = col // (8 * near)
    some = devices // 2
    source = me ^ (2 * (block % some) + block // some)
    patch_of = COUNT * source + (col % 8) // DEPTH
    round_of = DEPTH * (now ^ ((col // 8) % near)) + col % DEPTH
    spread = dot(every, (iota((LANES, columns), 0) == patch_of).astype(BF16))
    patch_sel = jnp.concatenate([spread[0:24], spread[24:32], spread[32:40], spread[32:40]], axis=0)

    def lanes_of(x):
        return jnp.broadcast_to(x[:, :1], (x.shape[0], columns))

    want = jnp.concatenate(
        [lanes_of(moment24), lanes_of(moment8 + step_far), lanes_of(moment8 - 1), lanes_of(moment8 + 1)], axis=0
    )
    for dt in range(3):
        choose = jnp.where(round_of == want + (dt - 1), patch_sel, 0.0)
        choose_ref[dt * MATES : (dt + 1) * MATES, :] = choose.astype(BF16)

    rows = near_ref.shape[0]
    col = iota((1, rows), 1)
    patch_of = (col % 8) // DEPTH
    round_of = DEPTH * (now ^ (col // 8)) + col % DEPTH
    unit = iota((24, rows), 0)
    gathered = []
    for dt in range(3):
        choose = (patch_of == unit % COUNT) & (round_of == first_round + unit // 4 + (dt - 1))
        gathered.append(dot(choose.astype(F32).astype(BF16), near_ref[:, :FLAT]))
    event_rows(gathered, x_ref, OWN)
    ahead = [moments[j] == round24[8 * j : 8 * j + 8] for j in range(3)]
    for b in range(BLOCKS):
        lanes = slice(b * WIDE, (b + 1) * WIDE)
        total = dot(x_ref[...], wf_ref[:, lanes])
        own = rounded(jnp.maximum(total + bs_ref[0:1, lanes], 0.0))
        own_ref[:, :, lanes] = own.reshape(HEIGHT, OWN, WIDE)
        latent = rounded(dot(own.astype(BF16), dn_ref[0:WIDE, :])).reshape(HEIGHT, OWN, LANES)
        for y in range(HEIGHT):
            mine = [latent[y, 8 * j : 8 * j + 8] for j in range(3)]
            mine = [jnp.where(ahead[j], mine[j], pltpu.roll(mine[j], 4, 0)) for j in range(3)]
            pick_ref[b, y] = half(mine[1], jnp.where(late, mine[2], mine[0]))


def late_kernel(
    here_ref, there_ref, own_ref, pick_ref, choose_ref, mask_ref, wf_ref, w2_ref, w3_ref, dn_ref, un_ref, rd_ref, bs_ref,
    cell_ref, out_ref, x_ref, f_ref, s_ref, t_ref, c2_ref, s3_ref,
):
    now = lax.axis_index("tm")
    steps = lax.axis_size("tm")
    late = now < steps // 2
    low_half = iota((8, LANES), 0) < 4

    def mask(name, wide=True):
        at, rows = MASK_AT[name]
        value = mask_ref[at : at + rows, :]
        return (jnp.concatenate([value] * 2, axis=1) if wide else value) > 0.5

    def swap(x):
        return pltpu.roll(x, 4, 0)

    events = jnp.concatenate([here_ref[...], there_ref[...]], axis=0)
    picked = dot(choose_ref[...], events)
    event_rows([picked[dt * MATES : (dt + 1) * MATES] for dt in range(3)], x_ref, MATES)

    half_mask = jnp.concatenate([low_half.astype(F32)] * 2, axis=1) > 0.5

    def half(a, b):
        return jnp.where(half_mask, a, b)

    up_mask = mask("up", False)
    gate24, ok24 = mask("gate24"), mask("ok24")
    ok_low, ok_high, far_low, far_high = mask("low"), mask("high"), mask("far_low"), mask("far_high")
    own_mask = mask("own", False)
    gate16, ok16 = mask("gate16"), mask("ok16")
    size = HEIGHT * 16
    part = HALF * 16
    zero = jnp.zeros((8, WIDE), F32)
    s_ref[:, :, 0:16, :] = jnp.zeros((2, 3, 16, WIDE), BF16)
    s_ref[:, :, 27 * 16 :, :] = jnp.zeros((2, 3, 16, WIDE), BF16)

    for b in range(BLOCKS):
        lanes = slice(b * WIDE, (b + 1) * WIDE)
        turn = b % 2
        bias1 = bs_ref[0:1, lanes]
        bias2 = bs_ref[1:2, lanes]
        total = dot(x_ref[...], wf_ref[:, lanes])
        f_ref[turn] = rounded(jnp.maximum(total + bias1, 0.0)).reshape(HEIGHT, MATES, WIDE)
        packed = f_ref[turn, :, 0:32, :].reshape(HEIGHT * 32, WIDE).astype(BF16)
        latent = rounded(dot(packed, dn_ref[0:WIDE, :])).reshape(HEIGHT, 32, LANES)
        given = jnp.concatenate([latent[:, 0:24], pick_ref[b], latent[:, 24:32]], axis=1)
        both = jnp.concatenate([jnp.where(up_mask, given, 0.0), jnp.where(up_mask, 0.0, given)], axis=2)
        added = dot(both.reshape(HEIGHT * 40, WIDE).astype(BF16), un_ref[0:WIDE, :]).reshape(HEIGHT, 40, WIDE)

        def mate(y):
            here = f_ref[turn, y]
            add = added[y]
            own = rounded(own_ref[y, :, lanes] + jnp.where(gate24, add[0:24], 0.0))
            own = jnp.where(ok24, own, 0.0)
            turned = [swap(own[8 * j : 8 * j + 8]) for j in range(3)]
            center = jnp.concatenate([half(turned[0], turned[1]), half(turned[1], turned[2])], axis=0)
            top = (y + 1) * 16
            s_ref[turn, 0, top : top + 16, :] = own[0:16].astype(BF16)
            s_ref[turn, 1, top : top + 16, :] = center.astype(BF16)
            s_ref[turn, 2, top : top + 16, :] = own[8:24].astype(BF16)
            middle = half(here[8:16], jnp.where(late, here[16:24], here[0:8]))
            middle = rounded(middle + add[24:32])
            far = add[32:40]
            lower = jnp.where(ok_low, rounded(here[32:40] + jnp.where(far_low, far, 0.0)), 0.0)
            upper = jnp.where(ok_high, rounded(here[40:48] + jnp.where(far_high, far, 0.0)), 0.0)
            return lower, middle, upper

        def put(r, top, bottom):
            for dt in range(3):
                t_ref[turn, dt, r * 16 : (r + 1) * 16, :] = jnp.concatenate([top[dt], bottom[dt]], axis=0).astype(BF16)

        nothing = (zero, zero, zero)
        for y in range(HALF):
            top, bottom = mate(y), mate(y + HALF)
            put(y + 1, top, bottom)
            if y == 0:
                put(HALF + 1, bottom, nothing)
            if y == HALF - 1:
                put(0, nothing, top)

        acc = jnp.zeros((size + part, WIDE), F32)
        for tap in range(9):
            dt, dr = divmod(tap, 3)
            lhs = jnp.concatenate(
                [s_ref[turn, dt, dr * 16 : dr * 16 + size, :], t_ref[turn, dt, dr * 16 : dr * 16 + part, :]], axis=0
            )
            acc = acc + dot(lhs, w2_ref[tap * WIDE : (tap + 1) * WIDE, :])
        acc = jnp.maximum(acc + bias2, 0.0)
        mates = acc[size:] + t_ref[turn, 1, 16 : 16 + part, :].astype(F32)
        latent = rounded(dot(mates.astype(BF16), dn_ref[WIDE:, :])).reshape(HALF, 16, LANES)
        both = jnp.concatenate([jnp.where(own_mask, latent, 0.0), jnp.where(own_mask, 0.0, latent)], axis=2)
        added = dot(both.reshape(part, WIDE).astype(BF16), un_ref[WIDE:, :]).reshape(HALF, 16, WIDE)
        second = rounded(acc[:size] + s_ref[turn, 1, 16 : 16 + size, :].astype(F32)).reshape(HEIGHT, 16, WIDE)
        for y in range(HEIGHT):
            at = (y // HALF) * 8
            add = added[y % HALF, at : at + 8]
            add = jnp.concatenate([swap(add), add], axis=0)
            two = rounded(second[y] + jnp.where(gate16, add, 0.0))
            c2_ref[b, y] = jnp.where(ok16, two, 0.0)

    lane = iota((16, LANES), 1)
    left, right = lane < CHANS, lane >= LANES - CHANS

    def filled(y):
        tiles = []
        for b in range(BLOCKS):
            old = pltpu.roll(c2_ref[b - 1, y, :, LANES:], 64, 1) if b else jnp.zeros((16, LANES), F32)
            tiles.append(jnp.where(left, old, c2_ref[b, y, :, :LANES]))
            old = pltpu.roll(c2_ref[b + 1, y, :, :LANES], 64, 1) if b + 1 < BLOCKS else jnp.zeros((16, LANES), F32)
            tiles.append(jnp.where(right, old, c2_ref[b, y, :, LANES:]))
        whole = jnp.concatenate(tiles, axis=1)
        low, high = whole[0:8], whole[8:16]
        keep = iota((8, BLOCKS * WIDE), 0) < 4
        return low, jnp.where(keep, swap(low), swap(high)), high

    def store(r, top, bottom):
        for dt in range(3):
            s3_ref[dt, r * 16 : (r + 1) * 16, :] = jnp.concatenate([top[dt], bottom[dt]], axis=0).astype(BF16)

    nothing = (jnp.zeros((8, BLOCKS * WIDE), F32),) * 3
    for y in range(HALF):
        top, bottom = filled(y), filled(y + HALF)
        store(y + 1, top, bottom)
        if y == 0:
            store(HALF + 1, bottom, nothing)
        if y == HALF - 1:
            store(0, nothing, top)

    def windows(dt, start):
        return jnp.concatenate(
            [s3_ref[dt, start : start + part, b * WIDE : (b + 1) * WIDE] for b in range(BLOCKS)], axis=0
        )

    acc = jnp.zeros((BLOCKS * part, WIDE), F32)
    for tap in range(9):
        dt, dr = divmod(tap, 3)
        acc = acc + dot(windows(dt, dr * 16), w3_ref[tap * WIDE : (tap + 1) * WIDE, :])
    logits = jnp.zeros((part, LANES), F32)
    for b in range(BLOCKS):
        lanes = slice(b * WIDE, (b + 1) * WIDE)
        third = jnp.maximum(acc[b * part : (b + 1) * part] + bs_ref[2:3, lanes], 0.0)
        third = third + s3_ref[1, 16 : 16 + part, lanes].astype(F32)
        high = third.astype(BF16)
        rest = (third - high.astype(F32)).astype(BF16)
        sums = dot(jnp.concatenate([high, rest], axis=0), rd_ref[lanes, :])
        logits = logits + sums[:part] + sums[part:]
    finish(logits.reshape(HALF, 16, LANES), cell_ref, out_ref)


def finish(logits, cell_ref, out_ref):
    lane8 = iota((8, LANES), 1)
    flat = [jnp.zeros((8, LANES), F32) for _ in range(FLAT // LANES)]
    for y in range(HEIGHT):
        row = logits[y % HALF, (y // HALF) * 8 : (y // HALF) * 8 + 8]
        begin = y * WIDTH
        turned = pltpu.roll(row, begin % LANES, 1) if begin % LANES else row
        for dst in range(FLAT // LANES):
            a = max(begin, dst * LANES) - dst * LANES
            e = min(begin + WIDTH, (dst + 1) * LANES) - dst * LANES
            if a < e:
                flat[dst] = jnp.where((lane8 >= a) & (lane8 < e), turned, flat[dst])
    flat = jnp.concatenate(flat, axis=1)[:, : HEIGHT * WIDTH] + cell_ref[...]
    for j in range(DEPTH):
        for p in range(COUNT):
            out_ref[p, j : j + 1, :] = flat[4 * j + p : 4 * j + p + 1, :]


def in_hbm(x):
    return pltpu.with_memory_space_constraint(x, pltpu.HBM)


def swapped(block, axis, mask):
    count = lax.axis_size(axis)
    return lax.ppermute(block, axis, [(i, i ^ mask) for i in range(count)])


def shifted(block, axis, offset):
    count = lax.axis_size(axis)
    return lax.ppermute(block, axis, [(i, i - offset) for i in range(count) if 0 <= i - offset < count])


def shards(
    bits, partners, gate_round, first_kernel, second_kernels, conv_bias, couple_down, couple_up, head, cell_bias
):
    devices, steps = lax.axis_size("patch"), lax.axis_size("tm")
    latent = couple_down.shape[-1]
    total = BLOCKS * WIDE
    vmem = pl.BlockSpec(memory_space=pltpu.VMEM)
    hbm = pl.BlockSpec(memory_space=pltpu.HBM)
    mine = pl.pallas_call(
        pack_kernel,
        out_shape=jax.ShapeDtypeStruct((8, FLAT + LANES), BF16),
        in_specs=[hbm, hbm, pl.BlockSpec(memory_space=pltpu.SMEM)],
        out_specs=vmem,
        scratch_shapes=[
            pltpu.VMEM((COUNT, DEPTH, WIDTH, HEIGHT), jnp.int32),
            pltpu.VMEM(partners.shape, jnp.int32),
            pltpu.SemaphoreType.DMA((2,)),
        ],
        compiler_params=pltpu.CompilerParams(vmem_limit_bytes=2 << 20),
        name="pack",
    )(in_hbm(jnp.swapaxes(bits, 2, 3)), in_hbm(partners), gate_round)

    exact = steps == 4 and devices > 1
    if exact:
        blocks = [mine] + [
            lax.ppermute(mine, "tm", [(i, i ^ k) for i in range(steps) if abs(i - (i ^ k)) <= 2])
            for k in range(1, steps)
        ]
    else:
        blocks = [mine] + [shifted(mine, "tm", k) for k in (1, -1, 2, -2)]
    near = jnp.concatenate(blocks, axis=0)
    params = (
        first_kernel,
        second_kernels.reshape(54 * CHANS, CHANS),
        conv_bias,
        jnp.swapaxes(couple_down, 1, 2),
        couple_up,
        head.reshape(1, CHANS),
    )
    weights = pl.pallas_call(
        weights_kernel,
        out_shape=[
            jax.ShapeDtypeStruct((WIDE, total), BF16),
            jax.ShapeDtypeStruct((9 * WIDE, WIDE), BF16),
            jax.ShapeDtypeStruct((9 * WIDE, WIDE), BF16),
            jax.ShapeDtypeStruct((2 * WIDE, SLOTS * latent), BF16),
            jax.ShapeDtypeStruct((4 * SLOTS * latent, WIDE), BF16),
            jax.ShapeDtypeStruct((total, LANES), BF16),
            jax.ShapeDtypeStruct((8, total), F32),
        ],
        in_specs=[hbm] * 6,
        out_specs=[vmem] * 7,
        scratch_shapes=[pltpu.VMEM((WIDE, total), F32)]
        + [pltpu.VMEM(x.shape, x.dtype) for x in params]
        + [pltpu.SemaphoreType.DMA((6,))],
        cost_estimate=pl.CostEstimate(flops=10**9, bytes_accessed=10**7, transcendentals=0),
        compiler_params=pltpu.CompilerParams(vmem_limit_bytes=12 << 20),
        name="weights",
    )(*map(in_hbm, params))

    near, weights = lax.optimization_barrier((near, weights))
    every = near[:, :FLAT]
    parts = [every] + [swapped(every, "patch", 2 * m) for m in range(1, devices // 2)]
    every = jnp.concatenate(parts, axis=0)
    others = swapped(every, "patch", 1)

    if exact:
        wf, w2, w3, dn, un, rd, bs = weights
        early = pl.pallas_call(
            functools.partial(early_kernel, (devices, steps)),
            out_shape=[
                jax.ShapeDtypeStruct((HEIGHT, OWN, total), F32),
                jax.ShapeDtypeStruct((BLOCKS, HEIGHT, 8, LANES), F32),
                jax.ShapeDtypeStruct((3 * MATES, 8 * steps * devices), BF16),
                jax.ShapeDtypeStruct((MASK_ROWS, LANES), F32),
            ],
            in_specs=[vmem] * 4,
            out_specs=[vmem] * 4,
            scratch_shapes=[pltpu.VMEM((HEIGHT * OWN, WIDE), BF16), pltpu.VMEM((8, LANES), F32)],
            cost_estimate=pl.CostEstimate(flops=10**9, bytes_accessed=10**7, transcendentals=0),
            compiler_params=pltpu.CompilerParams(vmem_limit_bytes=14 << 20),
            name="early",
        )(near, wf, dn, bs)
        return pl.pallas_call(
            late_kernel,
            out_shape=jax.ShapeDtypeStruct((COUNT, DEPTH, HEIGHT * WIDTH), F32),
            in_specs=[vmem] * 14,
            out_specs=vmem,
            scratch_shapes=[
                pltpu.VMEM((HEIGHT * MATES, WIDE), BF16),
                pltpu.VMEM((2, HEIGHT, MATES, WIDE), F32),
                pltpu.VMEM((2, 3, 28 * 16, WIDE), BF16),
                pltpu.VMEM((2, 3, (HALF + 2) * 16, WIDE), BF16),
                pltpu.VMEM((BLOCKS, HEIGHT, 16, WIDE), F32),
                pltpu.VMEM((3, (HALF + 2) * 16, total), BF16),
            ],
            compiler_params=pltpu.CompilerParams(vmem_limit_bytes=36 << 20),
            name="late",
        )(every, others, *early, wf, w2, w3, dn, un, rd, bs, cell_bias.reshape(1, HEIGHT * WIDTH))
    return pl.pallas_call(
        functools.partial(main_kernel, (devices, steps, exact)),
        out_shape=jax.ShapeDtypeStruct((COUNT, DEPTH, HEIGHT * WIDTH), F32),
        in_specs=[vmem] * 11,
        out_specs=vmem,
        scratch_shapes=[
            pltpu.VMEM((HEIGHT * UNITS, WIDE), BF16),
            pltpu.VMEM((HEIGHT, UNITS, WIDE), F32),
            pltpu.VMEM((3, 28 * 32, WIDE), BF16),
            pltpu.VMEM((BLOCKS, HEIGHT, 16, WIDE), F32),
            pltpu.VMEM((3, (HALF + 2) * 16, total), BF16),
        ],
        compiler_params=pltpu.CompilerParams(vmem_limit_bytes=40 << 20),
        name="decode",
    )(every, others, near, *weights, cell_bias.reshape(1, HEIGHT * WIDTH))


def solution(mesh):
    in_specs = (
        P("patch", "tm", None, None),
        P("tm", None),
        P("tm"),
        P(),
        P(),
        P(),
        P(),
        P(),
        P(),
        P(),
    )
    out_specs = P("patch", "tm", None)
    return jax.shard_map(shards, mesh=mesh, in_specs=in_specs, out_specs=out_specs, check_vma=False)
```

```python
import functools

import jax
import jax.numpy as jnp
from jax import lax
from jax.experimental import pallas as pl
from jax.experimental.pallas import tpu as pltpu
from jax.sharding import PartitionSpec as P

F32 = jnp.float32
BF16 = jnp.bfloat16
LANES = 128
COUNT = 4
DEPTH = 2
HEIGHT = 26
WIDTH = 24
CHANS = 32
WINDOW = 6
SLOTS = 8
BLOCKS = WIDTH // WINDOW
WIDE = SLOTS * CHANS
FLAT = 640
OWN, MATE, UNITS = 24, 16, 96
HALF = HEIGHT // 2


def iota(shape, dim):
    return lax.broadcasted_iota(jnp.int32, shape, dim)


def rounded(x):
    return x.astype(BF16).astype(F32)


def dot(a, b):
    return jnp.dot(a, b, preferred_element_type=F32)


def fetch(pairs, sems):
    copies = [pltpu.make_async_copy(src, dst, sems.at[i]) for i, (src, dst) in enumerate(pairs)]
    for copy in copies:
        copy.start()
    for copy in copies:
        copy.wait()


def pack_kernel(bits_hbm, partners_hbm, gate_ref, out_ref, bits_ref, partners_ref, sems):
    fetch(((bits_hbm, bits_ref), (partners_hbm, partners_ref)), sems)
    units = COUNT * DEPTH
    bits = bits_ref[...].reshape(units, WIDTH, HEIGHT).astype(F32)
    bits = jnp.swapaxes(bits, 1, 2)
    rows = [bits[:, y, :] for y in range(HEIGHT)]
    flat = jnp.concatenate(rows + [jnp.zeros((units, FLAT - HEIGHT * WIDTH), F32)], axis=1)
    out_ref[:, :FLAT] = flat.astype(BF16)
    patches = partners_ref.shape[1]
    names = partners_ref[...].astype(F32)
    if patches < LANES:
        names = jnp.concatenate([names, jnp.full((1, LANES - patches), -1.0, F32)], axis=1)
    moment = jnp.full((1, LANES), gate_ref[0], jnp.int32).astype(F32)
    sub = iota((units, LANES), 0)
    out_ref[:, FLAT:] = jnp.where(sub == 0, names, jnp.where(sub == 1, moment, 0.0)).astype(BF16)


def weights_kernel(
    first_hbm, second_hbm, bias_hbm, down_hbm, up_hbm, head_hbm,
    wf_ref, w2_ref, w3_ref, dn_ref, un_ref, rd_ref, bs_ref,
    scr_ref, first_ref, second_ref, bias_ref, down_ref, up_ref, head_ref, sems,
):
    sources = (first_hbm, second_hbm, bias_hbm, down_hbm, up_hbm, head_hbm)
    fetch(zip(sources, (first_ref, second_ref, bias_ref, down_ref, up_ref, head_ref)), sems)
    total = BLOCKS * WIDE
    spread = (iota((CHANS, WIDE), 1) % CHANS == iota((CHANS, WIDE), 0)).astype(BF16)
    slot = iota((CHANS, WIDE), 1) // CHANS
    inner = (slot >= 1) & (slot <= WINDOW)
    for layer, w_ref in enumerate((w2_ref, w3_ref)):
        for tap in range(9):
            base = (layer * 27 + tap * 3) * CHANS
            tiled = dot(second_ref[base : base + 3 * CHANS, :], spread)
            for kc in range(SLOTS):
                block = jnp.zeros((CHANS, WIDE), F32)
                for dc in range(3):
                    block = jnp.where(
                        inner & (slot == kc - dc + 1), tiled[dc * CHANS : (dc + 1) * CHANS], block
                    )
                w_ref[tap * WIDE + kc * CHANS : tap * WIDE + (kc + 1) * CHANS, :] = block.astype(BF16)
    across = (iota((CHANS, total), 1) % CHANS == iota((CHANS, total), 0)).astype(BF16)
    for pair in range(9):
        scr_ref[8 * pair : 8 * pair + 3, :CHANS] = first_ref[pair // 3, pair % 3].astype(F32)
    taps = dot(scr_ref[0:72, :CHANS].astype(BF16), across)
    lane = iota((WIDTH, total), 1)
    column = (lane // WIDE) * WINDOW - 1 + (lane % WIDE) // CHANS
    real = (column >= 0) & (column < WIDTH)
    offset = iota((WIDTH, total), 0) - column + 1
    for pair in range(9):
        block = jnp.zeros((WIDTH, total), F32)
        for dc in range(3):
            block = jnp.where(real & (offset == dc), taps[pair * 8 + dc : pair * 8 + dc + 1, :], block)
        scr_ref[pair * WIDTH : (pair + 1) * WIDTH, :] = block
    scr_ref[9 * WIDTH :, :] = jnp.zeros((WIDE - 9 * WIDTH, total), F32)
    wf_ref[...] = scr_ref[...].astype(BF16)
    latent = down_ref.shape[1]
    low = SLOTS * latent
    thin = (iota((latent, low), 1) % latent == iota((latent, low), 0)).astype(BF16)
    for layer in range(2):
        tiled = lax.dot_general(
            down_ref[layer], thin, (((0,), (0,)), ((), ())), preferred_element_type=F32
        )
        for kc in range(SLOTS):
            keep = iota((CHANS, low), 1) // latent == kc
            dn_ref[layer * WIDE + kc * CHANS : layer * WIDE + (kc + 1) * CHANS, :] = jnp.where(
                keep, tiled, 0.0
            ).astype(BF16)
        for role in range(2):
            tiled = dot(up_ref[layer, role], spread)
            for kc in range(SLOTS):
                keep = iota((latent, WIDE), 1) // CHANS == kc
                top = (layer * 2 + role) * low + kc * latent
                un_ref[top : top + latent, :] = jnp.where(keep, tiled, 0.0).astype(BF16)
    row = iota((total, CHANS), 0)
    chosen = jnp.where(row % CHANS == iota((total, CHANS), 1), head_ref[...].astype(F32), 0.0)
    values = dot(chosen.astype(BF16), jnp.ones((CHANS, LANES), BF16))
    row = iota((total, LANES), 0)
    place = (row % WIDE) // CHANS
    target = (row // WIDE) * WINDOW - 1 + place
    keep = (place >= 1) & (place <= WINDOW) & (target == iota((total, LANES), 1))
    rd_ref[...] = jnp.where(keep, values, 0.0).astype(BF16)
    scr_ref[0:8, :CHANS] = jnp.zeros((8, CHANS), F32)
    scr_ref[0:3, :CHANS] = bias_ref[...]
    biases = jnp.dot(
        scr_ref[0:8, :CHANS], across.astype(F32), preferred_element_type=F32, precision=lax.Precision.HIGHEST
    )
    lane = iota((8, total), 1)
    place = (lane % WIDE) // CHANS
    column = (lane // WIDE) * WINDOW - 1 + place
    real = (column >= 0) & (column < WIDTH)
    inside = (place >= 1) & (place <= WINDOW)
    top = iota((8, total), 0) == 0
    keep = (top & real) | (~top & inside)
    bs_ref[...] = jnp.where(keep, biases, 0.0)


def window_rows(gathered, y, lane):
    start = WIDTH * (y - 1)
    length = 3 * WIDTH
    tiles = [None, None]
    for dt in range(3):
        begin = length * dt
        shift = begin - start
        for src in range(FLAT // LANES):
            lo = max(start, 0, src * LANES)
            hi = min(start + length, FLAT, (src + 1) * LANES)
            if lo >= hi:
                continue
            source = gathered[dt][:, src * LANES : (src + 1) * LANES]
            turned = pltpu.roll(source, shift % LANES, 1) if shift % LANES else source
            for dst in range(2):
                a = max(lo + shift, dst * LANES) - dst * LANES
                b = min(hi + shift, (dst + 1) * LANES) - dst * LANES
                if a >= b:
                    continue
                old = jnp.zeros_like(turned) if tiles[dst] is None else tiles[dst]
                tiles[dst] = jnp.where((lane >= a) & (lane < b), turned, old)
    return tiles


def main_kernel(
    sizes, here_ref, there_ref, meta_ref, wf_ref, w2_ref, w3_ref, dn_ref, un_ref, rd_ref, bs_ref, cell_ref,
    out_ref, x_ref, f_ref, s_ref, c2_ref, s3_ref,
):
    devices, steps, exact = sizes
    near = meta_ref.shape[0] // 8
    me = lax.axis_index("patch")
    now = lax.axis_index("tm")
    sub = iota((8, LANES), 0)
    low_half = sub < 4

    names, moments = gate_layers(meta_ref, now, steps, exact)
    first_round = 2 * now - 2
    own_patch = COUNT * me + sub % COUNT

    def pair(parts):
        return jnp.concatenate(
            [jnp.where(low_half, parts[0], parts[1]), jnp.where(low_half, parts[1], parts[2])], axis=0
        )

    hot = [(jnp.broadcast_to(names[j], (8, LANES)) == own_patch).astype(F32) for j in range(3)]
    hot24 = jnp.concatenate(hot, axis=0).astype(BF16)
    hot16f = pair(hot)
    hot16 = hot16f.astype(BF16)
    square = iota((LANES, LANES), 0)
    even = moments[1] == 2 * now
    other = jnp.where(even[0:1, :], names[0], names[2])
    perm_one = (square == names[1]).astype(BF16)
    perm_other = (square == other).astype(BF16)
    middle = (iota((16, LANES), 0) >= 4) & (iota((16, LANES), 0) < 12)
    hot_far = jnp.where(middle, dot(hot16, perm_other), dot(hot16, perm_one))
    hots = jnp.concatenate([hot24, hot_far.astype(BF16), hot16], axis=0)
    index = dot(hots, square.astype(F32).astype(BF16)).astype(jnp.int32)
    mate24, far16, mate16 = index[0:24], index[24:40], index[40:56]
    own24 = jnp.concatenate([own_patch] * 3, axis=0)
    own16 = jnp.concatenate([own_patch] * 2, axis=0)

    moment24 = jnp.concatenate(moments, axis=0)
    moment16 = pair(moments)
    round24 = first_round + iota((24, LANES), 0) // 4
    round16 = first_round + 1 + iota((16, LANES), 0) // 4
    last = DEPTH * steps - 1
    step_far = pair([jnp.full((8, LANES), 1, jnp.int32), jnp.where(even, -1, 1), jnp.full((8, LANES), -1, jnp.int32)])
    moment_far = pair([moments[1], jnp.where(even, moments[0], moments[2]), moments[1]])
    touches = moment_far == moment16 + step_far
    far_low = touches & (step_far < 0)
    far_high = touches & (step_far > 0)

    columns = 2 * here_ref.shape[0]
    events = jnp.concatenate([here_ref[...], there_ref[...]], axis=0)
    col = iota((1, columns), 1)
    block = col // (8 * near)
    half = devices // 2
    source = me ^ (2 * (block % half) + block // half) if devices > 1 else me + 0 * block
    patch_of = COUNT * source + (col % 8) // DEPTH
    step = (col // 8) % near
    if exact:
        time_of = now ^ step
    else:
        time_of = now + jnp.where(step == 1, 1, jnp.where(step == 2, -1, jnp.where(step == 3, 2, jnp.where(step == 4, -2, 0))))
    round_of = DEPTH * time_of + col % DEPTH
    expand = (iota((LANES, columns), 0) == patch_of).astype(BF16)
    spread = dot(hots, expand)

    def lanes_of(x):
        return jnp.broadcast_to(x[:, :1], (x.shape[0], columns))

    is_own = (patch_of == lanes_of(own24)).astype(F32)
    patch_sel = jnp.concatenate(
        [is_own, spread[0:24], spread[24:40], spread[40:56], spread[40:56]], axis=0
    )
    want = jnp.concatenate(
        [
            lanes_of(round24),
            lanes_of(moment24),
            lanes_of(moment16 + step_far),
            lanes_of(moment16 - 1),
            lanes_of(moment16 + 1),
        ],
        axis=0,
    )
    gathered = []
    for dt in range(3):
        choose = jnp.where(round_of == want + (dt - 1), patch_sel, 0.0).astype(BF16)
        gathered.append(dot(choose, events))
    lane = iota((UNITS, LANES), 1)
    for y in range(HEIGHT):
        tiles = window_rows(gathered, y, lane)
        x_ref[y * UNITS : (y + 1) * UNITS, :] = jnp.concatenate(tiles, axis=1).astype(BF16)

    s_ref[:, 0:32, :] = jnp.zeros((3, 32, WIDE), BF16)
    s_ref[:, 27 * 32 :, :] = jnp.zeros((3, 32, WIDE), BF16)

    def wide(mask):
        return jnp.concatenate([mask.astype(jnp.int32)] * 2, axis=1) != 0

    ctrl_up = jnp.concatenate([mate24 - own24, own16 - mate16, far16 - mate16], axis=0) > 0
    gate24 = wide(round24 == moment24)
    gate16 = wide(round16 == moment16)
    ok24 = wide((round24 >= 0) & (round24 <= last))
    ok16 = wide((round16 >= 0) & (round16 <= last))
    ok_low = wide((moment16 - 1 >= 0) & (moment16 - 1 <= last))
    ok_high = wide((moment16 + 1 >= 0) & (moment16 + 1 <= last))
    far_low, far_high = wide(far_low), wide(far_high)
    ctrl_own16 = own16 < mate16
    at_moment = round24 == moment24

    def swap(x):
        return pltpu.roll(x, 4, 0)

    def body(b, carry):
        lanes = pl.ds(pl.multiple_of(b * WIDE, WIDE), WIDE)
        bias1 = bs_ref[0:1, lanes]
        bias2 = bs_ref[1:2, lanes]
        total = dot(x_ref[...], wf_ref[:, lanes])
        f_ref[...] = rounded(jnp.maximum(total + bias1, 0.0)).reshape(HEIGHT, UNITS, WIDE)
        packed = f_ref[:, 0:64, :].reshape(HEIGHT * 64, WIDE).astype(BF16)
        latent = rounded(dot(packed, dn_ref[0:WIDE, :])).reshape(HEIGHT, 64, LANES)
        rows = []
        for y in range(HEIGHT):
            lat = latent[y]
            mine = [lat[8 * j : 8 * j + 8] for j in range(3)]
            mine = [jnp.where(at_moment[8 * j : 8 * j + 8], mine[j], swap(mine[j])) for j in range(3)]
            rows.append(jnp.concatenate([lat[24:48], pair(mine), lat[48:64]], axis=0))
        given = jnp.stack(rows, axis=0)
        both = jnp.concatenate(
            [jnp.where(ctrl_up, given, 0.0), jnp.where(ctrl_up, 0.0, given)], axis=2
        ).reshape(HEIGHT * 56, WIDE)
        added = dot(both.astype(BF16), un_ref[0:WIDE, :]).reshape(HEIGHT, 56, WIDE)
        half_mask = wide(low_half)
        for y in range(HEIGHT):
            here = f_ref[y]
            add = added[y]
            own = rounded(here[0:24] + jnp.where(gate24, add[0:24], 0.0))
            own = jnp.where(ok24, own, 0.0)
            m = [here[24 + 8 * j : 32 + 8 * j] for j in range(3)]
            mid = jnp.concatenate(
                [jnp.where(half_mask, m[0], m[1]), jnp.where(half_mask, m[1], m[2])], axis=0
            )
            mid = rounded(mid + add[24:40])
            far = add[40:56]
            lower = jnp.where(ok_low, rounded(here[64:80] + jnp.where(far_low, far, 0.0)), 0.0)
            upper = jnp.where(ok_high, rounded(here[80:96] + jnp.where(far_high, far, 0.0)), 0.0)
            turned = [swap(own[8 * j : 8 * j + 8]) for j in range(3)]
            center = jnp.concatenate(
                [jnp.where(half_mask, turned[0], turned[1]), jnp.where(half_mask, turned[1], turned[2])], axis=0
            )
            top = (y + 1) * 32
            s_ref[0, top : top + 32, :] = jnp.concatenate([own[0:16], lower], axis=0).astype(BF16)
            s_ref[1, top : top + 32, :] = jnp.concatenate([center, mid], axis=0).astype(BF16)
            s_ref[2, top : top + 32, :] = jnp.concatenate([own[8:24], upper], axis=0).astype(BF16)
        size = HEIGHT * 32
        acc = jnp.zeros((size, WIDE), F32)
        for tap in range(9):
            dt, dr = divmod(tap, 3)
            acc = acc + dot(
                s_ref[dt, dr * 32 : dr * 32 + size, :], w2_ref[tap * WIDE : (tap + 1) * WIDE, :]
            )
        second = jnp.maximum(acc + bias2, 0.0) + s_ref[1, 32 : 32 + size, :].astype(F32)
        second = second.reshape(HEIGHT, 32, WIDE)
        mates = second[:, 16:32, :].reshape(HEIGHT * 16, WIDE).astype(BF16)
        latent = rounded(dot(mates, dn_ref[WIDE:, :])).reshape(HEIGHT, 16, LANES)
        both = jnp.concatenate(
            [jnp.where(ctrl_own16, latent, 0.0), jnp.where(ctrl_own16, 0.0, latent)], axis=2
        ).reshape(HEIGHT * 16, WIDE)
        added = dot(both.astype(BF16), un_ref[WIDE:, :]).reshape(HEIGHT, 16, WIDE)
        two = rounded(rounded(second[:, 0:16, :]) + jnp.where(gate16, added, 0.0))
        c2_ref[b] = jnp.where(ok16, two, 0.0)
        return carry

    lax.fori_loop(0, BLOCKS, body, 0)


    def placed(y, dt):
        if y < 0 or y >= HEIGHT:
            return jnp.zeros((8, BLOCKS * WIDE), F32)
        tiles = []
        for b in range(BLOCKS):
            for t in range(2):
                group = c2_ref[b, y, :, t * LANES : (t + 1) * LANES]
                if t == 0:
                    old = pltpu.roll(c2_ref[b - 1, y, :, LANES:], 64, 1) if b else jnp.zeros((16, LANES), F32)
                    group = jnp.where(iota((16, LANES), 1) < CHANS, old, group)
                else:
                    old = pltpu.roll(c2_ref[b + 1, y, :, :LANES], 64, 1) if b + 1 < BLOCKS else jnp.zeros((16, LANES), F32)
                    group = jnp.where(iota((16, LANES), 1) >= LANES - CHANS, old, group)
                if dt == 0:
                    group = group[0:8]
                elif dt == 2:
                    group = group[8:16]
                else:
                    group = jnp.where(low_half, swap(group[0:8]), swap(group[8:16]))
                tiles.append(group)
        return jnp.concatenate(tiles, axis=1)

    for dt in range(3):
        for r in range(HALF + 2):
            s3_ref[dt, r * 16 : (r + 1) * 16, :] = jnp.concatenate(
                [placed(r - 1, dt), placed(r + HALF - 1, dt)], axis=0
            ).astype(BF16)

    size = HALF * 16
    logits = jnp.zeros((size, LANES), F32)
    for b in range(BLOCKS):
        lanes = slice(b * WIDE, (b + 1) * WIDE)
        acc = jnp.zeros((size, WIDE), F32)
        for tap in range(9):
            dt, dr = divmod(tap, 3)
            acc = acc + dot(
                s3_ref[dt, dr * 16 : dr * 16 + size, lanes], w3_ref[tap * WIDE : (tap + 1) * WIDE, :]
            )
        third = jnp.maximum(acc + bs_ref[2:3, lanes], 0.0) + s3_ref[1, 16 : 16 + size, lanes].astype(F32)
        high = third.astype(BF16)
        rest = (third - high.astype(F32)).astype(BF16)
        logits = logits + dot(high, rd_ref[lanes, :]) + dot(rest, rd_ref[lanes, :])
    finish(logits.reshape(HALF, 16, LANES), cell_ref, out_ref)


def gate_layers(near_ref, now, steps, exact):
    names, moments = [], []
    for j in range(3):
        there = now - 1 + j
        valid = (there >= 0) & (there < steps)
        safe = jnp.clip(there, 0, steps - 1)
        block = (safe ^ now) if exact else (2, 0, 1)[j]
        tile = near_ref[pl.ds(pl.multiple_of(block * 8, 8), 8), FLAT:].astype(F32).astype(jnp.int32)
        names.append(jnp.where(valid, tile[0:1, :], -1))
        moments.append(jnp.broadcast_to(jnp.where(valid, tile[1:2, :], -1000), (8, LANES)))
    return names, moments


def event_rows(gathered, x_ref, units):
    lane = iota((units, LANES), 1)
    for y in range(HEIGHT):
        tiles = window_rows(gathered, y, lane)
        x_ref[y * units : (y + 1) * units, :] = jnp.concatenate(tiles, axis=1).astype(BF16)


MASKS = (("up", 40), ("gate24", 24), ("ok24", 24), ("low", 8), ("high", 8), ("far_low", 8), ("far_high", 8), ("own", 16), ("gate16", 16), ("ok16", 16))
MASK_AT = {}
MASK_ROWS = 0
for _name, _rows in MASKS:
    MASK_AT[_name] = (MASK_ROWS, _rows)
    MASK_ROWS += _rows
MATES = 48


def early_kernel(
    sizes, near_ref, wf_ref, dn_ref, bs_ref, own_ref, pick_ref, choose_ref, mask_ref, x_ref, f_ref
):
    devices, steps = sizes
    near = steps
    me = lax.axis_index("patch")
    now = lax.axis_index("tm")
    sub = iota((8, LANES), 0)
    low_half = sub < 4
    names, moments = gate_layers(near_ref, now, steps, True)
    late = now < steps // 2
    first_round = 2 * now - 2
    last = DEPTH * steps - 1
    own8 = COUNT * me + sub % COUNT
    name_x = jnp.where(late, names[2], names[0])
    moment_x = jnp.where(late, moments[2], moments[0])

    def half(a, b):
        return jnp.where(low_half, a, b)

    def hot(name):
        return (jnp.broadcast_to(name, (8, LANES)) == own8).astype(F32)

    hots = [hot(name) for name in names]
    hot8 = half(hots[1], hot(name_x))
    moment8 = half(moments[1], moment_x)
    even = moments[1] == 2 * now
    other = jnp.where(even[0:1, :], names[0], names[2])
    square = iota((LANES, LANES), 0)
    wide_hot = jnp.concatenate([hot8, hot8], axis=0).astype(BF16)
    to_own = dot(wide_hot, (square == names[1]).astype(BF16))[0:8]
    to_other = dot(wide_hot, (square == other).astype(BF16))[0:8]
    hot_far = half(to_other, to_own)
    every = jnp.concatenate(hots + [hot_far, hot8, jnp.zeros((8, LANES), F32)], axis=0).astype(BF16)
    index = dot(every, square.astype(F32).astype(BF16)).astype(jnp.int32)
    mate24, far8, mate8 = index[0:24], index[24:32], index[32:40]
    own24 = jnp.concatenate([own8] * 3, axis=0)
    moment24 = jnp.concatenate(moments, axis=0)
    round24 = first_round + iota((24, LANES), 0) // 4
    round16 = first_round + 1 + iota((16, LANES), 0) // 4
    moment16 = jnp.concatenate([half(moments[0], moments[1]), half(moments[1], moments[2])], axis=0)
    step_far = half(jnp.where(even, -1, 1), jnp.where(late, -1, 1))
    moment_far = half(jnp.where(even, moments[0], moments[2]), moments[1])
    touches = (moment_far == moment8 + step_far).astype(F32)
    values = dict(
        up=jnp.concatenate([(own24 < mate24).astype(F32), (mate8 < own8).astype(F32), (mate8 < far8).astype(F32)], axis=0),
        gate24=(round24 == moment24).astype(F32),
        ok24=((round24 >= 0) & (round24 <= last)).astype(F32),
        low=((moment8 - 1 >= 0) & (moment8 - 1 <= last)).astype(F32),
        high=((moment8 + 1 >= 0) & (moment8 + 1 <= last)).astype(F32),
        far_low=jnp.where(step_far < 0, touches, 0.0),
        far_high=jnp.where(step_far > 0, touches, 0.0),
        own=jnp.concatenate([(own8 < mate8).astype(F32)] * 2, axis=0),
        gate16=(round16 == moment16).astype(F32),
        ok16=((round16 >= 0) & (round16 <= last)).astype(F32),
    )
    for name, (at, rows) in MASK_AT.items():
        mask_ref[at : at + rows, :] = values[name]

    columns = choose_ref.shape[1]
    col = iota((1, columns), 1)
    block = col // (8 * near)
    some = devices // 2
    source = me ^ (2 * (block % some) + block // some)
    patch_of = COUNT * source + (col % 8) // DEPTH
    round_of = DEPTH * (now ^ ((col // 8) % near)) + col % DEPTH
    spread = dot(every, (iota((LANES, columns), 0) == patch_of).astype(BF16))
    patch_sel = jnp.concatenate([spread[0:24], spread[24:32], spread[32:40], spread[32:40]], axis=0)

    def lanes_of(x):
        return jnp.broadcast_to(x[:, :1], (x.shape[0], columns))

    want = jnp.concatenate(
        [lanes_of(moment24), lanes_of(moment8 + step_far), lanes_of(moment8 - 1), lanes_of(moment8 + 1)], axis=0
    )
    for dt in range(3):
        choose = jnp.where(round_of == want + (dt - 1), patch_sel, 0.0)
        choose_ref[dt * MATES : (dt + 1) * MATES, :] = choose.astype(BF16)

    rows = near_ref.shape[0]
    col = iota((1, rows), 1)
    patch_of = (col % 8) // DEPTH
    round_of = DEPTH * (now ^ (col // 8)) + col % DEPTH
    unit = iota((24, rows), 0)
    gathered = []
    for dt in range(3):
        choose = (patch_of == unit % COUNT) & (round_of == first_round + unit // 4 + (dt - 1))
        gathered.append(dot(choose.astype(F32).astype(BF16), near_ref[:, :FLAT]))
    event_rows(gathered, x_ref, OWN)
    ahead = [moments[j] == round24[8 * j : 8 * j + 8] for j in range(3)]
    for b in range(BLOCKS):
        lanes = slice(b * WIDE, (b + 1) * WIDE)
        total = dot(x_ref[...], wf_ref[:, lanes])
        own = rounded(jnp.maximum(total + bs_ref[0:1, lanes], 0.0))
        own_ref[:, :, lanes] = own.reshape(HEIGHT, OWN, WIDE)
        latent = rounded(dot(own.astype(BF16), dn_ref[0:WIDE, :])).reshape(HEIGHT, OWN, LANES)
        for y in range(HEIGHT):
            mine = [latent[y, 8 * j : 8 * j + 8] for j in range(3)]
            mine = [jnp.where(ahead[j], mine[j], pltpu.roll(mine[j], 4, 0)) for j in range(3)]
            pick_ref[b, y] = half(mine[1], jnp.where(late, mine[2], mine[0]))


def late_kernel(
    here_ref, there_ref, own_ref, pick_ref, choose_ref, mask_ref, wf_ref, w2_ref, w3_ref, dn_ref, un_ref, rd_ref, bs_ref,
    cell_ref, out_ref, x_ref, f_ref, s_ref, t_ref, c2_ref, s3_ref,
):
    now = lax.axis_index("tm")
    steps = lax.axis_size("tm")
    late = now < steps // 2
    low_half = iota((8, LANES), 0) < 4

    def mask(name, wide=True):
        at, rows = MASK_AT[name]
        value = mask_ref[at : at + rows, :]
        return (jnp.concatenate([value] * 2, axis=1) if wide else value) > 0.5

    def swap(x):
        return pltpu.roll(x, 4, 0)

    events = jnp.concatenate([here_ref[...], there_ref[...]], axis=0)
    picked = dot(choose_ref[...], events)
    event_rows([picked[dt * MATES : (dt + 1) * MATES] for dt in range(3)], x_ref, MATES)

    half_mask = jnp.concatenate([low_half.astype(F32)] * 2, axis=1) > 0.5

    def half(a, b):
        return jnp.where(half_mask, a, b)

    up_mask = mask("up", False)
    gate24, ok24 = mask("gate24"), mask("ok24")
    ok_low, ok_high, far_low, far_high = mask("low"), mask("high"), mask("far_low"), mask("far_high")
    own_mask = mask("own", False)
    gate16, ok16 = mask("gate16"), mask("ok16")
    size = HEIGHT * 16
    part = HALF * 16
    zero = jnp.zeros((8, WIDE), F32)
    s_ref[:, :, 0:16, :] = jnp.zeros((BLOCKS, 3, 16, WIDE), BF16)
    s_ref[:, :, 27 * 16 :, :] = jnp.zeros((BLOCKS, 3, 16, WIDE), BF16)

    def prepare(b):
        lanes = slice(b * WIDE, (b + 1) * WIDE)
        turn = b % 2
        held = {}

        def first():
            held["total"] = dot(x_ref[...], wf_ref[:, lanes])

        def keep():
            total = jnp.maximum(held.pop("total") + bs_ref[0:1, lanes], 0.0)
            f_ref[turn] = rounded(total).reshape(HEIGHT, MATES, WIDE)

        def latents():
            packed = f_ref[turn, :, 0:32, :].reshape(HEIGHT * 32, WIDE).astype(BF16)
            held["latent"] = rounded(dot(packed, dn_ref[0:WIDE, :])).reshape(HEIGHT, 32, LANES)

        def ups():
            latent = held.pop("latent")
            given = jnp.concatenate([latent[:, 0:24], pick_ref[b], latent[:, 24:32]], axis=1)
            both = jnp.concatenate([jnp.where(up_mask, given, 0.0), jnp.where(up_mask, 0.0, given)], axis=2)
            both = both.reshape(HEIGHT * 40, WIDE).astype(BF16)
            held["added"] = dot(both, un_ref[0:WIDE, :]).reshape(HEIGHT, 40, WIDE)

        def mate(y):
            here = f_ref[turn, y]
            add = held["added"][y]
            own = rounded(own_ref[y, :, lanes] + jnp.where(gate24, add[0:24], 0.0))
            own = jnp.where(ok24, own, 0.0)
            turned = [swap(own[8 * j : 8 * j + 8]) for j in range(3)]
            center = jnp.concatenate([half(turned[0], turned[1]), half(turned[1], turned[2])], axis=0)
            top = (y + 1) * 16
            s_ref[b, 0, top : top + 16, :] = own[0:16].astype(BF16)
            s_ref[b, 1, top : top + 16, :] = center.astype(BF16)
            s_ref[b, 2, top : top + 16, :] = own[8:24].astype(BF16)
            middle = half(here[8:16], jnp.where(late, here[16:24], here[0:8]))
            middle = rounded(middle + add[24:32])
            far = add[32:40]
            lower = jnp.where(ok_low, rounded(here[32:40] + jnp.where(far_low, far, 0.0)), 0.0)
            upper = jnp.where(ok_high, rounded(here[40:48] + jnp.where(far_high, far, 0.0)), 0.0)
            return lower, middle, upper

        def put(r, top, bottom):
            for dt in range(3):
                t_ref[b, dt, r * 16 : (r + 1) * 16, :] = jnp.concatenate([top[dt], bottom[dt]], axis=0).astype(BF16)

        def rows(y):
            nothing = (zero, zero, zero)
            top, bottom = mate(y), mate(y + HALF)
            put(y + 1, top, bottom)
            if y == 0:
                put(HALF + 1, bottom, nothing)
            if y == HALF - 1:
                put(0, nothing, top)

        return [first, keep, latents, ups], [functools.partial(rows, y) for y in range(HALF)]

    def convolve(b, held):
        def step(tap):
            dt, dr = divmod(tap, 3)
            lhs = jnp.concatenate(
                [s_ref[b, dt, dr * 16 : dr * 16 + size, :], t_ref[b, dt, dr * 16 : dr * 16 + part, :]], axis=0
            )
            held["acc"] = held.get("acc", jnp.zeros((size + part, WIDE), F32)) + dot(
                lhs, w2_ref[tap * WIDE : (tap + 1) * WIDE, :]
            )

        return [functools.partial(step, tap) for tap in range(9)]

    def conclude(b, held):
        bias2 = bs_ref[1:2, b * WIDE : (b + 1) * WIDE]

        def begin():
            acc = jnp.maximum(held.pop("acc") + bias2, 0.0)
            mates = acc[size:] + t_ref[b, 1, 16 : 16 + part, :].astype(F32)
            held["latent"] = rounded(dot(mates.astype(BF16), dn_ref[WIDE:, :])).reshape(HALF, 16, LANES)
            held["second"] = rounded(acc[:size] + s_ref[b, 1, 16 : 16 + size, :].astype(F32)).reshape(HEIGHT, 16, WIDE)

        def ups():
            latent = held.pop("latent")
            both = jnp.concatenate([jnp.where(own_mask, latent, 0.0), jnp.where(own_mask, 0.0, latent)], axis=2)
            held["added"] = dot(both.reshape(part, WIDE).astype(BF16), un_ref[WIDE:, :]).reshape(HALF, 16, WIDE)

        def row(y):
            at = (y // HALF) * 8
            add = held["added"][y % HALF, at : at + 8]
            add = jnp.concatenate([swap(add), add], axis=0)
            two = rounded(held["second"][y] + jnp.where(gate16, add, 0.0))
            c2_ref[b, y] = jnp.where(ok16, two, 0.0)

        return [begin, ups] + [functools.partial(row, y) for y in range(HEIGHT)]

    def weave(*streams):
        order = []
        for s, stream in enumerate(streams):
            order += [((i + 0.5) / len(stream), s, i) for i in range(len(stream))]
        for _, s, i in sorted(order):
            streams[s][i]()

    lane = iota((16, LANES), 1)
    left, right = lane < CHANS, lane >= LANES - CHANS

    def spread_rows(pair):
        width = 2 * WIDE
        keep = iota((8, width), 0) < 4
        nothing = (jnp.zeros((8, width), F32),) * 3

        def filled(y):
            tiles = []
            for b in (2 * pair, 2 * pair + 1):
                old = pltpu.roll(c2_ref[b - 1, y, :, LANES:], 64, 1) if b else jnp.zeros((16, LANES), F32)
                tiles.append(jnp.where(left, old, c2_ref[b, y, :, :LANES]))
                old = pltpu.roll(c2_ref[b + 1, y, :, :LANES], 64, 1) if b + 1 < BLOCKS else jnp.zeros((16, LANES), F32)
                tiles.append(jnp.where(right, old, c2_ref[b, y, :, LANES:]))
            whole = jnp.concatenate(tiles, axis=1)
            low, high = whole[0:8], whole[8:16]
            return low, jnp.where(keep, swap(low), swap(high)), high

        def store(r, top, bottom):
            for dt in range(3):
                s3_ref[dt, r * 16 : (r + 1) * 16, pair * width : (pair + 1) * width] = jnp.concatenate(
                    [top[dt], bottom[dt]], axis=0
                ).astype(BF16)

        def step(y):
            top, bottom = filled(y), filled(y + HALF)
            store(y + 1, top, bottom)
            if y == 0:
                store(HALF + 1, bottom, nothing)
            if y == HALF - 1:
                store(0, nothing, top)

        return [functools.partial(step, y) for y in range(HALF)]

    def last_layer(pair, held):
        def step(tap):
            dt, dr = divmod(tap, 3)
            lhs = jnp.concatenate(
                [
                    s3_ref[dt, dr * 16 : dr * 16 + part, b * WIDE : (b + 1) * WIDE]
                    for b in (2 * pair, 2 * pair + 1)
                ],
                axis=0,
            )
            held["acc"] = held.get("acc", jnp.zeros((2 * part, WIDE), F32)) + dot(
                lhs, w3_ref[tap * WIDE : (tap + 1) * WIDE, :]
            )

        return [functools.partial(step, tap) for tap in range(9)]

    logits = []

    def readout(pair, held):
        def step(i):
            b = 2 * pair + i
            lanes = slice(b * WIDE, (b + 1) * WIDE)
            third = jnp.maximum(held["acc"][i * part : (i + 1) * part] + bs_ref[2:3, lanes], 0.0)
            third = third + s3_ref[1, 16 : 16 + part, lanes].astype(F32)
            high = third.astype(BF16)
            rest = (third - high.astype(F32)).astype(BF16)
            sums = dot(jnp.concatenate([high, rest], axis=0), rd_ref[lanes, :])
            logits.append(sums[:part] + sums[part:])

        return [functools.partial(step, i) for i in range(2)]

    plans = [prepare(b) for b in range(BLOCKS)]
    helds = [{} for _ in range(BLOCKS)]
    weave(plans[0][0])
    weave(plans[0][1], plans[1][0])
    for b in range(BLOCKS):
        streams = [convolve(b, helds[b])]
        ends = conclude(b - 1, helds[b - 1]) if b else []
        if b + 1 < BLOCKS:
            if ends:
                streams.append(ends)
            streams.append(plans[b + 1][1])
        else:
            streams.append(ends + spread_rows(0))
        if b + 2 < BLOCKS:
            streams.append(plans[b + 2][0])
        weave(*streams)
    thirds = [{}, {}]
    weave(last_layer(0, thirds[0]), conclude(BLOCKS - 1, helds[-1]) + spread_rows(1))
    weave(last_layer(1, thirds[1]), readout(0, thirds[0]))
    weave(readout(1, thirds[1]))
    finish(sum(logits[1:], logits[0]).reshape(HALF, 16, LANES), cell_ref, out_ref)


def finish(logits, cell_ref, out_ref):
    lane8 = iota((8, LANES), 1)
    flat = [jnp.zeros((8, LANES), F32) for _ in range(FLAT // LANES)]
    for y in range(HEIGHT):
        row = logits[y % HALF, (y // HALF) * 8 : (y // HALF) * 8 + 8]
        begin = y * WIDTH
        turned = pltpu.roll(row, begin % LANES, 1) if begin % LANES else row
        for dst in range(FLAT // LANES):
            a = max(begin, dst * LANES) - dst * LANES
            e = min(begin + WIDTH, (dst + 1) * LANES) - dst * LANES
            if a < e:
                flat[dst] = jnp.where((lane8 >= a) & (lane8 < e), turned, flat[dst])
    flat = jnp.concatenate(flat, axis=1)[:, : HEIGHT * WIDTH] + cell_ref[...]
    for j in range(DEPTH):
        for p in range(COUNT):
            out_ref[p, j : j + 1, :] = flat[4 * j + p : 4 * j + p + 1, :]


def in_hbm(x):
    return pltpu.with_memory_space_constraint(x, pltpu.HBM)


def swapped(block, axis, mask):
    count = lax.axis_size(axis)
    return lax.ppermute(block, axis, [(i, i ^ mask) for i in range(count)])


def shifted(block, axis, offset):
    count = lax.axis_size(axis)
    return lax.ppermute(block, axis, [(i, i - offset) for i in range(count) if 0 <= i - offset < count])


def shards(
    bits, partners, gate_round, first_kernel, second_kernels, conv_bias, couple_down, couple_up, head, cell_bias
):
    devices, steps = lax.axis_size("patch"), lax.axis_size("tm")
    latent = couple_down.shape[-1]
    total = BLOCKS * WIDE
    vmem = pl.BlockSpec(memory_space=pltpu.VMEM)
    hbm = pl.BlockSpec(memory_space=pltpu.HBM)
    mine = pl.pallas_call(
        pack_kernel,
        out_shape=jax.ShapeDtypeStruct((8, FLAT + LANES), BF16),
        in_specs=[hbm, hbm, pl.BlockSpec(memory_space=pltpu.SMEM)],
        out_specs=vmem,
        scratch_shapes=[
            pltpu.VMEM((COUNT, DEPTH, WIDTH, HEIGHT), jnp.int32),
            pltpu.VMEM(partners.shape, jnp.int32),
            pltpu.SemaphoreType.DMA((2,)),
        ],
        compiler_params=pltpu.CompilerParams(vmem_limit_bytes=2 << 20),
        name="pack",
    )(in_hbm(jnp.swapaxes(bits, 2, 3)), in_hbm(partners), gate_round)

    exact = steps == 4 and devices > 1
    if exact:
        blocks = [mine] + [
            lax.ppermute(mine, "tm", [(i, i ^ k if abs(i - (i ^ k)) <= 2 else i) for i in range(steps)])
            for k in (1, 2, 3)
        ]
    else:
        blocks = [mine] + [shifted(mine, "tm", k) for k in (1, -1, 2, -2)]
    near = jnp.concatenate(blocks, axis=0)
    params = (
        first_kernel,
        second_kernels.reshape(54 * CHANS, CHANS),
        conv_bias,
        jnp.swapaxes(couple_down, 1, 2),
        couple_up,
        head.reshape(1, CHANS),
    )
    weights = pl.pallas_call(
        weights_kernel,
        out_shape=[
            jax.ShapeDtypeStruct((WIDE, total), BF16),
            jax.ShapeDtypeStruct((9 * WIDE, WIDE), BF16),
            jax.ShapeDtypeStruct((9 * WIDE, WIDE), BF16),
            jax.ShapeDtypeStruct((2 * WIDE, SLOTS * latent), BF16),
            jax.ShapeDtypeStruct((4 * SLOTS * latent, WIDE), BF16),
            jax.ShapeDtypeStruct((total, LANES), BF16),
            jax.ShapeDtypeStruct((8, total), F32),
        ],
        in_specs=[hbm] * 6,
        out_specs=[vmem] * 7,
        scratch_shapes=[pltpu.VMEM((WIDE, total), F32)]
        + [pltpu.VMEM(x.shape, x.dtype) for x in params]
        + [pltpu.SemaphoreType.DMA((6,))],
        cost_estimate=pl.CostEstimate(flops=10**9, bytes_accessed=10**7, transcendentals=0),
        compiler_params=pltpu.CompilerParams(vmem_limit_bytes=12 << 20),
        name="weights",
    )(*map(in_hbm, params))

    every = near[:, :FLAT]
    parts = [every] + [swapped(every, "patch", 2 * m) for m in range(1, devices // 2)]
    every = jnp.concatenate(parts, axis=0)
    every, weights = lax.optimization_barrier((every, weights))
    others = swapped(every, "patch", 1)

    if exact:
        wf, w2, w3, dn, un, rd, bs = weights
        early = pl.pallas_call(
            functools.partial(early_kernel, (devices, steps)),
            out_shape=[
                jax.ShapeDtypeStruct((HEIGHT, OWN, total), F32),
                jax.ShapeDtypeStruct((BLOCKS, HEIGHT, 8, LANES), F32),
                jax.ShapeDtypeStruct((3 * MATES, 8 * steps * devices), BF16),
                jax.ShapeDtypeStruct((MASK_ROWS, LANES), F32),
            ],
            in_specs=[vmem] * 4,
            out_specs=[vmem] * 4,
            scratch_shapes=[pltpu.VMEM((HEIGHT * OWN, WIDE), BF16), pltpu.VMEM((8, LANES), F32)],
            cost_estimate=pl.CostEstimate(flops=10**9, bytes_accessed=10**7, transcendentals=0),
            compiler_params=pltpu.CompilerParams(vmem_limit_bytes=14 << 20),
            name="early",
        )(near, wf, dn, bs)
        return pl.pallas_call(
            late_kernel,
            out_shape=jax.ShapeDtypeStruct((COUNT, DEPTH, HEIGHT * WIDTH), F32),
            in_specs=[vmem] * 14,
            out_specs=vmem,
            scratch_shapes=[
                pltpu.VMEM((HEIGHT * MATES, WIDE), BF16),
                pltpu.VMEM((2, HEIGHT, MATES, WIDE), F32),
                pltpu.VMEM((BLOCKS, 3, 28 * 16, WIDE), BF16),
                pltpu.VMEM((BLOCKS, 3, (HALF + 2) * 16, WIDE), BF16),
                pltpu.VMEM((BLOCKS, HEIGHT, 16, WIDE), F32),
                pltpu.VMEM((3, (HALF + 2) * 16, total), BF16),
            ],
            compiler_params=pltpu.CompilerParams(vmem_limit_bytes=36 << 20),
            name="late",
        )(every, others, *early, wf, w2, w3, dn, un, rd, bs, cell_bias.reshape(1, HEIGHT * WIDTH))
    return pl.pallas_call(
        functools.partial(main_kernel, (devices, steps, exact)),
        out_shape=jax.ShapeDtypeStruct((COUNT, DEPTH, HEIGHT * WIDTH), F32),
        in_specs=[vmem] * 11,
        out_specs=vmem,
        scratch_shapes=[
            pltpu.VMEM((HEIGHT * UNITS, WIDE), BF16),
            pltpu.VMEM((HEIGHT, UNITS, WIDE), F32),
            pltpu.VMEM((3, 28 * 32, WIDE), BF16),
            pltpu.VMEM((BLOCKS, HEIGHT, 16, WIDE), F32),
            pltpu.VMEM((3, (HALF + 2) * 16, total), BF16),
        ],
        compiler_params=pltpu.CompilerParams(vmem_limit_bytes=40 << 20),
        name="decode",
    )(every, others, near, *weights, cell_bias.reshape(1, HEIGHT * WIDTH))


def solution(mesh):
    in_specs = (
        P("patch", "tm", None, None),
        P("tm", None),
        P("tm"),
        P(),
        P(),
        P(),
        P(),
        P(),
        P(),
        P(),
    )
    out_specs = P("patch", "tm", None)
    return jax.shard_map(shards, mesh=mesh, in_specs=in_specs, out_specs=out_specs, check_vma=False)
```

```python
import functools

import jax
import jax.numpy as jnp
from jax import lax
from jax.experimental import pallas as pl
from jax.experimental.pallas import tpu as pltpu
from jax.sharding import PartitionSpec as P

F32 = jnp.float32
BF16 = jnp.bfloat16
LANES = 128
COUNT = 4
DEPTH = 2
HEIGHT = 26
WIDTH = 24
CHANS = 32
WINDOW = 6
SLOTS = 8
BLOCKS = WIDTH // WINDOW
WIDE = SLOTS * CHANS
FLAT = 640
OWN, MATE, UNITS = 24, 16, 96
HALF = HEIGHT // 2


def iota(shape, dim):
    return lax.broadcasted_iota(jnp.int32, shape, dim)


def rounded(x):
    return x.astype(BF16).astype(F32)


def dot(a, b):
    return jnp.dot(a, b, preferred_element_type=F32)


def fetch(pairs, sems):
    copies = [pltpu.make_async_copy(src, dst, sems.at[i]) for i, (src, dst) in enumerate(pairs)]
    for copy in copies:
        copy.start()
    for copy in copies:
        copy.wait()


def pack_kernel(bits_hbm, partners_hbm, gate_ref, out_ref, bits_ref, partners_ref, sems):
    fetch(((bits_hbm, bits_ref), (partners_hbm, partners_ref)), sems)
    units = COUNT * DEPTH
    bits = bits_ref[...].reshape(units, WIDTH, HEIGHT).astype(F32)
    bits = jnp.swapaxes(bits, 1, 2)
    rows = [bits[:, y, :] for y in range(HEIGHT)]
    flat = jnp.concatenate(rows + [jnp.zeros((units, FLAT - HEIGHT * WIDTH), F32)], axis=1)
    out_ref[:, :FLAT] = flat.astype(BF16)
    patches = partners_ref.shape[1]
    names = partners_ref[...].astype(F32)
    if patches < LANES:
        names = jnp.concatenate([names, jnp.full((1, LANES - patches), -1.0, F32)], axis=1)
    moment = jnp.full((1, LANES), gate_ref[0], jnp.int32).astype(F32)
    sub = iota((units, LANES), 0)
    out_ref[:, FLAT:] = jnp.where(sub == 0, names, jnp.where(sub == 1, moment, 0.0)).astype(BF16)


def weights_kernel(
    first_hbm, second_hbm, bias_hbm, down_hbm, up_hbm, head_hbm,
    wf_ref, w2_ref, w3_ref, dn_ref, un_ref, rd_ref, bs_ref,
    scr_ref, first_ref, second_ref, bias_ref, down_ref, up_ref, head_ref, sems,
):
    sources = (first_hbm, second_hbm, bias_hbm, down_hbm, up_hbm, head_hbm)
    fetch(zip(sources, (first_ref, second_ref, bias_ref, down_ref, up_ref, head_ref)), sems)
    total = BLOCKS * WIDE
    spread = (iota((CHANS, WIDE), 1) % CHANS == iota((CHANS, WIDE), 0)).astype(BF16)
    slot = iota((CHANS, WIDE), 1) // CHANS
    inner = (slot >= 1) & (slot <= WINDOW)
    for layer, w_ref in enumerate((w2_ref, w3_ref)):
        for tap in range(9):
            base = (layer * 27 + tap * 3) * CHANS
            tiled = dot(second_ref[base : base + 3 * CHANS, :], spread)
            for kc in range(SLOTS):
                block = jnp.zeros((CHANS, WIDE), F32)
                for dc in range(3):
                    block = jnp.where(
                        inner & (slot == kc - dc + 1), tiled[dc * CHANS : (dc + 1) * CHANS], block
                    )
                w_ref[tap * WIDE + kc * CHANS : tap * WIDE + (kc + 1) * CHANS, :] = block.astype(BF16)
    across = (iota((CHANS, total), 1) % CHANS == iota((CHANS, total), 0)).astype(BF16)
    for pair in range(9):
        scr_ref[8 * pair : 8 * pair + 3, :CHANS] = first_ref[pair // 3, pair % 3].astype(F32)
    taps = dot(scr_ref[0:72, :CHANS].astype(BF16), across)
    lane = iota((WIDTH, total), 1)
    column = (lane // WIDE) * WINDOW - 1 + (lane % WIDE) // CHANS
    real = (column >= 0) & (column < WIDTH)
    offset = iota((WIDTH, total), 0) - column + 1
    for pair in range(9):
        block = jnp.zeros((WIDTH, total), F32)
        for dc in range(3):
            block = jnp.where(real & (offset == dc), taps[pair * 8 + dc : pair * 8 + dc + 1, :], block)
        scr_ref[pair * WIDTH : (pair + 1) * WIDTH, :] = block
    scr_ref[9 * WIDTH :, :] = jnp.zeros((WIDE - 9 * WIDTH, total), F32)
    wf_ref[...] = scr_ref[...].astype(BF16)
    latent = down_ref.shape[1]
    low = SLOTS * latent
    thin = (iota((latent, low), 1) % latent == iota((latent, low), 0)).astype(BF16)
    for layer in range(2):
        tiled = lax.dot_general(
            down_ref[layer], thin, (((0,), (0,)), ((), ())), preferred_element_type=F32
        )
        for kc in range(SLOTS):
            keep = iota((CHANS, low), 1) // latent == kc
            dn_ref[layer * WIDE + kc * CHANS : layer * WIDE + (kc + 1) * CHANS, :] = jnp.where(
                keep, tiled, 0.0
            ).astype(BF16)
        for role in range(2):
            tiled = dot(up_ref[layer, role], spread)
            for kc in range(SLOTS):
                keep = iota((latent, WIDE), 1) // CHANS == kc
                top = (layer * 2 + role) * low + kc * latent
                un_ref[top : top + latent, :] = jnp.where(keep, tiled, 0.0).astype(BF16)
    row = iota((total, CHANS), 0)
    chosen = jnp.where(row % CHANS == iota((total, CHANS), 1), head_ref[...].astype(F32), 0.0)
    values = dot(chosen.astype(BF16), jnp.ones((CHANS, LANES), BF16))
    row = iota((total, LANES), 0)
    place = (row % WIDE) // CHANS
    target = (row // WIDE) * WINDOW - 1 + place
    keep = (place >= 1) & (place <= WINDOW) & (target == iota((total, LANES), 1))
    rd_ref[...] = jnp.where(keep, values, 0.0).astype(BF16)
    scr_ref[0:8, :CHANS] = jnp.zeros((8, CHANS), F32)
    scr_ref[0:3, :CHANS] = bias_ref[...]
    biases = jnp.dot(
        scr_ref[0:8, :CHANS], across.astype(F32), preferred_element_type=F32, precision=lax.Precision.HIGHEST
    )
    lane = iota((8, total), 1)
    place = (lane % WIDE) // CHANS
    column = (lane // WIDE) * WINDOW - 1 + place
    real = (column >= 0) & (column < WIDTH)
    inside = (place >= 1) & (place <= WINDOW)
    top = iota((8, total), 0) == 0
    keep = (top & real) | (~top & inside)
    bs_ref[...] = jnp.where(keep, biases, 0.0)


def window_rows(gathered, y, lane):
    start = WIDTH * (y - 1)
    length = 3 * WIDTH
    tiles = [None, None]
    for dt in range(3):
        begin = length * dt
        shift = begin - start
        for src in range(FLAT // LANES):
            lo = max(start, 0, src * LANES)
            hi = min(start + length, FLAT, (src + 1) * LANES)
            if lo >= hi:
                continue
            source = gathered[dt][:, src * LANES : (src + 1) * LANES]
            turned = pltpu.roll(source, shift % LANES, 1) if shift % LANES else source
            for dst in range(2):
                a = max(lo + shift, dst * LANES) - dst * LANES
                b = min(hi + shift, (dst + 1) * LANES) - dst * LANES
                if a >= b:
                    continue
                old = jnp.zeros_like(turned) if tiles[dst] is None else tiles[dst]
                tiles[dst] = jnp.where((lane >= a) & (lane < b), turned, old)
    return tiles


def main_kernel(
    sizes, here_ref, there_ref, meta_ref, wf_ref, w2_ref, w3_ref, dn_ref, un_ref, rd_ref, bs_ref, cell_ref,
    out_ref, x_ref, f_ref, s_ref, c2_ref, s3_ref,
):
    devices, steps, exact = sizes
    near = meta_ref.shape[0] // 8
    me = lax.axis_index("patch")
    now = lax.axis_index("tm")
    sub = iota((8, LANES), 0)
    low_half = sub < 4

    names, moments = gate_layers(meta_ref, now, steps, exact)
    first_round = 2 * now - 2
    own_patch = COUNT * me + sub % COUNT

    def pair(parts):
        return jnp.concatenate(
            [jnp.where(low_half, parts[0], parts[1]), jnp.where(low_half, parts[1], parts[2])], axis=0
        )

    hot = [(jnp.broadcast_to(names[j], (8, LANES)) == own_patch).astype(F32) for j in range(3)]
    hot24 = jnp.concatenate(hot, axis=0).astype(BF16)
    hot16f = pair(hot)
    hot16 = hot16f.astype(BF16)
    square = iota((LANES, LANES), 0)
    even = moments[1] == 2 * now
    other = jnp.where(even[0:1, :], names[0], names[2])
    perm_one = (square == names[1]).astype(BF16)
    perm_other = (square == other).astype(BF16)
    middle = (iota((16, LANES), 0) >= 4) & (iota((16, LANES), 0) < 12)
    hot_far = jnp.where(middle, dot(hot16, perm_other), dot(hot16, perm_one))
    hots = jnp.concatenate([hot24, hot_far.astype(BF16), hot16], axis=0)
    index = dot(hots, square.astype(F32).astype(BF16)).astype(jnp.int32)
    mate24, far16, mate16 = index[0:24], index[24:40], index[40:56]
    own24 = jnp.concatenate([own_patch] * 3, axis=0)
    own16 = jnp.concatenate([own_patch] * 2, axis=0)

    moment24 = jnp.concatenate(moments, axis=0)
    moment16 = pair(moments)
    round24 = first_round + iota((24, LANES), 0) // 4
    round16 = first_round + 1 + iota((16, LANES), 0) // 4
    last = DEPTH * steps - 1
    step_far = pair([jnp.full((8, LANES), 1, jnp.int32), jnp.where(even, -1, 1), jnp.full((8, LANES), -1, jnp.int32)])
    moment_far = pair([moments[1], jnp.where(even, moments[0], moments[2]), moments[1]])
    touches = moment_far == moment16 + step_far
    far_low = touches & (step_far < 0)
    far_high = touches & (step_far > 0)

    columns = 2 * here_ref.shape[0]
    events = jnp.concatenate([here_ref[...], there_ref[...]], axis=0)
    col = iota((1, columns), 1)
    block = col // (8 * near)
    half = devices // 2
    source = me ^ (2 * (block % half) + block // half) if devices > 1 else me + 0 * block
    patch_of = COUNT * source + (col % 8) // DEPTH
    step = (col // 8) % near
    if exact:
        time_of = now ^ step
    else:
        time_of = now + jnp.where(step == 1, 1, jnp.where(step == 2, -1, jnp.where(step == 3, 2, jnp.where(step == 4, -2, 0))))
    round_of = DEPTH * time_of + col % DEPTH
    expand = (iota((LANES, columns), 0) == patch_of).astype(BF16)
    spread = dot(hots, expand)

    def lanes_of(x):
        return jnp.broadcast_to(x[:, :1], (x.shape[0], columns))

    is_own = (patch_of == lanes_of(own24)).astype(F32)
    patch_sel = jnp.concatenate(
        [is_own, spread[0:24], spread[24:40], spread[40:56], spread[40:56]], axis=0
    )
    want = jnp.concatenate(
        [
            lanes_of(round24),
            lanes_of(moment24),
            lanes_of(moment16 + step_far),
            lanes_of(moment16 - 1),
            lanes_of(moment16 + 1),
        ],
        axis=0,
    )
    gathered = []
    for dt in range(3):
        choose = jnp.where(round_of == want + (dt - 1), patch_sel, 0.0).astype(BF16)
        gathered.append(dot(choose, events))
    lane = iota((UNITS, LANES), 1)
    for y in range(HEIGHT):
        tiles = window_rows(gathered, y, lane)
        x_ref[y * UNITS : (y + 1) * UNITS, :] = jnp.concatenate(tiles, axis=1).astype(BF16)

    s_ref[:, 0:32, :] = jnp.zeros((3, 32, WIDE), BF16)
    s_ref[:, 27 * 32 :, :] = jnp.zeros((3, 32, WIDE), BF16)

    def wide(mask):
        return jnp.concatenate([mask.astype(jnp.int32)] * 2, axis=1) != 0

    ctrl_up = jnp.concatenate([mate24 - own24, own16 - mate16, far16 - mate16], axis=0) > 0
    gate24 = wide(round24 == moment24)
    gate16 = wide(round16 == moment16)
    ok24 = wide((round24 >= 0) & (round24 <= last))
    ok16 = wide((round16 >= 0) & (round16 <= last))
    ok_low = wide((moment16 - 1 >= 0) & (moment16 - 1 <= last))
    ok_high = wide((moment16 + 1 >= 0) & (moment16 + 1 <= last))
    far_low, far_high = wide(far_low), wide(far_high)
    ctrl_own16 = own16 < mate16
    at_moment = round24 == moment24

    def swap(x):
        return pltpu.roll(x, 4, 0)

    def body(b, carry):
        lanes = pl.ds(pl.multiple_of(b * WIDE, WIDE), WIDE)
        bias1 = bs_ref[0:1, lanes]
        bias2 = bs_ref[1:2, lanes]
        total = dot(x_ref[...], wf_ref[:, lanes])
        f_ref[...] = rounded(jnp.maximum(total + bias1, 0.0)).reshape(HEIGHT, UNITS, WIDE)
        packed = f_ref[:, 0:64, :].reshape(HEIGHT * 64, WIDE).astype(BF16)
        latent = rounded(dot(packed, dn_ref[0:WIDE, :])).reshape(HEIGHT, 64, LANES)
        rows = []
        for y in range(HEIGHT):
            lat = latent[y]
            mine = [lat[8 * j : 8 * j + 8] for j in range(3)]
            mine = [jnp.where(at_moment[8 * j : 8 * j + 8], mine[j], swap(mine[j])) for j in range(3)]
            rows.append(jnp.concatenate([lat[24:48], pair(mine), lat[48:64]], axis=0))
        given = jnp.stack(rows, axis=0)
        both = jnp.concatenate(
            [jnp.where(ctrl_up, given, 0.0), jnp.where(ctrl_up, 0.0, given)], axis=2
        ).reshape(HEIGHT * 56, WIDE)
        added = dot(both.astype(BF16), un_ref[0:WIDE, :]).reshape(HEIGHT, 56, WIDE)
        half_mask = wide(low_half)
        for y in range(HEIGHT):
            here = f_ref[y]
            add = added[y]
            own = rounded(here[0:24] + jnp.where(gate24, add[0:24], 0.0))
            own = jnp.where(ok24, own, 0.0)
            m = [here[24 + 8 * j : 32 + 8 * j] for j in range(3)]
            mid = jnp.concatenate(
                [jnp.where(half_mask, m[0], m[1]), jnp.where(half_mask, m[1], m[2])], axis=0
            )
            mid = rounded(mid + add[24:40])
            far = add[40:56]
            lower = jnp.where(ok_low, rounded(here[64:80] + jnp.where(far_low, far, 0.0)), 0.0)
            upper = jnp.where(ok_high, rounded(here[80:96] + jnp.where(far_high, far, 0.0)), 0.0)
            turned = [swap(own[8 * j : 8 * j + 8]) for j in range(3)]
            center = jnp.concatenate(
                [jnp.where(half_mask, turned[0], turned[1]), jnp.where(half_mask, turned[1], turned[2])], axis=0
            )
            top = (y + 1) * 32
            s_ref[0, top : top + 32, :] = jnp.concatenate([own[0:16], lower], axis=0).astype(BF16)
            s_ref[1, top : top + 32, :] = jnp.concatenate([center, mid], axis=0).astype(BF16)
            s_ref[2, top : top + 32, :] = jnp.concatenate([own[8:24], upper], axis=0).astype(BF16)
        size = HEIGHT * 32
        acc = jnp.zeros((size, WIDE), F32)
        for tap in range(9):
            dt, dr = divmod(tap, 3)
            acc = acc + dot(
                s_ref[dt, dr * 32 : dr * 32 + size, :], w2_ref[tap * WIDE : (tap + 1) * WIDE, :]
            )
        second = jnp.maximum(acc + bias2, 0.0) + s_ref[1, 32 : 32 + size, :].astype(F32)
        second = second.reshape(HEIGHT, 32, WIDE)
        mates = second[:, 16:32, :].reshape(HEIGHT * 16, WIDE).astype(BF16)
        latent = rounded(dot(mates, dn_ref[WIDE:, :])).reshape(HEIGHT, 16, LANES)
        both = jnp.concatenate(
            [jnp.where(ctrl_own16, latent, 0.0), jnp.where(ctrl_own16, 0.0, latent)], axis=2
        ).reshape(HEIGHT * 16, WIDE)
        added = dot(both.astype(BF16), un_ref[WIDE:, :]).reshape(HEIGHT, 16, WIDE)
        two = rounded(rounded(second[:, 0:16, :]) + jnp.where(gate16, added, 0.0))
        c2_ref[b] = jnp.where(ok16, two, 0.0)
        return carry

    lax.fori_loop(0, BLOCKS, body, 0)


    def placed(y, dt):
        if y < 0 or y >= HEIGHT:
            return jnp.zeros((8, BLOCKS * WIDE), F32)
        tiles = []
        for b in range(BLOCKS):
            for t in range(2):
                group = c2_ref[b, y, :, t * LANES : (t + 1) * LANES]
                if t == 0:
                    old = pltpu.roll(c2_ref[b - 1, y, :, LANES:], 64, 1) if b else jnp.zeros((16, LANES), F32)
                    group = jnp.where(iota((16, LANES), 1) < CHANS, old, group)
                else:
                    old = pltpu.roll(c2_ref[b + 1, y, :, :LANES], 64, 1) if b + 1 < BLOCKS else jnp.zeros((16, LANES), F32)
                    group = jnp.where(iota((16, LANES), 1) >= LANES - CHANS, old, group)
                if dt == 0:
                    group = group[0:8]
                elif dt == 2:
                    group = group[8:16]
                else:
                    group = jnp.where(low_half, swap(group[0:8]), swap(group[8:16]))
                tiles.append(group)
        return jnp.concatenate(tiles, axis=1)

    for dt in range(3):
        for r in range(HALF + 2):
            s3_ref[dt, r * 16 : (r + 1) * 16, :] = jnp.concatenate(
                [placed(r - 1, dt), placed(r + HALF - 1, dt)], axis=0
            ).astype(BF16)

    size = HALF * 16
    logits = jnp.zeros((size, LANES), F32)
    for b in range(BLOCKS):
        lanes = slice(b * WIDE, (b + 1) * WIDE)
        acc = jnp.zeros((size, WIDE), F32)
        for tap in range(9):
            dt, dr = divmod(tap, 3)
            acc = acc + dot(
                s3_ref[dt, dr * 16 : dr * 16 + size, lanes], w3_ref[tap * WIDE : (tap + 1) * WIDE, :]
            )
        third = jnp.maximum(acc + bs_ref[2:3, lanes], 0.0) + s3_ref[1, 16 : 16 + size, lanes].astype(F32)
        high = third.astype(BF16)
        rest = (third - high.astype(F32)).astype(BF16)
        logits = logits + dot(high, rd_ref[lanes, :]) + dot(rest, rd_ref[lanes, :])
    finish(logits.reshape(HALF, 16, LANES), cell_ref, out_ref)


def gate_layers(near_ref, now, steps, exact):
    names, moments = [], []
    for j in range(3):
        there = now - 1 + j
        valid = (there >= 0) & (there < steps)
        safe = jnp.clip(there, 0, steps - 1)
        block = (safe ^ now) if exact else (2, 0, 1)[j]
        tile = near_ref[pl.ds(pl.multiple_of(block * 8, 8), 8), FLAT:].astype(F32).astype(jnp.int32)
        names.append(jnp.where(valid, tile[0:1, :], -1))
        moments.append(jnp.broadcast_to(jnp.where(valid, tile[1:2, :], -1000), (8, LANES)))
    return names, moments


def event_rows(gathered, x_ref, units):
    lane = iota((units, LANES), 1)
    for y in range(HEIGHT):
        tiles = window_rows(gathered, y, lane)
        x_ref[y * units : (y + 1) * units, :] = jnp.concatenate(tiles, axis=1).astype(BF16)


MASKS = (("up", 40), ("gate24", 24), ("ok24", 24), ("low", 8), ("high", 8), ("far_low", 8), ("far_high", 8), ("own", 16), ("gate16", 16), ("ok16", 16))
MASK_AT = {}
MASK_ROWS = 0
for _name, _rows in MASKS:
    MASK_AT[_name] = (MASK_ROWS, _rows)
    MASK_ROWS += _rows
MATES = 48


def early_kernel(
    sizes, near_ref, wf_ref, dn_ref, bs_ref, own_ref, pick_ref, choose_ref, mask_ref, x_ref, f_ref
):
    devices, steps = sizes
    near = steps
    me = lax.axis_index("patch")
    now = lax.axis_index("tm")
    sub = iota((8, LANES), 0)
    low_half = sub < 4
    names, moments = gate_layers(near_ref, now, steps, True)
    late = now < steps // 2
    first_round = 2 * now - 2
    last = DEPTH * steps - 1
    own8 = COUNT * me + sub % COUNT
    name_x = jnp.where(late, names[2], names[0])
    moment_x = jnp.where(late, moments[2], moments[0])

    def half(a, b):
        return jnp.where(low_half, a, b)

    def hot(name):
        return (jnp.broadcast_to(name, (8, LANES)) == own8).astype(F32)

    hots = [hot(name) for name in names]
    hot8 = half(hots[1], hot(name_x))
    moment8 = half(moments[1], moment_x)
    even = moments[1] == 2 * now
    other = jnp.where(even[0:1, :], names[0], names[2])
    square = iota((LANES, LANES), 0)
    wide_hot = jnp.concatenate([hot8, hot8], axis=0).astype(BF16)
    to_own = dot(wide_hot, (square == names[1]).astype(BF16))[0:8]
    to_other = dot(wide_hot, (square == other).astype(BF16))[0:8]
    hot_far = half(to_other, to_own)
    every = jnp.concatenate(hots + [hot_far, hot8, jnp.zeros((8, LANES), F32)], axis=0).astype(BF16)
    index = dot(every, square.astype(F32).astype(BF16)).astype(jnp.int32)
    mate24, far8, mate8 = index[0:24], index[24:32], index[32:40]
    own24 = jnp.concatenate([own8] * 3, axis=0)
    moment24 = jnp.concatenate(moments, axis=0)
    round24 = first_round + iota((24, LANES), 0) // 4
    round16 = first_round + 1 + iota((16, LANES), 0) // 4
    moment16 = jnp.concatenate([half(moments[0], moments[1]), half(moments[1], moments[2])], axis=0)
    step_far = half(jnp.where(even, -1, 1), jnp.where(late, -1, 1))
    moment_far = half(jnp.where(even, moments[0], moments[2]), moments[1])
    touches = (moment_far == moment8 + step_far).astype(F32)
    values = dict(
        up=jnp.concatenate([(own24 < mate24).astype(F32), (mate8 < own8).astype(F32), (mate8 < far8).astype(F32)], axis=0),
        gate24=(round24 == moment24).astype(F32),
        ok24=((round24 >= 0) & (round24 <= last)).astype(F32),
        low=((moment8 - 1 >= 0) & (moment8 - 1 <= last)).astype(F32),
        high=((moment8 + 1 >= 0) & (moment8 + 1 <= last)).astype(F32),
        far_low=jnp.where(step_far < 0, touches, 0.0),
        far_high=jnp.where(step_far > 0, touches, 0.0),
        own=jnp.concatenate([(own8 < mate8).astype(F32)] * 2, axis=0),
        gate16=(round16 == moment16).astype(F32),
        ok16=((round16 >= 0) & (round16 <= last)).astype(F32),
    )
    for name, (at, rows) in MASK_AT.items():
        mask_ref[at : at + rows, :] = values[name]

    columns = choose_ref.shape[1]
    col = iota((1, columns), 1)
    block = col // (8 * near)
    some = devices // 2
    source = me ^ (2 * (block % some) + block // some)
    patch_of = COUNT * source + (col % 8) // DEPTH
    round_of = DEPTH * (now ^ ((col // 8) % near)) + col % DEPTH
    spread = dot(every, (iota((LANES, columns), 0) == patch_of).astype(BF16))
    patch_sel = jnp.concatenate([spread[0:24], spread[24:32], spread[32:40], spread[32:40]], axis=0)

    def lanes_of(x):
        return jnp.broadcast_to(x[:, :1], (x.shape[0], columns))

    want = jnp.concatenate(
        [lanes_of(moment24), lanes_of(moment8 + step_far), lanes_of(moment8 - 1), lanes_of(moment8 + 1)], axis=0
    )
    for dt in range(3):
        choose = jnp.where(round_of == want + (dt - 1), patch_sel, 0.0)
        choose_ref[dt * MATES : (dt + 1) * MATES, :] = choose.astype(BF16)

    rows = near_ref.shape[0]
    col = iota((1, rows), 1)
    patch_of = (col % 8) // DEPTH
    round_of = DEPTH * (now ^ (col // 8)) + col % DEPTH
    unit = iota((24, rows), 0)
    gathered = []
    for dt in range(3):
        choose = (patch_of == unit % COUNT) & (round_of == first_round + unit // 4 + (dt - 1))
        gathered.append(dot(choose.astype(F32).astype(BF16), near_ref[:, :FLAT]))
    event_rows(gathered, x_ref, OWN)
    kept = jnp.concatenate([values["ok24"]] * 2, axis=1) > 0.5
    ahead = [moments[j] == round24[8 * j : 8 * j + 8] for j in range(3)]
    for b in range(BLOCKS):
        lanes = slice(b * WIDE, (b + 1) * WIDE)
        total = dot(x_ref[...], wf_ref[:, lanes])
        own = rounded(jnp.maximum(total + bs_ref[0:1, lanes], 0.0))
        own_ref[:, :, lanes] = jnp.where(kept, own.reshape(HEIGHT, OWN, WIDE), 0.0)
        latent = dot(own.astype(BF16), dn_ref[0:WIDE, :]).reshape(HEIGHT, OWN, LANES)
        for y in range(HEIGHT):
            mine = [latent[y, 8 * j : 8 * j + 8] for j in range(3)]
            mine = [jnp.where(ahead[j], mine[j], pltpu.roll(mine[j], 4, 0)) for j in range(3)]
            pick_ref[b, y] = half(mine[1], jnp.where(late, mine[2], mine[0]))


def late_kernel(
    here_ref, there_ref, own_ref, pick_ref, choose_ref, mask_ref, wf_ref, w2_ref, w3_ref, dn_ref, un_ref, rd_ref, bs_ref,
    cell_ref, out_ref, x_ref, f_ref, s_ref, t_ref, c2_ref, s3_ref,
):
    now = lax.axis_index("tm")
    steps = lax.axis_size("tm")
    late = now < steps // 2
    low_half = iota((8, LANES), 0) < 4

    def mask(name, wide=True):
        at, rows = MASK_AT[name]
        value = mask_ref[at : at + rows, :]
        return (jnp.concatenate([value] * 2, axis=1) if wide else value) > 0.5

    def swap(x):
        return pltpu.roll(x, 4, 0)

    events = jnp.concatenate([here_ref[...], there_ref[...]], axis=0)
    picked = dot(choose_ref[...], events)
    event_rows([picked[dt * MATES : (dt + 1) * MATES] for dt in range(3)], x_ref, MATES)

    half_mask = jnp.concatenate([low_half.astype(F32)] * 2, axis=1) > 0.5

    def half(a, b):
        return jnp.where(half_mask, a, b)

    up_mask = mask("up", False)
    gate24 = mask("gate24")
    ok_low, ok_high, far_low, far_high = mask("low"), mask("high"), mask("far_low"), mask("far_high")
    own_mask = mask("own", False)
    gate16, ok16 = mask("gate16"), mask("ok16")
    size = HEIGHT * 16
    part = HALF * 16
    zero = jnp.zeros((8, WIDE), F32)
    s_ref[:, :, 0:16, :] = jnp.zeros((BLOCKS, 3, 16, WIDE), BF16)
    s_ref[:, :, 27 * 16 :, :] = jnp.zeros((BLOCKS, 3, 16, WIDE), BF16)

    def prepare(b):
        lanes = slice(b * WIDE, (b + 1) * WIDE)
        turn = b % 2
        held = {}

        def first():
            held["total"] = dot(x_ref[...], wf_ref[:, lanes])

        def keep():
            total = jnp.maximum(held.pop("total") + bs_ref[0:1, lanes], 0.0)
            f_ref[turn] = total.astype(BF16).reshape(HEIGHT, MATES, WIDE)

        def latents():
            packed = f_ref[turn, :, 0:32, :].reshape(HEIGHT * 32, WIDE)
            held["latent"] = dot(packed, dn_ref[0:WIDE, :]).reshape(HEIGHT, 32, LANES)

        def ups():
            latent = held.pop("latent")
            given = jnp.concatenate([latent[:, 0:24], pick_ref[b], latent[:, 24:32]], axis=1)
            both = jnp.concatenate([jnp.where(up_mask, given, 0.0), jnp.where(up_mask, 0.0, given)], axis=2)
            both = both.reshape(HEIGHT * 40, WIDE).astype(BF16)
            held["added"] = dot(both, un_ref[0:WIDE, :]).reshape(HEIGHT, 40, WIDE)

        def mate(y):
            here = f_ref[turn, y].astype(F32)
            add = held["added"][y]
            own = own_ref[y, :, lanes] + jnp.where(gate24, add[0:24], 0.0)
            turned = [swap(own[8 * j : 8 * j + 8]) for j in range(3)]
            center = jnp.concatenate([half(turned[0], turned[1]), half(turned[1], turned[2])], axis=0)
            top = (y + 1) * 16
            s_ref[b, 0, top : top + 16, :] = own[0:16].astype(BF16)
            s_ref[b, 1, top : top + 16, :] = center.astype(BF16)
            s_ref[b, 2, top : top + 16, :] = own[8:24].astype(BF16)
            middle = half(here[8:16], jnp.where(late, here[16:24], here[0:8]))
            middle = middle + add[24:32]
            far = add[32:40]
            lower = jnp.where(ok_low, here[32:40] + jnp.where(far_low, far, 0.0), 0.0)
            upper = jnp.where(ok_high, here[40:48] + jnp.where(far_high, far, 0.0), 0.0)
            return lower, middle, upper

        def put(r, top, bottom):
            for dt in range(3):
                t_ref[b, dt, r * 16 : (r + 1) * 16, :] = jnp.concatenate([top[dt], bottom[dt]], axis=0).astype(BF16)

        def rows(y):
            nothing = (zero, zero, zero)
            top, bottom = mate(y), mate(y + HALF)
            put(y + 1, top, bottom)
            if y == 0:
                put(HALF + 1, bottom, nothing)
            if y == HALF - 1:
                put(0, nothing, top)

        return [first, keep, latents, ups], [functools.partial(rows, y) for y in range(HALF)]

    def convolve_part(b, held, name):
        ref, rows = (t_ref, part) if name == "mates" else (s_ref, size)

        def step(tap):
            dt, dr = divmod(tap, 3)
            held[name] = held.get(name, jnp.zeros((rows, WIDE), F32)) + dot(
                ref[b, dt, dr * 16 : dr * 16 + rows, :], w2_ref[tap * WIDE : (tap + 1) * WIDE, :]
            )

        return [functools.partial(step, tap) for tap in range(9)]

    def convolve(b, held):
        def step(tap):
            dt, dr = divmod(tap, 3)
            lhs = jnp.concatenate(
                [s_ref[b, dt, dr * 16 : dr * 16 + size, :], t_ref[b, dt, dr * 16 : dr * 16 + part, :]], axis=0
            )
            held["acc"] = held.get("acc", jnp.zeros((size + part, WIDE), F32)) + dot(
                lhs, w2_ref[tap * WIDE : (tap + 1) * WIDE, :]
            )

        return [functools.partial(step, tap) for tap in range(9)]

    def conclude(b, held):
        bias2 = bs_ref[1:2, b * WIDE : (b + 1) * WIDE]

        def begin():
            if "acc" in held:
                acc = held.pop("acc")
                held["own"], held["mates"] = acc[:size], acc[size:]
            mates = jnp.maximum(held.pop("mates") + bias2, 0.0) + t_ref[b, 1, 16 : 16 + part, :].astype(F32)
            held["latent"] = dot(mates.astype(BF16), dn_ref[WIDE:, :]).reshape(HALF, 16, LANES)

        def ups():
            latent = held.pop("latent")
            both = jnp.concatenate([jnp.where(own_mask, latent, 0.0), jnp.where(own_mask, 0.0, latent)], axis=2)
            held["added"] = dot(both.reshape(part, WIDE).astype(BF16), un_ref[WIDE:, :]).reshape(HALF, 16, WIDE)

        def row(y):
            at = (y // HALF) * 8
            add = held["added"][y % HALF, at : at + 8]
            add = jnp.concatenate([swap(add), add], axis=0)
            second = jnp.maximum(held["own"][y * 16 : y * 16 + 16] + bias2, 0.0)
            second = rounded(second + s_ref[b, 1, (y + 1) * 16 : (y + 2) * 16, :].astype(F32))
            two = second + jnp.where(gate16, add, 0.0)
            c2_ref[b, y] = jnp.where(ok16, two, 0.0)

        return [begin, ups] + [functools.partial(row, y) for y in range(HEIGHT)]

    def weave(*streams):
        order = []
        for s, stream in enumerate(streams):
            order += [((i + 0.5) / len(stream), s, i) for i in range(len(stream))]
        for _, s, i in sorted(order):
            streams[s][i]()

    lane = iota((16, LANES), 1)
    left, right = lane < CHANS, lane >= LANES - CHANS

    def spread_rows(pair):
        width = 2 * WIDE
        keep = iota((8, width), 0) < 4
        nothing = (jnp.zeros((8, width), F32),) * 3

        def filled(y):
            tiles = []
            for b in (2 * pair, 2 * pair + 1):
                old = pltpu.roll(c2_ref[b - 1, y, :, LANES:], 64, 1) if b else jnp.zeros((16, LANES), F32)
                tiles.append(jnp.where(left, old, c2_ref[b, y, :, :LANES]))
                old = pltpu.roll(c2_ref[b + 1, y, :, :LANES], 64, 1) if b + 1 < BLOCKS else jnp.zeros((16, LANES), F32)
                tiles.append(jnp.where(right, old, c2_ref[b, y, :, LANES:]))
            whole = jnp.concatenate(tiles, axis=1)
            low, high = whole[0:8], whole[8:16]
            return low, jnp.where(keep, swap(low), swap(high)), high

        def store(r, top, bottom):
            for dt in range(3):
                s3_ref[dt, r * 16 : (r + 1) * 16, pair * width : (pair + 1) * width] = jnp.concatenate(
                    [top[dt], bottom[dt]], axis=0
                ).astype(BF16)

        def step(y):
            top, bottom = filled(y), filled(y + HALF)
            store(y + 1, top, bottom)
            if y == 0:
                store(HALF + 1, bottom, nothing)
            if y == HALF - 1:
                store(0, nothing, top)

        return [functools.partial(step, y) for y in range(HALF)]

    def last_layer(pair, held):
        def step(tap):
            dt, dr = divmod(tap, 3)
            lhs = jnp.concatenate(
                [
                    s3_ref[dt, dr * 16 : dr * 16 + part, b * WIDE : (b + 1) * WIDE]
                    for b in (2 * pair, 2 * pair + 1)
                ],
                axis=0,
            )
            held["acc"] = held.get("acc", jnp.zeros((2 * part, WIDE), F32)) + dot(
                lhs, w3_ref[tap * WIDE : (tap + 1) * WIDE, :]
            )

        return [functools.partial(step, tap) for tap in range(9)]

    logits = []

    def readout(pair, held):
        def step(i):
            b = 2 * pair + i
            lanes = slice(b * WIDE, (b + 1) * WIDE)
            third = jnp.maximum(held["acc"][i * part : (i + 1) * part] + bs_ref[2:3, lanes], 0.0)
            third = third + s3_ref[1, 16 : 16 + part, lanes].astype(F32)
            high = third.astype(BF16)
            rest = (third - high.astype(F32)).astype(BF16)
            sums = dot(jnp.concatenate([high, rest], axis=0), rd_ref[lanes, :])
            logits.append(sums[:part] + sums[part:])

        return [functools.partial(step, i) for i in range(2)]

    plans = [prepare(b) for b in range(BLOCKS)]
    helds = [{} for _ in range(BLOCKS)]
    weave(plans[0][0])
    weave(plans[0][1], plans[1][0])
    for b in range(BLOCKS - 1):
        streams = [convolve(b, helds[b])]
        if b:
            streams.append(conclude(b - 1, helds[b - 1]))
        streams.append(plans[b + 1][1])
        if b + 2 < BLOCKS:
            streams.append(plans[b + 2][0])
        weave(*streams)
    final = BLOCKS - 1
    weave(convolve_part(final, helds[final], "mates"), conclude(final - 1, helds[final - 1]))
    ends = conclude(final, helds[final])
    weave(convolve_part(final, helds[final], "own"), ends[:2], spread_rows(0))
    thirds = [{}, {}]
    places = spread_rows(1)
    rest = []
    for y in range(HALF):
        rest += [ends[2 + y], ends[2 + y + HALF], places[y]]
    weave(last_layer(0, thirds[0]), rest)
    weave(last_layer(1, thirds[1]), readout(0, thirds[0]))
    weave(readout(1, thirds[1]))
    finish(sum(logits[1:], logits[0]).reshape(HALF, 16, LANES), cell_ref, out_ref)


def finish(logits, cell_ref, out_ref):
    lane8 = iota((8, LANES), 1)
    flat = [jnp.zeros((8, LANES), F32) for _ in range(FLAT // LANES)]
    for y in range(HEIGHT):
        row = logits[y % HALF, (y // HALF) * 8 : (y // HALF) * 8 + 8]
        begin = y * WIDTH
        turned = pltpu.roll(row, begin % LANES, 1) if begin % LANES else row
        for dst in range(FLAT // LANES):
            a = max(begin, dst * LANES) - dst * LANES
            e = min(begin + WIDTH, (dst + 1) * LANES) - dst * LANES
            if a < e:
                flat[dst] = jnp.where((lane8 >= a) & (lane8 < e), turned, flat[dst])
    flat = jnp.concatenate(flat, axis=1)[:, : HEIGHT * WIDTH] + cell_ref[...]
    for j in range(DEPTH):
        for p in range(COUNT):
            out_ref[p, j : j + 1, :] = flat[4 * j + p : 4 * j + p + 1, :]


def in_hbm(x):
    return pltpu.with_memory_space_constraint(x, pltpu.HBM)


def swapped(block, axis, mask):
    count = lax.axis_size(axis)
    return lax.ppermute(block, axis, [(i, i ^ mask) for i in range(count)])


def shifted(block, axis, offset):
    count = lax.axis_size(axis)
    return lax.ppermute(block, axis, [(i, i - offset) for i in range(count) if 0 <= i - offset < count])


def shards(
    bits, partners, gate_round, first_kernel, second_kernels, conv_bias, couple_down, couple_up, head, cell_bias
):
    devices, steps = lax.axis_size("patch"), lax.axis_size("tm")
    latent = couple_down.shape[-1]
    total = BLOCKS * WIDE
    vmem = pl.BlockSpec(memory_space=pltpu.VMEM)
    hbm = pl.BlockSpec(memory_space=pltpu.HBM)
    mine = pl.pallas_call(
        pack_kernel,
        out_shape=jax.ShapeDtypeStruct((8, FLAT + LANES), BF16),
        in_specs=[hbm, hbm, pl.BlockSpec(memory_space=pltpu.SMEM)],
        out_specs=vmem,
        scratch_shapes=[
            pltpu.VMEM((COUNT, DEPTH, WIDTH, HEIGHT), jnp.int32),
            pltpu.VMEM(partners.shape, jnp.int32),
            pltpu.SemaphoreType.DMA((2,)),
        ],
        compiler_params=pltpu.CompilerParams(vmem_limit_bytes=2 << 20),
        name="pack",
    )(in_hbm(jnp.swapaxes(bits, 2, 3)), in_hbm(partners), gate_round)

    exact = steps == 4 and devices > 1
    if exact:
        blocks = [mine] + [
            lax.ppermute(mine, "tm", [(i, i ^ k if abs(i - (i ^ k)) <= 2 else i) for i in range(steps)])
            for k in (1, 2, 3)
        ]
    else:
        blocks = [mine] + [shifted(mine, "tm", k) for k in (1, -1, 2, -2)]
    near = jnp.concatenate(blocks, axis=0)
    params = (
        first_kernel,
        second_kernels.reshape(54 * CHANS, CHANS),
        conv_bias,
        jnp.swapaxes(couple_down, 1, 2),
        couple_up,
        head.reshape(1, CHANS),
    )
    weights = pl.pallas_call(
        weights_kernel,
        out_shape=[
            jax.ShapeDtypeStruct((WIDE, total), BF16),
            jax.ShapeDtypeStruct((9 * WIDE, WIDE), BF16),
            jax.ShapeDtypeStruct((9 * WIDE, WIDE), BF16),
            jax.ShapeDtypeStruct((2 * WIDE, SLOTS * latent), BF16),
            jax.ShapeDtypeStruct((4 * SLOTS * latent, WIDE), BF16),
            jax.ShapeDtypeStruct((total, LANES), BF16),
            jax.ShapeDtypeStruct((8, total), F32),
        ],
        in_specs=[hbm] * 6,
        out_specs=[vmem] * 7,
        scratch_shapes=[pltpu.VMEM((WIDE, total), F32)]
        + [pltpu.VMEM(x.shape, x.dtype) for x in params]
        + [pltpu.SemaphoreType.DMA((6,))],
        cost_estimate=pl.CostEstimate(flops=10**9, bytes_accessed=10**7, transcendentals=0),
        compiler_params=pltpu.CompilerParams(vmem_limit_bytes=12 << 20),
        name="weights",
    )(*map(in_hbm, params))

    every = near[:, :FLAT]
    parts = [every] + [swapped(every, "patch", 2 * m) for m in range(1, devices // 2)]
    every = jnp.concatenate(parts, axis=0)
    every, weights = lax.optimization_barrier((every, weights))
    others = swapped(every, "patch", 1)

    if exact:
        wf, w2, w3, dn, un, rd, bs = weights
        early = pl.pallas_call(
            functools.partial(early_kernel, (devices, steps)),
            out_shape=[
                jax.ShapeDtypeStruct((HEIGHT, OWN, total), F32),
                jax.ShapeDtypeStruct((BLOCKS, HEIGHT, 8, LANES), F32),
                jax.ShapeDtypeStruct((3 * MATES, 8 * steps * devices), BF16),
                jax.ShapeDtypeStruct((MASK_ROWS, LANES), F32),
            ],
            in_specs=[vmem] * 4,
            out_specs=[vmem] * 4,
            scratch_shapes=[pltpu.VMEM((HEIGHT * OWN, WIDE), BF16), pltpu.VMEM((8, LANES), F32)],
            cost_estimate=pl.CostEstimate(flops=10**9, bytes_accessed=10**7, transcendentals=0),
            compiler_params=pltpu.CompilerParams(vmem_limit_bytes=14 << 20),
            name="early",
        )(near, wf, dn, bs)
        return pl.pallas_call(
            late_kernel,
            out_shape=jax.ShapeDtypeStruct((COUNT, DEPTH, HEIGHT * WIDTH), F32),
            in_specs=[vmem] * 14,
            out_specs=vmem,
            scratch_shapes=[
                pltpu.VMEM((HEIGHT * MATES, WIDE), BF16),
                pltpu.VMEM((2, HEIGHT, MATES, WIDE), BF16),
                pltpu.VMEM((BLOCKS, 3, 28 * 16, WIDE), BF16),
                pltpu.VMEM((BLOCKS, 3, (HALF + 2) * 16, WIDE), BF16),
                pltpu.VMEM((BLOCKS, HEIGHT, 16, WIDE), F32),
                pltpu.VMEM((3, (HALF + 2) * 16, total), BF16),
            ],
            compiler_params=pltpu.CompilerParams(vmem_limit_bytes=36 << 20),
            name="late",
        )(every, others, *early, wf, w2, w3, dn, un, rd, bs, cell_bias.reshape(1, HEIGHT * WIDTH))
    return pl.pallas_call(
        functools.partial(main_kernel, (devices, steps, exact)),
        out_shape=jax.ShapeDtypeStruct((COUNT, DEPTH, HEIGHT * WIDTH), F32),
        in_specs=[vmem] * 11,
        out_specs=vmem,
        scratch_shapes=[
            pltpu.VMEM((HEIGHT * UNITS, WIDE), BF16),
            pltpu.VMEM((HEIGHT, UNITS, WIDE), F32),
            pltpu.VMEM((3, 28 * 32, WIDE), BF16),
            pltpu.VMEM((BLOCKS, HEIGHT, 16, WIDE), F32),
            pltpu.VMEM((3, (HALF + 2) * 16, total), BF16),
        ],
        compiler_params=pltpu.CompilerParams(vmem_limit_bytes=40 << 20),
        name="decode",
    )(every, others, near, *weights, cell_bias.reshape(1, HEIGHT * WIDTH))


def solution(mesh):
    in_specs = (
        P("patch", "tm", None, None),
        P("tm", None),
        P("tm"),
        P(),
        P(),
        P(),
        P(),
        P(),
        P(),
        P(),
    )
    out_specs = P("patch", "tm", None)
    return jax.shard_map(shards, mesh=mesh, in_specs=in_specs, out_specs=out_specs, check_vma=False)
```

```python
import functools

import jax
import jax.numpy as jnp
from jax import lax
from jax.experimental import pallas as pl
from jax.experimental.pallas import tpu as pltpu
from jax.sharding import PartitionSpec as P


F32 = jnp.float32
BF16 = jnp.bfloat16
LANES = 128
COUNT = 4
DEPTH = 2
HEIGHT = 26
WIDTH = 24
CHANS = 32
WINDOW = 6
SLOTS = 8
BLOCKS = WIDTH // WINDOW
WIDE = SLOTS * CHANS
FLAT = 640
OWN, UNITS = 24, 96
HALF = HEIGHT // 2


def iota(shape, dim):
    return lax.broadcasted_iota(jnp.int32, shape, dim)


def rounded(x):
    return x.astype(BF16).astype(F32)


def dot(a, b):
    return jnp.dot(a, b, preferred_element_type=F32)


def fetch(pairs, sems):
    copies = [pltpu.make_async_copy(src, dst, sems.at[i]) for i, (src, dst) in enumerate(pairs)]
    for copy in copies:
        copy.start()
    for copy in copies:
        copy.wait()


def pack_kernel(bits_hbm, partners_hbm, gate_ref, out_ref, bits_ref, partners_ref, sems):
    fetch(((bits_hbm, bits_ref), (partners_hbm, partners_ref)), sems)
    units = COUNT * DEPTH
    bits = bits_ref[...].reshape(units, WIDTH, HEIGHT).astype(F32)
    bits = jnp.swapaxes(bits, 1, 2)
    rows = [bits[:, y, :] for y in range(HEIGHT)]
    flat = jnp.concatenate(rows + [jnp.zeros((units, FLAT - HEIGHT * WIDTH), F32)], axis=1)
    out_ref[:, :FLAT] = flat.astype(BF16)
    patches = partners_ref.shape[1]
    names = partners_ref[...].astype(F32)
    if patches < LANES:
        names = jnp.concatenate([names, jnp.full((1, LANES - patches), -1.0, F32)], axis=1)
    moment = jnp.full((1, LANES), gate_ref[0], jnp.int32).astype(F32)
    sub = iota((units, LANES), 0)
    out_ref[:, FLAT:] = jnp.where(sub == 0, names, jnp.where(sub == 1, moment, 0.0)).astype(BF16)


def weights_kernel(
    first_hbm, second_hbm, bias_hbm, down_hbm, up_hbm, head_hbm,
    wf_ref, w2_ref, w3_ref, dn_ref, un_ref, rd_ref, bs_ref,
    scr_ref, first_ref, second_ref, bias_ref, down_ref, up_ref, head_ref, sems,
):
    sources = (first_hbm, second_hbm, bias_hbm, down_hbm, up_hbm, head_hbm)
    fetch(zip(sources, (first_ref, second_ref, bias_ref, down_ref, up_ref, head_ref)), sems)
    total = BLOCKS * WIDE
    spread = (iota((CHANS, WIDE), 1) % CHANS == iota((CHANS, WIDE), 0)).astype(BF16)
    slot = iota((CHANS, WIDE), 1) // CHANS
    inner = (slot >= 1) & (slot <= WINDOW)
    for layer, w_ref in enumerate((w2_ref, w3_ref)):
        for tap in range(9):
            base = (layer * 27 + tap * 3) * CHANS
            tiled = dot(second_ref[base : base + 3 * CHANS, :], spread)
            for kc in range(SLOTS):
                block = jnp.zeros((CHANS, WIDE), F32)
                for dc in range(3):
                    block = jnp.where(
                        inner & (slot == kc - dc + 1), tiled[dc * CHANS : (dc + 1) * CHANS], block
                    )
                w_ref[tap * WIDE + kc * CHANS : tap * WIDE + (kc + 1) * CHANS, :] = block.astype(BF16)
    across = (iota((CHANS, total), 1) % CHANS == iota((CHANS, total), 0)).astype(BF16)
    for pair in range(9):
        scr_ref[8 * pair : 8 * pair + 3, :CHANS] = first_ref[pair // 3, pair % 3].astype(F32)
    taps = dot(scr_ref[0:72, :CHANS].astype(BF16), across)
    lane = iota((WIDTH, total), 1)
    column = (lane // WIDE) * WINDOW - 1 + (lane % WIDE) // CHANS
    real = (column >= 0) & (column < WIDTH)
    offset = iota((WIDTH, total), 0) - column + 1
    for pair in range(9):
        block = jnp.zeros((WIDTH, total), F32)
        for dc in range(3):
            block = jnp.where(real & (offset == dc), taps[pair * 8 + dc : pair * 8 + dc + 1, :], block)
        scr_ref[pair * WIDTH : (pair + 1) * WIDTH, :] = block
    scr_ref[9 * WIDTH :, :] = jnp.zeros((WIDE - 9 * WIDTH, total), F32)
    wf_ref[...] = scr_ref[...].astype(BF16)
    latent = down_ref.shape[1]
    low = SLOTS * latent
    thin = (iota((latent, low), 1) % latent == iota((latent, low), 0)).astype(BF16)
    for layer in range(2):
        tiled = lax.dot_general(
            down_ref[layer], thin, (((0,), (0,)), ((), ())), preferred_element_type=F32
        )
        for kc in range(SLOTS):
            keep = iota((CHANS, low), 1) // latent == kc
            dn_ref[layer * WIDE + kc * CHANS : layer * WIDE + (kc + 1) * CHANS, :] = jnp.where(
                keep, tiled, 0.0
            ).astype(BF16)
        for role in range(2):
            tiled = dot(up_ref[layer, role], spread)
            for kc in range(SLOTS):
                keep = iota((latent, WIDE), 1) // CHANS == kc
                top = (layer * 2 + role) * low + kc * latent
                un_ref[top : top + latent, :] = jnp.where(keep, tiled, 0.0).astype(BF16)
    row = iota((total, CHANS), 0)
    chosen = jnp.where(row % CHANS == iota((total, CHANS), 1), head_ref[...].astype(F32), 0.0)
    values = dot(chosen.astype(BF16), jnp.ones((CHANS, LANES), BF16))
    row = iota((total, LANES), 0)
    place = (row % WIDE) // CHANS
    target = (row // WIDE) * WINDOW - 1 + place
    keep = (place >= 1) & (place <= WINDOW) & (target == iota((total, LANES), 1))
    rd_ref[...] = jnp.where(keep, values, 0.0).astype(BF16)
    scr_ref[0:8, :CHANS] = jnp.zeros((8, CHANS), F32)
    scr_ref[0:3, :CHANS] = bias_ref[...]
    biases = jnp.dot(
        scr_ref[0:8, :CHANS], across.astype(F32), preferred_element_type=F32, precision=lax.Precision.HIGHEST
    )
    lane = iota((8, total), 1)
    place = (lane % WIDE) // CHANS
    column = (lane // WIDE) * WINDOW - 1 + place
    real = (column >= 0) & (column < WIDTH)
    inside = (place >= 1) & (place <= WINDOW)
    top = iota((8, total), 0) == 0
    keep = (top & real) | (~top & inside)
    bs_ref[...] = jnp.where(keep, biases, 0.0)


def window_rows(gathered, y, lane):
    start = WIDTH * (y - 1)
    length = 3 * WIDTH
    tiles = [None, None]
    for dt in range(3):
        begin = length * dt
        shift = begin - start
        for src in range(FLAT // LANES):
            lo = max(start, 0, src * LANES)
            hi = min(start + length, FLAT, (src + 1) * LANES)
            if lo >= hi:
                continue
            source = gathered[dt][:, src * LANES : (src + 1) * LANES]
            turned = pltpu.roll(source, shift % LANES, 1) if shift % LANES else source
            for dst in range(2):
                a = max(lo + shift, dst * LANES) - dst * LANES
                b = min(hi + shift, (dst + 1) * LANES) - dst * LANES
                if a >= b:
                    continue
                old = jnp.zeros_like(turned) if tiles[dst] is None else tiles[dst]
                tiles[dst] = jnp.where((lane >= a) & (lane < b), turned, old)
    return tiles


def main_kernel(
    sizes, here_ref, there_ref, meta_ref, wf_ref, w2_ref, w3_ref, dn_ref, un_ref, rd_ref, bs_ref, cell_ref,
    out_ref, x_ref, f_ref, s_ref, c2_ref, s3_ref,
):
    devices, steps, exact = sizes
    near = meta_ref.shape[0] // 8
    me = lax.axis_index("patch")
    now = lax.axis_index("tm")
    sub = iota((8, LANES), 0)
    low_half = sub < 4

    names, moments = gate_layers(meta_ref, now, steps, exact)
    first_round = 2 * now - 2
    own_patch = COUNT * me + sub % COUNT

    def pair(parts):
        return jnp.concatenate(
            [jnp.where(low_half, parts[0], parts[1]), jnp.where(low_half, parts[1], parts[2])], axis=0
        )

    hot = [(jnp.broadcast_to(names[j], (8, LANES)) == own_patch).astype(F32) for j in range(3)]
    hot24 = jnp.concatenate(hot, axis=0).astype(BF16)
    hot16f = pair(hot)
    hot16 = hot16f.astype(BF16)
    square = iota((LANES, LANES), 0)
    even = moments[1] == 2 * now
    other = jnp.where(even[0:1, :], names[0], names[2])
    perm_one = (square == names[1]).astype(BF16)
    perm_other = (square == other).astype(BF16)
    middle = (iota((16, LANES), 0) >= 4) & (iota((16, LANES), 0) < 12)
    hot_far = jnp.where(middle, dot(hot16, perm_other), dot(hot16, perm_one))
    hots = jnp.concatenate([hot24, hot_far.astype(BF16), hot16], axis=0)
    index = dot(hots, square.astype(F32).astype(BF16)).astype(jnp.int32)
    mate24, far16, mate16 = index[0:24], index[24:40], index[40:56]
    own24 = jnp.concatenate([own_patch] * 3, axis=0)
    own16 = jnp.concatenate([own_patch] * 2, axis=0)

    moment24 = jnp.concatenate(moments, axis=0)
    moment16 = pair(moments)
    round24 = first_round + iota((24, LANES), 0) // 4
    round16 = first_round + 1 + iota((16, LANES), 0) // 4
    last = DEPTH * steps - 1
    step_far = pair([jnp.full((8, LANES), 1, jnp.int32), jnp.where(even, -1, 1), jnp.full((8, LANES), -1, jnp.int32)])
    moment_far = pair([moments[1], jnp.where(even, moments[0], moments[2]), moments[1]])
    touches = moment_far == moment16 + step_far
    far_low = touches & (step_far < 0)
    far_high = touches & (step_far > 0)

    columns = 2 * here_ref.shape[0]
    events = jnp.concatenate([here_ref[...], there_ref[...]], axis=0)
    col = iota((1, columns), 1)
    block = col // (8 * near)
    half = devices // 2
    source = me ^ (2 * (block % half) + block // half) if devices > 1 else me + 0 * block
    patch_of = COUNT * source + (col % 8) // DEPTH
    step = (col // 8) % near
    if exact:
        time_of = now ^ step
    else:
        time_of = now + jnp.where(step == 1, 1, jnp.where(step == 2, -1, jnp.where(step == 3, 2, jnp.where(step == 4, -2, 0))))
    round_of = DEPTH * time_of + col % DEPTH
    expand = (iota((LANES, columns), 0) == patch_of).astype(BF16)
    spread = dot(hots, expand)

    def lanes_of(x):
        return jnp.broadcast_to(x[:, :1], (x.shape[0], columns))

    is_own = (patch_of == lanes_of(own24)).astype(F32)
    patch_sel = jnp.concatenate(
        [is_own, spread[0:24], spread[24:40], spread[40:56], spread[40:56]], axis=0
    )
    want = jnp.concatenate(
        [
            lanes_of(round24),
            lanes_of(moment24),
            lanes_of(moment16 + step_far),
            lanes_of(moment16 - 1),
            lanes_of(moment16 + 1),
        ],
        axis=0,
    )
    gathered = []
    for dt in range(3):
        choose = jnp.where(round_of == want + (dt - 1), patch_sel, 0.0).astype(BF16)
        gathered.append(dot(choose, events))
    lane = iota((UNITS, LANES), 1)
    for y in range(HEIGHT):
        tiles = window_rows(gathered, y, lane)
        x_ref[y * UNITS : (y + 1) * UNITS, :] = jnp.concatenate(tiles, axis=1).astype(BF16)

    s_ref[:, 0:32, :] = jnp.zeros((3, 32, WIDE), BF16)
    s_ref[:, 27 * 32 :, :] = jnp.zeros((3, 32, WIDE), BF16)

    def wide(mask):
        return jnp.concatenate([mask.astype(jnp.int32)] * 2, axis=1) != 0

    ctrl_up = jnp.concatenate([mate24 - own24, own16 - mate16, far16 - mate16], axis=0) > 0
    gate24 = wide(round24 == moment24)
    gate16 = wide(round16 == moment16)
    ok24 = wide((round24 >= 0) & (round24 <= last))
    ok16 = wide((round16 >= 0) & (round16 <= last))
    ok_low = wide((moment16 - 1 >= 0) & (moment16 - 1 <= last))
    ok_high = wide((moment16 + 1 >= 0) & (moment16 + 1 <= last))
    far_low, far_high = wide(far_low), wide(far_high)
    ctrl_own16 = own16 < mate16
    at_moment = round24 == moment24

    def swap(x):
        return pltpu.roll(x, 4, 0)

    def body(b, carry):
        lanes = pl.ds(pl.multiple_of(b * WIDE, WIDE), WIDE)
        bias1 = bs_ref[0:1, lanes]
        bias2 = bs_ref[1:2, lanes]
        total = dot(x_ref[...], wf_ref[:, lanes])
        f_ref[...] = rounded(jnp.maximum(total + bias1, 0.0)).reshape(HEIGHT, UNITS, WIDE)
        packed = f_ref[:, 0:64, :].reshape(HEIGHT * 64, WIDE).astype(BF16)
        latent = rounded(dot(packed, dn_ref[0:WIDE, :])).reshape(HEIGHT, 64, LANES)
        rows = []
        for y in range(HEIGHT):
            lat = latent[y]
            mine = [lat[8 * j : 8 * j + 8] for j in range(3)]
            mine = [jnp.where(at_moment[8 * j : 8 * j + 8], mine[j], swap(mine[j])) for j in range(3)]
            rows.append(jnp.concatenate([lat[24:48], pair(mine), lat[48:64]], axis=0))
        given = jnp.stack(rows, axis=0)
        both = jnp.concatenate(
            [jnp.where(ctrl_up, given, 0.0), jnp.where(ctrl_up, 0.0, given)], axis=2
        ).reshape(HEIGHT * 56, WIDE)
        added = dot(both.astype(BF16), un_ref[0:WIDE, :]).reshape(HEIGHT, 56, WIDE)
        half_mask = wide(low_half)
        for y in range(HEIGHT):
            here = f_ref[y]
            add = added[y]
            own = rounded(here[0:24] + jnp.where(gate24, add[0:24], 0.0))
            own = jnp.where(ok24, own, 0.0)
            m = [here[24 + 8 * j : 32 + 8 * j] for j in range(3)]
            mid = jnp.concatenate(
                [jnp.where(half_mask, m[0], m[1]), jnp.where(half_mask, m[1], m[2])], axis=0
            )
            mid = rounded(mid + add[24:40])
            far = add[40:56]
            lower = jnp.where(ok_low, rounded(here[64:80] + jnp.where(far_low, far, 0.0)), 0.0)
            upper = jnp.where(ok_high, rounded(here[80:96] + jnp.where(far_high, far, 0.0)), 0.0)
            turned = [swap(own[8 * j : 8 * j + 8]) for j in range(3)]
            center = jnp.concatenate(
                [jnp.where(half_mask, turned[0], turned[1]), jnp.where(half_mask, turned[1], turned[2])], axis=0
            )
            top = (y + 1) * 32
            s_ref[0, top : top + 32, :] = jnp.concatenate([own[0:16], lower], axis=0).astype(BF16)
            s_ref[1, top : top + 32, :] = jnp.concatenate([center, mid], axis=0).astype(BF16)
            s_ref[2, top : top + 32, :] = jnp.concatenate([own[8:24], upper], axis=0).astype(BF16)
        size = HEIGHT * 32
        acc = jnp.zeros((size, WIDE), F32)
        for tap in range(9):
            dt, dr = divmod(tap, 3)
            acc = acc + dot(
                s_ref[dt, dr * 32 : dr * 32 + size, :], w2_ref[tap * WIDE : (tap + 1) * WIDE, :]
            )
        second = jnp.maximum(acc + bias2, 0.0) + s_ref[1, 32 : 32 + size, :].astype(F32)
        second = second.reshape(HEIGHT, 32, WIDE)
        mates = second[:, 16:32, :].reshape(HEIGHT * 16, WIDE).astype(BF16)
        latent = rounded(dot(mates, dn_ref[WIDE:, :])).reshape(HEIGHT, 16, LANES)
        both = jnp.concatenate(
            [jnp.where(ctrl_own16, latent, 0.0), jnp.where(ctrl_own16, 0.0, latent)], axis=2
        ).reshape(HEIGHT * 16, WIDE)
        added = dot(both.astype(BF16), un_ref[WIDE:, :]).reshape(HEIGHT, 16, WIDE)
        two = rounded(rounded(second[:, 0:16, :]) + jnp.where(gate16, added, 0.0))
        c2_ref[b] = jnp.where(ok16, two, 0.0)
        return carry

    lax.fori_loop(0, BLOCKS, body, 0)


    def placed(y, dt):
        if y < 0 or y >= HEIGHT:
            return jnp.zeros((8, BLOCKS * WIDE), F32)
        tiles = []
        for b in range(BLOCKS):
            for t in range(2):
                group = c2_ref[b, y, :, t * LANES : (t + 1) * LANES]
                if t == 0:
                    old = pltpu.roll(c2_ref[b - 1, y, :, LANES:], 64, 1) if b else jnp.zeros((16, LANES), F32)
                    group = jnp.where(iota((16, LANES), 1) < CHANS, old, group)
                else:
                    old = pltpu.roll(c2_ref[b + 1, y, :, :LANES], 64, 1) if b + 1 < BLOCKS else jnp.zeros((16, LANES), F32)
                    group = jnp.where(iota((16, LANES), 1) >= LANES - CHANS, old, group)
                if dt == 0:
                    group = group[0:8]
                elif dt == 2:
                    group = group[8:16]
                else:
                    group = jnp.where(low_half, swap(group[0:8]), swap(group[8:16]))
                tiles.append(group)
        return jnp.concatenate(tiles, axis=1)

    for dt in range(3):
        for r in range(HALF + 2):
            s3_ref[dt, r * 16 : (r + 1) * 16, :] = jnp.concatenate(
                [placed(r - 1, dt), placed(r + HALF - 1, dt)], axis=0
            ).astype(BF16)

    size = HALF * 16
    logits = jnp.zeros((size, LANES), F32)
    for b in range(BLOCKS):
        lanes = slice(b * WIDE, (b + 1) * WIDE)
        acc = jnp.zeros((size, WIDE), F32)
        for tap in range(9):
            dt, dr = divmod(tap, 3)
            acc = acc + dot(
                s3_ref[dt, dr * 16 : dr * 16 + size, lanes], w3_ref[tap * WIDE : (tap + 1) * WIDE, :]
            )
        third = jnp.maximum(acc + bs_ref[2:3, lanes], 0.0) + s3_ref[1, 16 : 16 + size, lanes].astype(F32)
        high = third.astype(BF16)
        rest = (third - high.astype(F32)).astype(BF16)
        logits = logits + dot(high, rd_ref[lanes, :]) + dot(rest, rd_ref[lanes, :])
    finish(logits.reshape(HALF, 16, LANES), cell_ref, out_ref)


def gate_layers(near_ref, now, steps, exact):
    names, moments = [], []
    for j in range(3):
        there = now - 1 + j
        valid = (there >= 0) & (there < steps)
        safe = jnp.clip(there, 0, steps - 1)
        block = (safe ^ now) if exact else (2, 0, 1)[j]
        tile = near_ref[pl.ds(pl.multiple_of(block * 8, 8), 8), FLAT:].astype(F32).astype(jnp.int32)
        names.append(jnp.where(valid, tile[0:1, :], -1))
        moments.append(jnp.broadcast_to(jnp.where(valid, tile[1:2, :], -1000), (8, LANES)))
    return names, moments


def event_rows(gathered, x_ref, units):
    lane = iota((units, LANES), 1)
    for y in range(HEIGHT):
        tiles = window_rows(gathered, y, lane)
        x_ref[y * units : (y + 1) * units, :] = jnp.concatenate(tiles, axis=1).astype(BF16)


MASKS = (("up", 40), ("gate24", 24), ("ok24", 24), ("low", 8), ("high", 8), ("far_low", 8), ("far_high", 8), ("own", 16), ("gate16", 16), ("ok16", 16))
MASK_AT = {}
MASK_ROWS = 0
for _name, _rows in MASKS:
    MASK_AT[_name] = (MASK_ROWS, _rows)
    MASK_ROWS += _rows
MATES = 48


def early_kernel(
    sizes, near_ref, wf_ref, dn_ref, bs_ref, own_ref, pick_ref, choose_ref, mask_ref, x_ref, f_ref
):
    devices, steps = sizes
    near = steps
    me = lax.axis_index("patch")
    now = lax.axis_index("tm")
    sub = iota((8, LANES), 0)
    low_half = sub < 4
    names, moments = gate_layers(near_ref, now, steps, True)
    late = now < steps // 2
    first_round = 2 * now - 2
    last = DEPTH * steps - 1
    own8 = COUNT * me + sub % COUNT
    name_x = jnp.where(late, names[2], names[0])
    moment_x = jnp.where(late, moments[2], moments[0])

    def half(a, b):
        return jnp.where(low_half, a, b)

    def hot(name):
        return (jnp.broadcast_to(name, (8, LANES)) == own8).astype(F32)

    hots = [hot(name) for name in names]
    hot8 = half(hots[1], hot(name_x))
    moment8 = half(moments[1], moment_x)
    even = moments[1] == 2 * now
    other = jnp.where(even[0:1, :], names[0], names[2])
    square = iota((LANES, LANES), 0)
    wide_hot = jnp.concatenate([hot8, hot8], axis=0).astype(BF16)
    to_own = dot(wide_hot, (square == names[1]).astype(BF16))[0:8]
    to_other = dot(wide_hot, (square == other).astype(BF16))[0:8]
    hot_far = half(to_other, to_own)
    every = jnp.concatenate(hots + [hot_far, hot8, jnp.zeros((8, LANES), F32)], axis=0).astype(BF16)
    index = dot(every, square.astype(F32).astype(BF16)).astype(jnp.int32)
    mate24, far8, mate8 = index[0:24], index[24:32], index[32:40]
    own24 = jnp.concatenate([own8] * 3, axis=0)
    moment24 = jnp.concatenate(moments, axis=0)
    round24 = first_round + iota((24, LANES), 0) // 4
    round16 = first_round + 1 + iota((16, LANES), 0) // 4
    moment16 = jnp.concatenate([half(moments[0], moments[1]), half(moments[1], moments[2])], axis=0)
    step_far = half(jnp.where(even, -1, 1), jnp.where(late, -1, 1))
    moment_far = half(jnp.where(even, moments[0], moments[2]), moments[1])
    touches = (moment_far == moment8 + step_far).astype(F32)
    values = dict(
        up=jnp.concatenate([(own24 < mate24).astype(F32), (mate8 < own8).astype(F32), (mate8 < far8).astype(F32)], axis=0),
        gate24=(round24 == moment24).astype(F32),
        ok24=((round24 >= 0) & (round24 <= last)).astype(F32),
        low=((moment8 - 1 >= 0) & (moment8 - 1 <= last)).astype(F32),
        high=((moment8 + 1 >= 0) & (moment8 + 1 <= last)).astype(F32),
        far_low=jnp.where(step_far < 0, touches, 0.0),
        far_high=jnp.where(step_far > 0, touches, 0.0),
        own=jnp.concatenate([(own8 < mate8).astype(F32)] * 2, axis=0),
        gate16=(round16 == moment16).astype(F32),
        ok16=((round16 >= 0) & (round16 <= last)).astype(F32),
    )
    for name, (at, rows) in MASK_AT.items():
        mask_ref[at : at + rows, :] = values[name]

    columns = choose_ref.shape[1]
    col = iota((1, columns), 1)
    block = col // (8 * near)
    some = devices // 2
    source = me ^ (2 * (block % some) + block // some)
    patch_of = COUNT * source + (col % 8) // DEPTH
    round_of = DEPTH * (now ^ ((col // 8) % near)) + col % DEPTH
    spread = dot(every, (iota((LANES, columns), 0) == patch_of).astype(BF16))
    patch_sel = jnp.concatenate([spread[0:24], spread[24:32], spread[32:40], spread[32:40]], axis=0)

    def lanes_of(x):
        return jnp.broadcast_to(x[:, :1], (x.shape[0], columns))

    want = jnp.concatenate(
        [lanes_of(moment24), lanes_of(moment8 + step_far), lanes_of(moment8 - 1), lanes_of(moment8 + 1)], axis=0
    )
    for dt in range(3):
        choose = jnp.where(round_of == want + (dt - 1), patch_sel, 0.0)
        choose_ref[dt * MATES : (dt + 1) * MATES, :] = choose.astype(BF16)

    rows = near_ref.shape[0]
    col = iota((1, rows), 1)
    patch_of = (col % 8) // DEPTH
    round_of = DEPTH * (now ^ (col // 8)) + col % DEPTH
    unit = iota((24, rows), 0)
    gathered = []
    for dt in range(3):
        choose = (patch_of == unit % COUNT) & (round_of == first_round + unit // 4 + (dt - 1))
        gathered.append(dot(choose.astype(F32).astype(BF16), near_ref[:, :FLAT]))
    event_rows(gathered, x_ref, OWN)
    kept = jnp.concatenate([values["ok24"]] * 2, axis=1) > 0.5
    ahead = [moments[j] == round24[8 * j : 8 * j + 8] for j in range(3)]
    for b in range(BLOCKS):
        lanes = slice(b * WIDE, (b + 1) * WIDE)
        total = dot(x_ref[...], wf_ref[:, lanes])
        own = rounded(jnp.maximum(total + bs_ref[0:1, lanes], 0.0))
        own_ref[:, :, lanes] = jnp.where(kept, own.reshape(HEIGHT, OWN, WIDE), 0.0)
        latent = dot(own.astype(BF16), dn_ref[0:WIDE, :]).reshape(HEIGHT, OWN, LANES)
        for y in range(HEIGHT):
            mine = [latent[y, 8 * j : 8 * j + 8] for j in range(3)]
            mine = [jnp.where(ahead[j], mine[j], pltpu.roll(mine[j], 4, 0)) for j in range(3)]
            pick_ref[b, y] = half(mine[1], jnp.where(late, mine[2], mine[0]))


def late_kernel(
    here_ref, there_ref, own_ref, pick_ref, choose_ref, mask_ref, wf_ref, w2_ref, w3_ref, dn_ref, un_ref, rd_ref, bs_ref,
    cell_ref, out_ref, x_ref, f_ref, s_ref, t_ref, c2_ref, s3_ref,
):
    now = lax.axis_index("tm")
    steps = lax.axis_size("tm")
    late = now < steps // 2
    low_half = iota((8, LANES), 0) < 4

    def mask(name, wide=True):
        at, rows = MASK_AT[name]
        value = mask_ref[at : at + rows, :]
        return (jnp.concatenate([value] * 2, axis=1) if wide else value) > 0.5

    def swap(x):
        return pltpu.roll(x, 4, 0)

    events = jnp.concatenate([here_ref[...], there_ref[...]], axis=0)
    picked = dot(choose_ref[...], events)
    event_rows([picked[dt * MATES : (dt + 1) * MATES] for dt in range(3)], x_ref, MATES)

    half_mask = jnp.concatenate([low_half.astype(F32)] * 2, axis=1) > 0.5

    def half(a, b):
        return jnp.where(half_mask, a, b)

    up_mask = mask("up", False)
    gate24 = mask("gate24")
    ok_low, ok_high, far_low, far_high = mask("low"), mask("high"), mask("far_low"), mask("far_high")
    own_mask = mask("own", False)
    gate16, ok16 = mask("gate16"), mask("ok16")
    size = HEIGHT * 16
    part = HALF * 16
    zero = jnp.zeros((8, WIDE), F32)
    s_ref[:, :, 0:16, :] = jnp.zeros((BLOCKS, 3, 16, WIDE), BF16)
    s_ref[:, :, 27 * 16 :, :] = jnp.zeros((BLOCKS, 3, 16, WIDE), BF16)

    def prepare(b):
        lanes = slice(b * WIDE, (b + 1) * WIDE)
        turn = b % 2
        held = {}

        def first():
            held["total"] = dot(x_ref[...], wf_ref[:, lanes])

        def keep():
            total = jnp.maximum(held.pop("total") + bs_ref[0:1, lanes], 0.0)
            f_ref[turn] = total.astype(BF16).reshape(HEIGHT, MATES, WIDE)

        def latents():
            packed = f_ref[turn, :, 0:32, :].reshape(HEIGHT * 32, WIDE)
            held["latent"] = dot(packed, dn_ref[0:WIDE, :]).reshape(HEIGHT, 32, LANES)

        def ups():
            latent = held.pop("latent")
            given = jnp.concatenate([latent[:, 0:24], pick_ref[b], latent[:, 24:32]], axis=1)
            both = jnp.concatenate([jnp.where(up_mask, given, 0.0), jnp.where(up_mask, 0.0, given)], axis=2)
            both = both.reshape(HEIGHT * 40, WIDE).astype(BF16)
            held["added"] = dot(both, un_ref[0:WIDE, :]).reshape(HEIGHT, 40, WIDE)

        def mate(y):
            here = f_ref[turn, y].astype(F32)
            add = held["added"][y]
            own = own_ref[y, :, lanes] + jnp.where(gate24, add[0:24], 0.0)
            turned = [swap(own[8 * j : 8 * j + 8]) for j in range(3)]
            center = jnp.concatenate([half(turned[0], turned[1]), half(turned[1], turned[2])], axis=0)
            top = (y + 1) * 16
            s_ref[b, 0, top : top + 16, :] = own[0:16].astype(BF16)
            s_ref[b, 1, top : top + 16, :] = center.astype(BF16)
            s_ref[b, 2, top : top + 16, :] = own[8:24].astype(BF16)
            middle = half(here[8:16], jnp.where(late, here[16:24], here[0:8]))
            middle = middle + add[24:32]
            far = add[32:40]
            lower = jnp.where(ok_low, here[32:40] + jnp.where(far_low, far, 0.0), 0.0)
            upper = jnp.where(ok_high, here[40:48] + jnp.where(far_high, far, 0.0), 0.0)
            return lower, middle, upper

        def put(r, top, bottom):
            for dt in range(3):
                t_ref[b, dt, r * 16 : (r + 1) * 16, :] = jnp.concatenate([top[dt], bottom[dt]], axis=0).astype(BF16)

        def rows(y):
            nothing = (zero, zero, zero)
            top, bottom = mate(y), mate(y + HALF)
            put(y + 1, top, bottom)
            if y == 0:
                put(HALF + 1, bottom, nothing)
            if y == HALF - 1:
                put(0, nothing, top)

        return [first, keep, latents, ups], [functools.partial(rows, y) for y in range(HALF)]

    def convolve_part(b, held, name):
        ref, rows = (t_ref, part) if name == "mates" else (s_ref, size)

        def step(tap):
            dt, dr = divmod(tap, 3)
            held[name] = held.get(name, jnp.zeros((rows, WIDE), F32)) + dot(
                ref[b, dt, dr * 16 : dr * 16 + rows, :], w2_ref[tap * WIDE : (tap + 1) * WIDE, :]
            )

        return [functools.partial(step, tap) for tap in range(9)]

    def convolve(b, held):
        def step(tap):
            dt, dr = divmod(tap, 3)
            lhs = jnp.concatenate(
                [s_ref[b, dt, dr * 16 : dr * 16 + size, :], t_ref[b, dt, dr * 16 : dr * 16 + part, :]], axis=0
            )
            held["acc"] = held.get("acc", jnp.zeros((size + part, WIDE), F32)) + dot(
                lhs, w2_ref[tap * WIDE : (tap + 1) * WIDE, :]
            )

        return [functools.partial(step, tap) for tap in range(9)]

    def conclude(b, held):
        bias2 = bs_ref[1:2, b * WIDE : (b + 1) * WIDE]

        def begin():
            if "acc" in held:
                acc = held.pop("acc")
                held["own"], held["mates"] = acc[:size], acc[size:]
            mates = jnp.maximum(held.pop("mates") + bias2, 0.0) + t_ref[b, 1, 16 : 16 + part, :].astype(F32)
            held["latent"] = dot(mates.astype(BF16), dn_ref[WIDE:, :]).reshape(HALF, 16, LANES)

        def ups():
            latent = held.pop("latent")
            both = jnp.concatenate([jnp.where(own_mask, latent, 0.0), jnp.where(own_mask, 0.0, latent)], axis=2)
            held["added"] = dot(both.reshape(part, WIDE).astype(BF16), un_ref[WIDE:, :]).reshape(HALF, 16, WIDE)

        def row(y):
            at = (y // HALF) * 8
            add = held["added"][y % HALF, at : at + 8]
            add = jnp.concatenate([swap(add), add], axis=0)
            second = jnp.maximum(held["own"][y * 16 : y * 16 + 16] + bias2, 0.0)
            second = rounded(second + s_ref[b, 1, (y + 1) * 16 : (y + 2) * 16, :].astype(F32))
            two = second + jnp.where(gate16, add, 0.0)
            c2_ref[b, y] = jnp.where(ok16, two, 0.0)

        return [begin, ups] + [functools.partial(row, y) for y in range(HEIGHT)]

    def weave(*streams):
        order = []
        for s, stream in enumerate(streams):
            order += [((i + 0.5) / len(stream), s, i) for i in range(len(stream))]
        for _, s, i in sorted(order):
            streams[s][i]()

    lane = iota((16, LANES), 1)
    left, right = lane < CHANS, lane >= LANES - CHANS

    def spread_rows(pair):
        width = 2 * WIDE
        keep = iota((8, width), 0) < 4
        nothing = (jnp.zeros((8, width), F32),) * 3

        def filled(y):
            tiles = []
            for b in (2 * pair, 2 * pair + 1):
                old = pltpu.roll(c2_ref[b - 1, y, :, LANES:], 64, 1) if b else jnp.zeros((16, LANES), F32)
                tiles.append(jnp.where(left, old, c2_ref[b, y, :, :LANES]))
                old = pltpu.roll(c2_ref[b + 1, y, :, :LANES], 64, 1) if b + 1 < BLOCKS else jnp.zeros((16, LANES), F32)
                tiles.append(jnp.where(right, old, c2_ref[b, y, :, LANES:]))
            whole = jnp.concatenate(tiles, axis=1)
            low, high = whole[0:8], whole[8:16]
            return low, jnp.where(keep, swap(low), swap(high)), high

        def store(r, top, bottom):
            for dt in range(3):
                s3_ref[dt, r * 16 : (r + 1) * 16, pair * width : (pair + 1) * width] = jnp.concatenate(
                    [top[dt], bottom[dt]], axis=0
                ).astype(BF16)

        def step(y):
            top, bottom = filled(y), filled(y + HALF)
            store(y + 1, top, bottom)
            if y == 0:
                store(HALF + 1, bottom, nothing)
            if y == HALF - 1:
                store(0, nothing, top)

        return [functools.partial(step, y) for y in range(HALF)]

    def last_layer(pair, held):
        def step(tap):
            dt, dr = divmod(tap, 3)
            lhs = jnp.concatenate(
                [
                    s3_ref[dt, dr * 16 : dr * 16 + part, b * WIDE : (b + 1) * WIDE]
                    for b in (2 * pair, 2 * pair + 1)
                ],
                axis=0,
            )
            held["acc"] = held.get("acc", jnp.zeros((2 * part, WIDE), F32)) + dot(
                lhs, w3_ref[tap * WIDE : (tap + 1) * WIDE, :]
            )

        return [functools.partial(step, tap) for tap in range(9)]

    logits = []

    def readout(pair, held):
        def step(i):
            b = 2 * pair + i
            lanes = slice(b * WIDE, (b + 1) * WIDE)
            third = jnp.maximum(held["acc"][i * part : (i + 1) * part] + bs_ref[2:3, lanes], 0.0)
            third = third + s3_ref[1, 16 : 16 + part, lanes].astype(F32)
            high = third.astype(BF16)
            rest = (third - high.astype(F32)).astype(BF16)
            sums = dot(jnp.concatenate([high, rest], axis=0), rd_ref[lanes, :])
            logits.append(sums[:part] + sums[part:])

        return [functools.partial(step, i) for i in range(2)]

    plans = [prepare(b) for b in range(BLOCKS)]
    helds = [{} for _ in range(BLOCKS)]
    weave(plans[0][0])
    weave(plans[0][1], plans[1][0])
    for b in range(BLOCKS - 1):
        streams = [convolve(b, helds[b])]
        if b:
            streams.append(conclude(b - 1, helds[b - 1]))
        streams.append(plans[b + 1][1])
        if b + 2 < BLOCKS:
            streams.append(plans[b + 2][0])
        weave(*streams)
    final = BLOCKS - 1
    weave(convolve_part(final, helds[final], "mates"), conclude(final - 1, helds[final - 1]))
    ends = conclude(final, helds[final])
    weave(convolve_part(final, helds[final], "own"), ends[:2], spread_rows(0))
    thirds = [{}, {}]
    places = spread_rows(1)
    rest = []
    for y in range(HALF):
        rest += [ends[2 + y], ends[2 + y + HALF], places[y]]
    weave(last_layer(0, thirds[0]), rest)
    weave(last_layer(1, thirds[1]), readout(0, thirds[0]))
    weave(readout(1, thirds[1]))
    finish(sum(logits[1:], logits[0]).reshape(HALF, 16, LANES), cell_ref, out_ref)


def finish(logits, cell_ref, out_ref):
    lane8 = iota((8, LANES), 1)
    flat = [jnp.zeros((8, LANES), F32) for _ in range(FLAT // LANES)]
    for y in range(HEIGHT):
        row = logits[y % HALF, (y // HALF) * 8 : (y // HALF) * 8 + 8]
        begin = y * WIDTH
        turned = pltpu.roll(row, begin % LANES, 1) if begin % LANES else row
        for dst in range(FLAT // LANES):
            a = max(begin, dst * LANES) - dst * LANES
            e = min(begin + WIDTH, (dst + 1) * LANES) - dst * LANES
            if a < e:
                flat[dst] = jnp.where((lane8 >= a) & (lane8 < e), turned, flat[dst])
    flat = jnp.concatenate(flat, axis=1)[:, : HEIGHT * WIDTH] + cell_ref[...]
    for j in range(DEPTH):
        for p in range(COUNT):
            out_ref[p, j : j + 1, :] = flat[4 * j + p : 4 * j + p + 1, :]


def in_hbm(x):
    return pltpu.with_memory_space_constraint(x, pltpu.HBM)


def swapped(block, axis, mask):
    count = lax.axis_size(axis)
    return lax.ppermute(block, axis, [(i, i ^ mask) for i in range(count)])


def shifted(block, axis, offset):
    count = lax.axis_size(axis)
    return lax.ppermute(block, axis, [(i, i - offset) for i in range(count) if 0 <= i - offset < count])


def shards(
    bits, partners, gate_round, first_kernel, second_kernels, conv_bias, couple_down, couple_up, head, cell_bias
):
    devices, steps = lax.axis_size("patch"), lax.axis_size("tm")
    latent = couple_down.shape[-1]
    total = BLOCKS * WIDE
    vmem = pl.BlockSpec(memory_space=pltpu.VMEM)
    hbm = pl.BlockSpec(memory_space=pltpu.HBM)
    mine = pl.pallas_call(
        pack_kernel,
        out_shape=jax.ShapeDtypeStruct((8, FLAT + LANES), BF16),
        in_specs=[hbm, hbm, pl.BlockSpec(memory_space=pltpu.SMEM)],
        out_specs=vmem,
        scratch_shapes=[
            pltpu.VMEM((COUNT, DEPTH, WIDTH, HEIGHT), jnp.int32),
            pltpu.VMEM(partners.shape, jnp.int32),
            pltpu.SemaphoreType.DMA((2,)),
        ],
        compiler_params=pltpu.CompilerParams(vmem_limit_bytes=2 << 20),
        name="pack",
    )(in_hbm(jnp.swapaxes(bits, 2, 3)), in_hbm(partners), gate_round)

    exact = steps == 4 and devices > 1
    if exact:
        blocks = [mine]
        for k in range(1, steps):
            pairs = [(i, i ^ k if abs(i - (i ^ k)) <= 2 else i) for i in range(steps)]
            blocks.append(lax.ppermute(mine, "tm", pairs))
    else:
        blocks = [mine] + [shifted(mine, "tm", k) for k in (1, -1, 2, -2)]
    near = jnp.concatenate(blocks, axis=0)
    params = (
        first_kernel,
        second_kernels.reshape(54 * CHANS, CHANS),
        conv_bias,
        jnp.swapaxes(couple_down, 1, 2),
        couple_up,
        head.reshape(1, CHANS),
    )
    weights = pl.pallas_call(
        weights_kernel,
        out_shape=[
            jax.ShapeDtypeStruct((WIDE, total), BF16),
            jax.ShapeDtypeStruct((9 * WIDE, WIDE), BF16),
            jax.ShapeDtypeStruct((9 * WIDE, WIDE), BF16),
            jax.ShapeDtypeStruct((2 * WIDE, SLOTS * latent), BF16),
            jax.ShapeDtypeStruct((4 * SLOTS * latent, WIDE), BF16),
            jax.ShapeDtypeStruct((total, LANES), BF16),
            jax.ShapeDtypeStruct((8, total), F32),
        ],
        in_specs=[hbm] * 6,
        out_specs=[vmem] * 7,
        scratch_shapes=[pltpu.VMEM((WIDE, total), F32)]
        + [pltpu.VMEM(x.shape, x.dtype) for x in params]
        + [pltpu.SemaphoreType.DMA((6,))],
        cost_estimate=pl.CostEstimate(flops=10**9, bytes_accessed=10**7, transcendentals=0),
        compiler_params=pltpu.CompilerParams(vmem_limit_bytes=12 << 20),
        name="weights",
    )(*map(in_hbm, params))

    every = near[:, :FLAT]
    parts = [every]
    for m in range(1, devices // 2):
        parts.append(swapped(every, "patch", 2 * m))
    every = jnp.concatenate(parts, axis=0)
    every, weights = lax.optimization_barrier((every, weights))
    others = swapped(every, "patch", 1)

    if exact:
        wf, w2, w3, dn, un, rd, bs = weights
        early = pl.pallas_call(
            functools.partial(early_kernel, (devices, steps)),
            out_shape=[
                jax.ShapeDtypeStruct((HEIGHT, OWN, total), F32),
                jax.ShapeDtypeStruct((BLOCKS, HEIGHT, 8, LANES), F32),
                jax.ShapeDtypeStruct((3 * MATES, 8 * steps * devices), BF16),
                jax.ShapeDtypeStruct((MASK_ROWS, LANES), F32),
            ],
            in_specs=[vmem] * 4,
            out_specs=[vmem] * 4,
            scratch_shapes=[pltpu.VMEM((HEIGHT * OWN, WIDE), BF16), pltpu.VMEM((8, LANES), F32)],
            cost_estimate=pl.CostEstimate(flops=10**9, bytes_accessed=10**7, transcendentals=0),
            compiler_params=pltpu.CompilerParams(vmem_limit_bytes=14 << 20),
            name="early",
        )(near, wf, dn, bs)
        return pl.pallas_call(
            late_kernel,
            out_shape=jax.ShapeDtypeStruct((COUNT, DEPTH, HEIGHT * WIDTH), F32),
            in_specs=[vmem] * 14,
            out_specs=vmem,
            scratch_shapes=[
                pltpu.VMEM((HEIGHT * MATES, WIDE), BF16),
                pltpu.VMEM((2, HEIGHT, MATES, WIDE), BF16),
                pltpu.VMEM((BLOCKS, 3, 28 * 16, WIDE), BF16),
                pltpu.VMEM((BLOCKS, 3, (HALF + 2) * 16, WIDE), BF16),
                pltpu.VMEM((BLOCKS, HEIGHT, 16, WIDE), F32),
                pltpu.VMEM((3, (HALF + 2) * 16, total), BF16),
            ],
            compiler_params=pltpu.CompilerParams(vmem_limit_bytes=36 << 20),
            name="late",
        )(every, others, *early, wf, w2, w3, dn, un, rd, bs, cell_bias.reshape(1, HEIGHT * WIDTH))
    return pl.pallas_call(
        functools.partial(main_kernel, (devices, steps, exact)),
        out_shape=jax.ShapeDtypeStruct((COUNT, DEPTH, HEIGHT * WIDTH), F32),
        in_specs=[vmem] * 11,
        out_specs=vmem,
        scratch_shapes=[
            pltpu.VMEM((HEIGHT * UNITS, WIDE), BF16),
            pltpu.VMEM((HEIGHT, UNITS, WIDE), F32),
            pltpu.VMEM((3, 28 * 32, WIDE), BF16),
            pltpu.VMEM((BLOCKS, HEIGHT, 16, WIDE), F32),
            pltpu.VMEM((3, (HALF + 2) * 16, total), BF16),
        ],
        compiler_params=pltpu.CompilerParams(vmem_limit_bytes=40 << 20),
        name="decode",
    )(every, others, near, *weights, cell_bias.reshape(1, HEIGHT * WIDTH))


def solution(mesh):
    in_specs = (
        P("patch", "tm", None, None),
        P("tm", None),
        P("tm"),
        P(),
        P(),
        P(),
        P(),
        P(),
        P(),
        P(),
    )
    out_specs = P("patch", "tm", None)
    return jax.shard_map(shards, mesh=mesh, in_specs=in_specs, out_specs=out_specs, check_vma=False)
```
